32 devices in a mesh: col: 2 (over x), row: 16 (over z, y, core).
Axes of the slice: x: 2, y: 2, z: 4, core: 2. Of those that a mesh axis runs over, the one named last changes fastest.
Arguments:
- residual: bfloat16 [1024, 2880], P('row'), may hold values from -6 to 6
- query_states: bfloat16 [1024, 4096], P('row', 'col'), may hold values from -48 to 48
- key_states: bfloat16 [1024, 512], P('row'), may hold values from -24 to 24
- value_states: bfloat16 [1024, 512], P('row'), may hold values from -6 to 6
- segment_ids: int32 [1024], P('row'), may hold values from 0 to 3, never falling along the last dimension, each value on 1 to 512 neighbouring positions
- sink_logits: float32 [64], P('col'), may hold values from -2 to 4
- w_out: bfloat16 [4096, 2880], P('col'), may hold values from -0.375 to 0.375
- norm_gain: float32 [2880], replicated, may hold values from 0.5 to 1.5
- expert_ids: int32 [1024, 4], P('row'), may hold values from 0 to 15, all different within a row; in each aligned block of 64 rows (0 to 63, 64 to 127, ...) at most 32 rows name the same one
- route_weight: float32 [1024, 4], P('row'), may hold values from 0.05 to 0.45
- w_gate_up: bfloat16 [16, 2, 2880, 2880], P('row', None, None, 'col'), may hold values from -0.109375 to 0.109375
- w_down: bfloat16 [16, 2880, 2880], P('row', 'col'), may hold values from -0.109375 to 0.109375
Outputs:
- layer_out: bfloat16 [1024, 2880], P('row', 'col')
The draws below stay inside these ranges and needn't reach their ends.
Inputs may be any that keep to these rules, and one draw needn't show every extreme that they name: `expert_ids`: each token names 4 different experts; among the 64 tokens of one index of row no expert is named by more than 32 tokens, and in every draw some expert is named by exactly 32 of them. `segment_ids`: segment numbers never fall along the tokens.
All inputs are finite; a program needn't handle non-finite values.
Results may differ from the reference program's by a relative error of at most 0.018.
Values may be sent and summed in bfloat16 or wider, within the bound.
A program may use at most 128 MiB of HBM per device.

```python
import math
import jax
import jax.numpy as jnp
import numpy as np
from jax import lax

D = 2880
HEADS = 64
KV_HEADS = 8
HEAD_DIM = 64
WINDOW = 128
FF = 2880
TOP = 4
TOK_ROW = 64
TOKENS = 1024
EXPERTS = 16
CAP = 32
N_ROW = 16


def shared_keys(key):
    base = jax.random.truncated_normal(jax.random.fold_in(key, 11), -6.0, 6.0, (TOKENS, KV_HEADS, HEAD_DIM), jnp.float32)
    return base


def draw_key_states(key, part):
    base = shared_keys(key)
    chosen = base
    return chosen.reshape(TOKENS, KV_HEADS * HEAD_DIM).astype(jnp.bfloat16)


def draw_query_states(key, part):
    drawn = jax.random.truncated_normal(jax.random.fold_in(key, 23), -6.0, 6.0, (TOKENS, HEADS * HEAD_DIM), jnp.float32)
    return drawn.astype(jnp.bfloat16)


def block_levels(key, dims, split, smallest, top_value):
    level = 1.0
    for axis_at, blocks in split:
        steps = jax.random.uniform(jax.random.fold_in(jax.random.fold_in(key, 6), axis_at), (blocks,), jnp.float32, smallest / len(split), top_value / len(split))
        level = level * jnp.repeat(jnp.exp(steps), dims[axis_at] // blocks).reshape((-1,) + (1,) * (len(dims) - 1 - axis_at))
    return level


def length_profile(count, total, reach, skew):
    portions = [(1 << 20) // math.isqrt(standing ** skew) + 1 for standing in range(2, count + 1)]
    spare, counts = total - reach - (count - 1), [1] * (count - 1)
    while spare > 0:
        candidates = [i for i in range(count - 1) if counts[i] < reach]
        whole, left = sum([portions[i] for i in candidates]), spare
        for i in candidates:
            addition = min(reach - counts[i], max(1, left * portions[i] // whole), spare)
            counts[i] = counts[i] + addition
            spare = spare - addition
    return np.array([reach] + counts)


def uneven_parts(own_key, amount, total, limit, skew):
    if amount == 2:
        one = jax.random.randint(own_key, (), max(1, total - limit), min(limit, total - 1) + 1)
        return jnp.stack([one, total - one])
    lengths = jnp.asarray(length_profile(amount, total, limit, skew), jnp.int32)
    pairs = (amount - 1) // 2
    donor, sink = lengths[1:1 + 2 * pairs:2], lengths[2:2 + 2 * pairs:2]
    room = jnp.minimum(donor - 1, limit - sink)
    moved = jax.random.randint(jax.random.fold_in(own_key, 1), (pairs,), 0, 1 << 20) % (room + 1)
    lengths = lengths.at[1:1 + 2 * pairs:2].set(donor - moved).at[2:2 + 2 * pairs:2].set(sink + moved)
    return lengths[jax.random.permutation(jax.random.fold_in(own_key, 2), amount)]


def assign_block(stream_key, own, number, rows, number_of, top, reach, lean):
    order = jax.random.permutation(stream_key, number_of)
    heavy_load, common = shares(number_of, rows * top, reach, lean, True), shares(number_of, rows * top, reach, lean, False)
    places = jnp.arange(number_of)

    def named(sizes, rotation):
        used = int((sizes > 0).sum())
        fixed = max(1, used // 4)
        moved = fixed + (places - fixed + rotation * (used - fixed)) % max(1, number_of - fixed)
        return jnp.zeros((number_of,), jnp.int32).at[order[jnp.where(places < fixed, places, moved)]].set(jnp.asarray(sizes, jnp.int32))

    sizes = jnp.where(number % 4 == 0, named(heavy_load, number // 4), named(common, number - number // 4 - 1))
    mixed = jax.random.permutation(jax.random.fold_in(own, 3), number_of)
    source_of, sink = mixed[0:number_of // 2 * 2:2], mixed[1:number_of // 2 * 2:2]
    margin = jnp.minimum(sizes[source_of] - 1, reach - sizes[sink]) // 2
    margin = jnp.where((source_of == order[0]) | (sink == order[0]) | (sizes[sink] == 0), 0, jnp.maximum(margin, 0))
    moved = jax.random.randint(jax.random.fold_in(own, 4), (number_of // 2,), 0, 1 << 20) % (margin + 1)
    sizes = sizes.at[source_of].add(-moved).at[sink].add(moved)
    labels = jnp.searchsorted(jnp.cumsum(sizes), jnp.arange(rows * top), side="right").astype(jnp.int32)
    listing = labels.reshape(top, rows).T
    listing = listing[jax.random.permutation(jax.random.fold_in(own, 1), rows)]
    rotation = jax.random.randint(jax.random.fold_in(own, 2), (rows, 1), 0, top)
    return jnp.take_along_axis(listing, (jnp.arange(top)[None, :] + rotation) % top, axis=1)


def shares(amount, total, limit, lean, full):
    weights = [(1 << 20) // math.isqrt(rank ** lean) + 1 for rank in range(1, amount + 1)]
    largest = limit if full else min(limit, max(-(-total // amount), total * weights[0] // sum(weights)))
    least = 1 if total - largest >= amount - 1 else 0
    given, spare = [largest] + [least] * (amount - 1), total - largest - least * (amount - 1)
    while spare > 0:
        candidates = [i for i in range(1, amount) if given[i] < largest] or [i for i in range(1, amount) if given[i] < limit]
        pool, left = sum([weights[i] for i in candidates]), spare
        for i in candidates:
            more = min(limit - given[i], max(1, left * weights[i] // pool), spare)
            given[i] = given[i] + more
            spare = spare - more
    return np.array(given)


def noise(rng, extent, deviation, most, split=(), kind=jnp.bfloat16):
    result = deviation * jax.random.normal(rng, extent, jnp.float32)
    if split:
        result = result * block_levels(rng, extent, split, -0.22, 0.18)
    return jnp.clip(result, -most, most).astype(kind)


def setup_inputs(seed: int = 0) -> dict:
    keys = jax.random.split(jax.random.key(seed), 13)
    residual = noise(keys[0], (TOKENS, D), 1.0, 6.0, ((0, 16),))
    query_states = draw_query_states(jax.random.fold_in(keys[12], 71), 0)
    key_states = draw_key_states(jax.random.fold_in(keys[12], 71), 0)
    value_states = noise(keys[3], (TOKENS, KV_HEADS * HEAD_DIM), 1.0, 6.0, ((0, 16),))
    segment_ids = jnp.searchsorted(jnp.cumsum(uneven_parts(keys[4], max(2, TOKENS // (2 * WINDOW)), TOKENS, min(4 * WINDOW, TOKENS // 2), 2)), jnp.arange(TOKENS), side="right").astype(jnp.int32)
    sink_logits = jnp.clip(-2.0 + 6.0 * jax.random.uniform(keys[5], (HEADS,), jnp.float32) ** block_levels(keys[5], (HEADS,), ((0, 2),), -0.2, 0.2), -2.0, 4.0)
    w_out = noise(keys[6], (HEADS * HEAD_DIM, D), (HEADS * HEAD_DIM // 16) ** -0.5, 0.375, ((0, 2),))
    norm_gain = jnp.clip(1.0 + 0.1 * jax.random.normal(keys[7], (D,), jnp.float32), 0.5, 1.5)
    expert_ids_keys = jax.random.split(jax.random.fold_in(keys[8], 1), TOKENS // TOK_ROW)
    expert_ids_turns = jax.random.permutation(jax.random.fold_in(keys[8], 3), TOKENS // TOK_ROW)
    expert_ids = jax.vmap(lambda own, number: assign_block(jax.random.fold_in(keys[8], 2), own, number, TOK_ROW, EXPERTS, TOP, CAP, 2))(expert_ids_keys, expert_ids_turns).reshape((TOKENS, TOP))
    route_weight = jnp.clip(0.05 + 0.39999999 * jax.random.uniform(keys[9], (TOKENS, TOP), jnp.float32) ** block_levels(keys[9], (TOKENS, TOP), ((0, 16),), -0.2, 0.2), 0.05, 0.45)
    w_gate_up = noise(keys[10], (EXPERTS, 2, D, FF), D ** -0.5, 0.109375, ((0, 16), (3, 2)))
    w_down = noise(keys[11], (EXPERTS, FF, D), FF ** -0.5, 0.109375, ((0, 16), (1, 2)))
    return dict(residual=residual, query_states=query_states, key_states=key_states, value_states=value_states, segment_ids=segment_ids, sink_logits=sink_logits, w_out=w_out, norm_gain=norm_gain, expert_ids=expert_ids, route_weight=route_weight, w_gate_up=w_gate_up, w_down=w_down)


epsilon = 1e-05
masked_score = -1e+30

def normalize(stream_rows, norm_gain):
    values32 = stream_rows.astype(jnp.float32)
    square_mean = lax.optimization_barrier(jnp.mean(values32 * values32, axis=-1, keepdims=True))
    return (values32 * lax.rsqrt(square_mean + epsilon) * norm_gain).astype(jnp.bfloat16)

def reference(residual, query_states, key_states, value_states, segment_ids, sink_logits, w_out, norm_gain, expert_ids, route_weight, w_gate_up, w_down):
    group_size = HEADS // KV_HEADS
    queries_all = query_states.astype(jnp.float32).reshape(TOKENS, KV_HEADS, group_size, HEAD_DIM)
    padding = jnp.zeros((WINDOW, KV_HEADS * HEAD_DIM), jnp.float32)
    keys_padded = jnp.concatenate([padding, key_states.astype(jnp.float32)], 0).reshape(TOKENS + WINDOW, KV_HEADS, HEAD_DIM)
    values_padded = jnp.concatenate([padding, value_states.astype(jnp.float32)], 0).reshape(TOKENS + WINDOW, KV_HEADS, HEAD_DIM)
    segments_padded = jnp.concatenate([jnp.full((WINDOW,), -1, jnp.int32), segment_ids], 0)
    sink_groups = sink_logits.reshape(KV_HEADS, group_size, 1, 1)

    def attend_block(block_at):
        start = block_at * WINDOW
        query_block = lax.dynamic_slice_in_dim(queries_all, start, WINDOW, 0)
        key_block = lax.dynamic_slice_in_dim(keys_padded, start, 2 * WINDOW, 0)
        value_block = lax.dynamic_slice_in_dim(values_padded, start, 2 * WINDOW, 0)
        key_segments = lax.dynamic_slice_in_dim(segments_padded, start, 2 * WINDOW, 0)
        query_segments = lax.dynamic_slice_in_dim(segment_ids, start, WINDOW, 0)
        query_position = start + jnp.arange(WINDOW, dtype=jnp.int32)
        key_position = start - WINDOW + jnp.arange(2 * WINDOW, dtype=jnp.int32)
        allowed = (key_position[None, :] >= 0) & (key_position[None, :] <= query_position[:, None])
        allowed = allowed & (key_position[None, :] > query_position[:, None] - WINDOW)
        allowed = allowed & (key_segments[None, :] == query_segments[:, None])
        scores = jnp.einsum('tgjd,lgd->gjtl', query_block, key_block) * HEAD_DIM ** (-0.5)
        scores = jnp.where(allowed[None, None], scores, masked_score)
        peak_score = jnp.maximum(lax.optimization_barrier(jnp.max(scores, axis=-1, keepdims=True)), sink_groups)
        numerator = jnp.exp(scores - peak_score)
        denominator = jnp.exp(sink_groups - peak_score) + lax.optimization_barrier(jnp.sum(numerator, axis=-1, keepdims=True))
        weights = (numerator / denominator).astype(jnp.bfloat16)
        weights = lax.optimization_barrier(weights).astype(jnp.float32)
        attended_block = jnp.einsum('gjtl,lgd->tgjd', weights, value_block)
        return attended_block.astype(jnp.bfloat16).reshape(WINDOW, HEADS * HEAD_DIM)
    attended = lax.map(attend_block, jnp.arange(TOKENS // WINDOW, dtype=jnp.int32)).reshape(TOKENS, HEADS * HEAD_DIM)
    stream = (residual.astype(jnp.float32) + jnp.dot(attended, w_out, preferred_element_type=jnp.float32)).astype(jnp.bfloat16)
    normed = normalize(stream, norm_gain)
    block_ids = expert_ids.reshape(N_ROW, TOK_ROW * TOP)
    expert_hot = (block_ids[:, :, None] == jnp.arange(EXPERTS, dtype=jnp.int32)[None, None, :]).astype(jnp.int32)
    earlier = jnp.cumsum(expert_hot, axis=1) - expert_hot
    slot_of = lax.optimization_barrier(jnp.sum(earlier * expert_hot, axis=2))
    block_index = jnp.arange(N_ROW, dtype=jnp.int32)[:, None]
    place = (block_ids * (N_ROW * CAP) + block_index * CAP + slot_of).reshape(-1).astype(jnp.int32)
    owner = jnp.repeat(jnp.arange(TOKENS, dtype=jnp.int32), TOP)
    table = jnp.full((EXPERTS * N_ROW * CAP,), -1, jnp.int32).at[place].set(owner).reshape(EXPERTS, N_ROW * CAP)

    def one_expert(expert_at):
        index_row = table[expert_at]
        picked = jnp.take(normed, jnp.maximum(index_row, 0), axis=0)
        slot_rows = jnp.where((index_row >= 0)[:, None], picked, jnp.zeros_like(picked))
        gate_part = jnp.dot(slot_rows, w_gate_up[expert_at, 0], preferred_element_type=jnp.float32)
        up_part = jnp.dot(slot_rows, w_gate_up[expert_at, 1], preferred_element_type=jnp.float32)
        active = ((up_part + 1.0) * gate_part * jax.nn.sigmoid(1.702 * gate_part)).astype(jnp.bfloat16)
        return jnp.dot(active, w_down[expert_at], preferred_element_type=jnp.float32).astype(jnp.bfloat16)
    expert_outputs = lax.map(one_expert, jnp.arange(EXPERTS, dtype=jnp.int32)).reshape(EXPERTS * N_ROW * CAP, D)
    gathered = jnp.take(expert_outputs, place.reshape(TOKENS, TOP), axis=0).astype(jnp.float32)
    expert_mix = lax.optimization_barrier(jnp.sum(route_weight[:, :, None] * gathered, axis=1))
    return (stream.astype(jnp.float32) + expert_mix).astype(jnp.bfloat16)
```

```python
import jax
import jax.numpy as jnp
from jax import lax
from jax.experimental import pallas as pl
from jax.experimental.pallas import tpu as pltpu
from jax.sharding import PartitionSpec as P

HEADS = 64
KV_HEADS = 8
HEAD_DIM = 64
WINDOW = 128
TOP = 4


epsilon = 1e-05
masked_score = -1e30


def shifted(shard, axis, by):
    size = lax.axis_size(axis)
    pairs = [(i, i + by) for i in range(size) if 0 <= i + by < size]
    return lax.ppermute(shard, axis, pairs)


def normalize(stream_rows, norm_gain):
    values32 = stream_rows.astype(jnp.float32)
    square_mean = jnp.mean(values32 * values32, axis=-1, keepdims=True)
    return (values32 * lax.rsqrt(square_mean + epsilon) * norm_gain).astype(jnp.bfloat16)


def attend(query_groups, key_groups, value_groups, allowed, sink_groups):
    scores = jnp.einsum(
        "tgjd,lgd->gjtl", query_groups, key_groups, preferred_element_type=jnp.float32
    )
    scores = scores * query_groups.shape[-1] ** (-0.5)
    scores = jnp.where(allowed[None, None], scores, masked_score)
    peak_score = jnp.maximum(jnp.max(scores, axis=-1, keepdims=True), sink_groups)
    numerator = jnp.exp(scores - peak_score)
    denominator = jnp.exp(sink_groups - peak_score) + jnp.sum(numerator, axis=-1, keepdims=True)
    weights = (numerator / denominator).astype(jnp.bfloat16)
    return jnp.einsum(
        "gjtl,lgd->tgjd", weights, value_groups, preferred_element_type=jnp.float32
    ).astype(jnp.bfloat16)


MESH = pl.DeviceIdType.MESH
VMEM = pl.BlockSpec(memory_space=pltpu.VMEM)
PIECES = 4
VMEM_BYTES = 60 * 1024 * 1024


def ring_place(row, chips):
    chip = lax.div(row, 2)
    along = lax.div(chip, 2)
    return jnp.where(lax.rem(chip, 2) == 0, along, chips - 1 - along)


def ring_row(place, chips, core):
    place = lax.rem(place + chips, chips)
    chip = jnp.where(place < chips // 2, 2 * place, 2 * (chips - 1 - place) + 1)
    return 2 * chip + core


def greet(devices):
    barrier = pltpu.get_barrier_semaphore()
    for device in devices:
        pl.semaphore_signal(barrier, inc=1, device_id=device, device_id_type=MESH)
    pl.semaphore_wait(barrier, len(devices))


def remote(src, dst, send, recv, device):
    return pltpu.make_async_remote_copy(
        src_ref=src, dst_ref=dst, send_sem=send, recv_sem=recv, device_id=device,
        device_id_type=MESH,
    )


def halo_kernel(rows, shifts, key_ref, value_ref, segment_ref, key_out, value_out, segment_out, send, recv):
    row = lax.axis_index("row")
    col = lax.axis_index("col")
    after = [{"row": lax.rem(row + shift, rows)} for shift in range(1, shifts + 1)]
    before = [{"row": lax.rem(row + rows - shift, rows)} for shift in range(1, shifts + 1)]
    greet(after + before)
    width = key_out.shape[2]
    lanes = pl.ds(pl.multiple_of(col * width, width), width)
    copies = []
    for at in range(shifts):
        for which, (src, dst) in enumerate([
            (segment_ref, segment_out.at[at]),
            (key_ref.at[:, lanes], key_out.at[at]),
            (value_ref.at[:, lanes], value_out.at[at]),
        ]):
            copies.append(remote(src, dst, send.at[at, which], recv.at[at, which], after[at]))
    for copy in copies:
        copy.start()
    for copy in copies:
        copy.wait()


def halo(keys, values, segments, rows, shifts, width):
    tokens = keys.shape[0]
    return pl.pallas_call(
        lambda *refs: halo_kernel(rows, shifts, *refs),
        out_shape=(
            jax.ShapeDtypeStruct((shifts, tokens, width), keys.dtype),
            jax.ShapeDtypeStruct((shifts, tokens, width), values.dtype),
            jax.ShapeDtypeStruct((shifts, 1, tokens), segments.dtype),
        ),
        in_specs=[VMEM] * 3,
        out_specs=(VMEM,) * 3,
        scratch_shapes=[
            pltpu.SemaphoreType.DMA((shifts, 3)),
            pltpu.SemaphoreType.DMA((shifts, 3)),
        ],
        compiler_params=pltpu.CompilerParams(
            collective_id=1, has_side_effects=True, vmem_limit_bytes=16 * 1024 * 1024
        ),
        name="halo",
    )(keys, values, segments.reshape(1, -1))


def ring_pieces(distance, half_way, way):
    if distance < half_way:
        return [1, 2, 0]
    return [1, 0] if way == 0 else [2]


def piece_rows(index, size):
    col = lax.axis_index("col")
    start = (index + col * (PIECES - 1 - 2 * index)) * size
    return pl.ds(pl.multiple_of(start, size), size)


def spread_kernel(rows, partial_ref, residual_ref, gain_ref, meta_ref, stream_ref, out_ref, meta_out, part_in,
                  x_sem, c_send, c_recv, m_send, m_recv, n_send, n_recv, l_sem, send, recv, over_send, over_recv, sib_send, sib_recv):
    chips = rows // 2
    half_way = chips // 2
    row = lax.axis_index("row")
    col = lax.axis_index("col")
    core = lax.rem(row, 2)
    place = ring_place(row, chips)
    sibling = {"row": row + 1 - 2 * core}
    partner = {"col": 1 - col}
    ways = [{"row": ring_row(place + 1, chips, core)}, {"row": ring_row(place - 1, chips, core)}]
    greet([sibling, partner] + ways)
    size = partial_ref.shape[0] // PIECES
    crosses = {}
    for index in [2, 1, 3, 0]:
        at = piece_rows(index, size)
        named = PIECES - 1 - index
        crosses[index] = remote(partial_ref.at[at], part_in.at[at], c_send.at[named],
                                c_recv.at[named], partner)
        crosses[index].start()
    local_meta = pltpu.make_async_copy(meta_ref, meta_out.at[row], l_sem)
    local_meta.start()

    def ready(index):
        at = piece_rows(index, size)
        remote(partial_ref.at[at], part_in.at[at], c_send.at[index], c_recv.at[index],
               partner).wait_recv()
        summed = partial_ref[at, :].astype(jnp.float32) + part_in[at, :].astype(jnp.float32)
        stream = (residual_ref[at, :].astype(jnp.float32) + summed).astype(jnp.bfloat16)
        stream_ref[at, :] = stream
        out_ref[row, at, :] = normalize(stream, gain_ref[...])

    def part(offset, index, which):
        return out_ref.at[ring_row(place + offset, chips, which), piece_rows(index, size)]

    def offset_of(way, distance):
        return -distance if way == 0 else distance

    def hop(way, distance, index, sending):
        at = part(offset_of(way, distance - 1 if sending else distance), index, core)
        return remote(at, at, send.at[way, distance - 1, index], recv.at[way, distance - 1, index],
                      ways[way])

    def over(way, distance, sending):
        at = part(offset_of(way, distance), 0 if sending else PIECES - 1, core)
        return remote(at, at, over_send.at[way, distance - 1], over_recv.at[way, distance - 1],
                      partner)

    def pass_on(way, distance, index, which):
        at = part(offset_of(way, distance), index, which)
        return remote(at, at, sib_send.at[way, distance, index], sib_recv.at[way, distance, index],
                      sibling)

    sent = []

    def go(copy):
        copy.start()
        sent.append(copy)

    for index in [1, 2, 0]:
        ready(index)
        for way in range(2):
            if index in ring_pieces(1, half_way, way):
                go(hop(way, 1, index, True))
    ready(PIECES - 1)
    local_meta.wait()

    def routing_hop(way, distance, sending):
        back = offset_of(way, distance - 1 if sending else distance)
        at = meta_out.at[ring_row(place + back, chips, core)]
        return remote(at, at, m_send.at[way, distance - 1], m_recv.at[way, distance - 1], ways[way])

    def routing_on(way, distance, which):
        at = meta_out.at[ring_row(place + offset_of(way, distance), chips, which)]
        return remote(at, at, n_send.at[way, distance], n_recv.at[way, distance], sibling)

    reach = [half_way, half_way - 1]
    for way in range(2):
        go(routing_hop(way, 1, True))
    go(routing_on(0, 0, core))
    mine = out_ref.at[row]
    theirs = out_ref.at[row + 1 - 2 * core]
    go(remote(mine, mine, x_sem.at[0], x_sem.at[1], sibling))
    for distance in range(1, half_way + 1):
        for index in [1, 2, 0]:
            for way in range(2):
                if index not in ring_pieces(distance, half_way, way):
                    continue
                hop(way, distance, index, False).wait_recv()
                if distance < half_way and index in ring_pieces(distance + 1, half_way, way):
                    go(hop(way, distance + 1, index, True))
                if index == 0:
                    go(over(way, distance, True))
                go(pass_on(way, distance, index, core))
        for way in range(2):
            if distance <= reach[way]:
                routing_hop(way, distance, False).wait_recv()
                if distance < reach[way]:
                    go(routing_hop(way, distance + 1, True))
                go(routing_on(way, distance, core))
        for way in range(2):
            if distance > 1 and 0 in ring_pieces(distance - 1, half_way, way):
                over(way, distance - 1, False).wait_recv()
                go(pass_on(way, distance - 1, PIECES - 1, core))
    for way in range(2):
        if 0 in ring_pieces(half_way, half_way, way):
            over(way, half_way, False).wait_recv()
            go(pass_on(way, half_way, PIECES - 1, core))
    remote(theirs, theirs, x_sem.at[0], x_sem.at[1], sibling).wait_recv()
    for way in range(2):
        for distance in range(way, reach[way] + 1):
            routing_on(way, distance, 1 - core).wait_recv()
    for index in range(PIECES):
        crosses[index].wait_send()
    for distance in range(1, half_way + 1):
        for way in range(2):
            indices = list(ring_pieces(distance, half_way, way))
            for index in indices + ([PIECES - 1] if 0 in indices else []):
                pass_on(way, distance, index, 1 - core).wait_recv()
    for copy in sent:
        copy.wait_send()


def spread(partial, residual, gain, meta, rows):
    half_way = rows // 4
    return pl.pallas_call(
        lambda *refs: spread_kernel(rows, *refs),
        out_shape=(
            jax.ShapeDtypeStruct(residual.shape, jnp.bfloat16),
            jax.ShapeDtypeStruct((rows, *residual.shape), jnp.bfloat16),
            jax.ShapeDtypeStruct((rows, *meta.shape), meta.dtype),
        ),
        in_specs=[VMEM] * 4,
        out_specs=(VMEM,) * 3,
        scratch_shapes=[
            pltpu.VMEM(residual.shape, jnp.bfloat16),
            pltpu.SemaphoreType.DMA((2,)),
            pltpu.SemaphoreType.DMA((PIECES,)),
            pltpu.SemaphoreType.DMA((PIECES,)),
            pltpu.SemaphoreType.DMA((2, half_way)),
            pltpu.SemaphoreType.DMA((2, half_way)),
            pltpu.SemaphoreType.DMA((2, half_way + 1)),
            pltpu.SemaphoreType.DMA((2, half_way + 1)),
            pltpu.SemaphoreType.DMA,
            pltpu.SemaphoreType.DMA((2, half_way, PIECES)),
            pltpu.SemaphoreType.DMA((2, half_way, PIECES)),
            pltpu.SemaphoreType.DMA((2, half_way)),
            pltpu.SemaphoreType.DMA((2, half_way)),
            pltpu.SemaphoreType.DMA((2, half_way + 1, PIECES)),
            pltpu.SemaphoreType.DMA((2, half_way + 1, PIECES)),
        ],
        compiler_params=pltpu.CompilerParams(
            collective_id=2, has_side_effects=True, vmem_limit_bytes=VMEM_BYTES // 4
        ),
        name="spread",
    )(partial, residual, gain.reshape(1, -1), meta)


def fold_kernel(rows, part_ref, out_ref, sib_buf, ring_in, ring_out, over_out, over_in, x_out, x_in,
                x_sem, send, recv, over_send, over_recv, sib_send, sib_recv):
    chips = rows // 2
    half_way = chips // 2
    row = lax.axis_index("row")
    col = lax.axis_index("col")
    core = lax.rem(row, 2)
    place = ring_place(row, chips)
    sibling = {"row": row + 1 - 2 * core}
    partner = {"col": 1 - col}
    ways = [{"row": ring_row(place + 1, chips, core)}, {"row": ring_row(place - 1, chips, core)}]
    greet([sibling, partner] + ways)
    order = [half_way]
    for distance in range(half_way - 1, 0, -1):
        order += [distance, chips - distance]
    order.append(0)
    shared = {}
    for offset in order:
        copy = remote(part_ref.at[ring_row(place + offset, chips, 1 - core)], sib_buf.at[offset],
                      sib_send.at[offset], sib_recv.at[offset], sibling)
        copy.start()
        shared[offset] = copy
    size = part_ref.shape[1] // PIECES
    seen = set()

    def own(offset, index):
        if offset not in seen:
            shared[offset].wait_recv()
            seen.add(offset)
        at = piece_rows(index, size)
        return part_ref[ring_row(place + offset, chips, core), at, :].astype(
            jnp.float32
        ) + sib_buf[offset, at, :].astype(jnp.float32)

    def hop(way, distance, index):
        at = pl.ds(index * size, size)
        return remote(ring_out.at[way, distance - 1, at], ring_in.at[way, distance - 1, at],
                      send.at[way, distance - 1, index], recv.at[way, distance - 1, index],
                      ways[way])

    def arrived(way, distance, index):
        hop(way, distance, index).wait_recv()
        return ring_in[way, distance - 1, pl.ds(index * size, size), :].astype(jnp.float32)

    def over(offset):
        return remote(over_out.at[offset], over_in.at[offset], over_send.at[offset],
                      over_recv.at[offset], partner)

    sent = []

    def go(copy):
        copy.start()
        sent.append(copy)

    for distance in range(half_way, 0, -1):
        for offset in sorted({distance, chips - distance}):
            over_out[offset] = own(offset, PIECES - 1).astype(jnp.bfloat16)
            go(over(offset))
        for index in [1, 2, 0]:
            for way in range(2):
                if index not in ring_pieces(distance, half_way, way):
                    continue
                offset = distance if way == 0 else chips - distance
                value = own(offset, index)
                if index == 0:
                    over(offset).wait_recv()
                    value = value + over_in[offset].astype(jnp.float32)
                if distance < half_way and index in ring_pieces(distance + 1, half_way, way):
                    value = value + arrived(way, distance + 1, index)
                ring_out[way, distance - 1, pl.ds(index * size, size), :] = value.astype(
                    jnp.bfloat16
                )
                go(hop(way, distance, index))
    width = out_ref.shape[1]
    crosses = []
    for index in [3, 1, 2, 0]:
        at = piece_rows(index, size)
        value = own(0, index)
        for way in range(2):
            if index in ring_pieces(1, half_way, way):
                value = value + arrived(way, 1, index)
        low, high = value[:, :width], value[:, width:]
        x_out[at, :] = jnp.where(col == 0, high, low).astype(jnp.bfloat16)
        out_ref[at, :] = jnp.where(col == 0, low, high)
        copy = remote(x_out.at[at], x_in.at[at], x_sem.at[0, index], x_sem.at[1, index], partner)
        go(copy)
    for index in [0, 2, 1, 3]:
        at = piece_rows(index, size)
        named = PIECES - 1 - index
        remote(x_out.at[at], x_in.at[at], x_sem.at[0, named], x_sem.at[1, named],
               partner).wait_recv()
        out_ref[at, :] += x_in[at, :].astype(jnp.float32)
    for copy in sent:
        copy.wait_send()
    for offset in order:
        shared[offset].wait_send()


def fold(part, rows, width):
    half_way = rows // 4
    block = part.shape[1:]
    return pl.pallas_call(
        lambda *refs: fold_kernel(rows, *refs),
        out_shape=jax.ShapeDtypeStruct((block[0], width), jnp.float32),
        in_specs=[VMEM],
        out_specs=VMEM,
        scratch_shapes=[
            pltpu.VMEM((rows // 2, *block), jnp.bfloat16),
            pltpu.VMEM((2, half_way, *block), jnp.bfloat16),
            pltpu.VMEM((2, half_way, *block), jnp.bfloat16),
            pltpu.VMEM((rows // 2, block[0] // PIECES, block[1]), jnp.bfloat16),
            pltpu.VMEM((rows // 2, block[0] // PIECES, block[1]), jnp.bfloat16),
            pltpu.VMEM((block[0], width), jnp.bfloat16),
            pltpu.VMEM((block[0], width), jnp.bfloat16),
            pltpu.SemaphoreType.DMA((2, PIECES)),
            pltpu.SemaphoreType.DMA((2, half_way, PIECES)),
            pltpu.SemaphoreType.DMA((2, half_way, PIECES)),
            pltpu.SemaphoreType.DMA((rows // 2,)),
            pltpu.SemaphoreType.DMA((rows // 2,)),
            pltpu.SemaphoreType.DMA((rows // 2,)),
            pltpu.SemaphoreType.DMA((rows // 2,)),
        ],
        compiler_params=pltpu.CompilerParams(
            collective_id=3, has_side_effects=True, vmem_limit_bytes=VMEM_BYTES // 5 * 2
        ),
        name="fold",
    )(part)


def local(
    residual,
    query_states,
    key_states,
    value_states,
    segment_ids,
    sink_logits,
    w_out,
    norm_gain,
    expert_ids,
    route_weight,
    w_gate_up,
    w_down,
):
    tok_rows = query_states.shape[0]
    row_count = lax.axis_size("row")
    col_count = lax.axis_size("col")
    row_index = lax.axis_index("row")
    col_index = lax.axis_index("col")
    local_heads = sink_logits.shape[0]
    group_size = HEADS // KV_HEADS
    if local_heads >= group_size:
        kv_count = local_heads // group_size
        kv_first = col_index * kv_count
    else:
        kv_count = 1
        kv_first = col_index * local_heads // group_size
    kv_width = kv_count * HEAD_DIM
    own_keys = lax.dynamic_slice_in_dim(key_states, kv_first * HEAD_DIM, kv_width, 1)
    own_values = lax.dynamic_slice_in_dim(value_states, kv_first * HEAD_DIM, kv_width, 1)
    shift_count = (WINDOW + tok_rows - 2) // tok_rows
    block_bytes = 2 * residual.shape[0] * residual.shape[1]
    in_kernels = (
        col_count == 2 and row_count % 4 == 0 and row_count >= 8 and tok_rows % 64 == 0
        and kv_width % 128 == 0 and kv_width * col_count == key_states.shape[1]
        and 4 * row_count * block_bytes < VMEM_BYTES
    )
    routing = jnp.concatenate([expert_ids.astype(jnp.float32), route_weight], 1).T
    key_parts = []
    value_parts = []
    segment_parts = []
    start_parts = []
    if in_kernels:
        keys_before, values_before, segments_before = halo(
            key_states, value_states, segment_ids, row_count, shift_count, kv_width
        )
    for offset in range(shift_count, 0, -1):
        if in_kernels:
            arrived = (
                keys_before[offset - 1],
                values_before[offset - 1],
                segments_before[offset - 1, 0],
            )
        else:
            arrived = shifted((own_keys, own_values, segment_ids), "row", offset)
        key_parts.append(arrived[0])
        value_parts.append(arrived[1])
        segment_parts.append(arrived[2])
        start_parts.append((row_index - offset) * tok_rows)
    key_parts.append(own_keys)
    value_parts.append(own_values)
    segment_parts.append(segment_ids)
    start_parts.append(row_index * tok_rows)
    key_groups = jnp.concatenate(key_parts, 0).reshape(-1, kv_count, HEAD_DIM)
    value_groups = jnp.concatenate(value_parts, 0).reshape(-1, kv_count, HEAD_DIM)
    key_segments = jnp.concatenate(segment_parts, 0)
    positions = jnp.arange(tok_rows, dtype=jnp.int32)
    key_position = jnp.concatenate([start + positions for start in start_parts], 0)
    query_position = row_index * tok_rows + positions
    allowed = (key_position[None, :] >= 0) & (key_position[None, :] <= query_position[:, None])
    allowed = allowed & (key_position[None, :] > query_position[:, None] - WINDOW)
    allowed = allowed & (key_segments[None, :] == segment_ids[:, None])
    query_groups = query_states.reshape(tok_rows, kv_count, local_heads // kv_count, HEAD_DIM)
    sink_groups = sink_logits.reshape(kv_count, local_heads // kv_count, 1, 1)
    attended = attend(query_groups, key_groups, value_groups, allowed, sink_groups).reshape(
        tok_rows, local_heads * HEAD_DIM
    )
    partial_value = jnp.dot(attended, w_out, preferred_element_type=jnp.float32)
    feature_count = residual.shape[1] // col_count
    experts_all = w_gate_up.shape[0] * row_count
    slot_cap = max(2, 2 * TOP * tok_rows // experts_all)
    expert_gate_up = w_gate_up[0]
    expert_down = w_down[0]
    partial_value = partial_value.astype(jnp.bfloat16)
    if in_kernels:
        stream, gathered, routing = spread(partial_value, residual, norm_gain, routing, row_count)
    else:
        summed = lax.psum(partial_value, "col").astype(jnp.float32)
        stream = (residual.astype(jnp.float32) + summed).astype(jnp.bfloat16)
        gathered = lax.all_gather(normalize(stream, norm_gain), "row", axis=0, tiled=False)
        routing = lax.all_gather(routing, "row", axis=0, tiled=False)
    stream_part = lax.dynamic_slice_in_dim(stream, col_index * feature_count, feature_count, 1)
    names_mine = routing[:, :TOP] == row_index.astype(jnp.float32)
    mine = jnp.any(names_mine, axis=1)
    weight = jnp.sum(jnp.where(names_mine, routing[:, TOP:], 0.0), axis=1)
    token_order = jnp.arange(tok_rows, dtype=jnp.int32)
    not_after = (token_order[:, None] <= token_order[None, :]).astype(jnp.bfloat16)
    slot_of = jnp.dot(
        mine.astype(jnp.bfloat16), not_after, preferred_element_type=jnp.float32
    ).astype(jnp.int32) - 1
    slots = jnp.arange(slot_cap, dtype=jnp.int32)
    chosen = mine[:, None, :] & (slot_of[:, None, :] == slots[None, :, None])
    selector = chosen.astype(jnp.bfloat16)
    combine = jnp.where(chosen, weight[:, None, :], 0.0)
    packed = jnp.einsum(
        "nst,ntd->nsd", selector, gathered, preferred_element_type=jnp.float32
    ).astype(jnp.bfloat16).reshape(row_count * slot_cap, -1)
    gate = jnp.dot(packed, expert_gate_up[0], preferred_element_type=jnp.float32)
    up = jnp.dot(packed, expert_gate_up[1], preferred_element_type=jnp.float32)
    active = ((up + 1.0) * gate * jax.nn.sigmoid(1.702 * gate)).astype(jnp.bfloat16)
    expert_partial = jnp.dot(active, expert_down, preferred_element_type=jnp.float32)
    scaled = expert_partial.reshape(row_count, slot_cap, -1) * jnp.sum(combine, 2)[:, :, None]
    mixed = jnp.einsum(
        "nst,nsd->ntd", selector, scaled.astype(jnp.bfloat16), preferred_element_type=jnp.float32
    ).astype(jnp.bfloat16)
    if in_kernels:
        mixed = fold(mixed, row_count, feature_count)
    else:
        mixed = mixed.reshape(row_count * tok_rows, -1)
        mixed = lax.psum_scatter(mixed, "row", scatter_dimension=0, tiled=True)
        mixed = lax.psum_scatter(mixed, "col", scatter_dimension=1, tiled=True)
    return (stream_part.astype(jnp.float32) + mixed.astype(jnp.float32)).astype(jnp.bfloat16)


def solution(mesh):
    in_specs = (
        P("row", None),
        P("row", "col"),
        P("row", None),
        P("row", None),
        P("row"),
        P("col"),
        P("col", None),
        P(),
        P("row", None),
        P("row", None),
        P("row", None, None, "col"),
        P("row", "col", None),
    )
    out_specs = P("row", "col")
    return jax.shard_map(local, mesh=mesh, in_specs=in_specs, out_specs=out_specs, check_vma=False)
```

```python
import jax
import jax.numpy as jnp
from jax import lax
from jax.experimental import pallas as pl
from jax.experimental.pallas import tpu as pltpu
from jax.sharding import PartitionSpec as P

HEADS = 64
KV_HEADS = 8
HEAD_DIM = 64
WINDOW = 128
TOP = 4


epsilon = 1e-05
masked_score = -1e30


def shifted(shard, axis, by):
    size = lax.axis_size(axis)
    pairs = [(i, i + by) for i in range(size) if 0 <= i + by < size]
    return lax.ppermute(shard, axis, pairs)


def normalize(stream_rows, norm_gain):
    values32 = stream_rows.astype(jnp.float32)
    square_mean = jnp.mean(values32 * values32, axis=-1, keepdims=True)
    return (values32 * lax.rsqrt(square_mean + epsilon) * norm_gain).astype(jnp.bfloat16)


def attend(query_groups, key_groups, value_groups, allowed, sink_groups):
    scores = jnp.einsum(
        "tgjd,lgd->gjtl", query_groups, key_groups, preferred_element_type=jnp.float32
    )
    scores = scores * query_groups.shape[-1] ** (-0.5)
    scores = jnp.where(allowed[None, None], scores, masked_score)
    peak_score = jnp.maximum(jnp.max(scores, axis=-1, keepdims=True), sink_groups)
    numerator = jnp.exp(scores - peak_score)
    denominator = jnp.exp(sink_groups - peak_score) + jnp.sum(numerator, axis=-1, keepdims=True)
    weights = (numerator / denominator).astype(jnp.bfloat16)
    return jnp.einsum(
        "gjtl,lgd->tgjd", weights, value_groups, preferred_element_type=jnp.float32
    ).astype(jnp.bfloat16)


MESH = pl.DeviceIdType.MESH
VMEM = pl.BlockSpec(memory_space=pltpu.VMEM)
PIECES = 4
VMEM_BYTES = 60 * 1024 * 1024


def ring_place(row, chips):
    chip = lax.div(row, 2)
    along = lax.div(chip, 2)
    return jnp.where(lax.rem(chip, 2) == 0, along, chips - 1 - along)


def ring_row(place, chips, core):
    place = lax.rem(place + chips, chips)
    chip = jnp.where(place < chips // 2, 2 * place, 2 * (chips - 1 - place) + 1)
    return 2 * chip + core


def greet(devices):
    barrier = pltpu.get_barrier_semaphore()
    for device in devices:
        pl.semaphore_signal(barrier, inc=1, device_id=device, device_id_type=MESH)
    pl.semaphore_wait(barrier, len(devices))


def remote(src, dst, send, recv, device):
    return pltpu.make_async_remote_copy(
        src_ref=src, dst_ref=dst, send_sem=send, recv_sem=recv, device_id=device,
        device_id_type=MESH,
    )


def halo_kernel(rows, shifts, key_ref, value_ref, segment_ref, key_out, value_out, segment_out, send, recv):
    row = lax.axis_index("row")
    col = lax.axis_index("col")
    after = [{"row": lax.rem(row + shift, rows)} for shift in range(1, shifts + 1)]
    before = [{"row": lax.rem(row + rows - shift, rows)} for shift in range(1, shifts + 1)]
    greet(after + before)
    width = key_out.shape[2]
    lanes = pl.ds(pl.multiple_of(col * width, width), width)
    copies = []
    for at in range(shifts):
        for which, (src, dst) in enumerate([
            (segment_ref, segment_out.at[at]),
            (key_ref.at[:, lanes], key_out.at[at]),
            (value_ref.at[:, lanes], value_out.at[at]),
        ]):
            copies.append(remote(src, dst, send.at[at, which], recv.at[at, which], after[at]))
    for copy in copies:
        copy.start()
    for copy in copies:
        copy.wait()


def halo(keys, values, segments, rows, shifts, width):
    tokens = keys.shape[0]
    return pl.pallas_call(
        lambda *refs: halo_kernel(rows, shifts, *refs),
        out_shape=(
            jax.ShapeDtypeStruct((shifts, tokens, width), keys.dtype),
            jax.ShapeDtypeStruct((shifts, tokens, width), values.dtype),
            jax.ShapeDtypeStruct((shifts, 1, tokens), segments.dtype),
        ),
        in_specs=[VMEM] * 3,
        out_specs=(VMEM,) * 3,
        scratch_shapes=[
            pltpu.SemaphoreType.DMA((shifts, 3)),
            pltpu.SemaphoreType.DMA((shifts, 3)),
        ],
        compiler_params=pltpu.CompilerParams(
            collective_id=1, has_side_effects=True, vmem_limit_bytes=16 * 1024 * 1024
        ),
        name="halo",
    )(keys, values, segments.reshape(1, -1))


def ring_pieces(distance, half_way, way):
    if distance < half_way:
        return [1, 2, 0]
    return [1, 0] if way == 0 else [2]


def piece_rows(index, size):
    col = lax.axis_index("col")
    start = (index + col * (PIECES - 1 - 2 * index)) * size
    return pl.ds(pl.multiple_of(start, size), size)


def tiles(total, step):
    return [(start, min(step, total - start)) for start in range(0, total, step)]


def expert_kernel(rows, cap, partial_ref, residual_ref, gain_ref, meta_ref, gate_up_hbm, down_hbm, out_ref,
                  gate_up, down, gathered, metas, part_in, stream, packed, active, slot_weight, select,
                  slots, sib_slots, mix, ring_in, ring_out, over_in, keep, x_out, x_in,
                  w_sem, x_sem, c_send, c_recv, m_send, m_recv, n_send, n_recv, l_sem, send, recv,
                  over_send, over_recv, sib_send, sib_recv, slot_sem, f_send, f_recv, fo_send, fo_recv, fx_sem):
    chips = rows // 2
    half_way = chips // 2
    row = lax.axis_index("row")
    col = lax.axis_index("col")
    core = lax.rem(row, 2)
    place = ring_place(row, chips)
    other = row + 1 - 2 * core
    sibling = {"row": other}
    partner = {"col": 1 - col}
    ways = [{"row": ring_row(place + 1, chips, core)}, {"row": ring_row(place - 1, chips, core)}]
    loads = [
        pltpu.make_async_copy(gate_up_hbm.at[0], gate_up, w_sem.at[0]),
        pltpu.make_async_copy(down_hbm.at[0], down, w_sem.at[1]),
    ]
    for load in loads:
        load.start()
    greet([sibling, partner] + ways)
    tokens = partial_ref.shape[0]
    size = tokens // PIECES
    crosses = {}
    for index in [2, 1, 3, 0]:
        at = piece_rows(index, size)
        named = PIECES - 1 - index
        crosses[index] = remote(partial_ref.at[at], part_in.at[at], c_send.at[named],
                                c_recv.at[named], partner)
        crosses[index].start()
    local_meta = pltpu.make_async_copy(meta_ref, metas.at[row], l_sem)
    local_meta.start()

    def ready(index):
        at = piece_rows(index, size)
        remote(partial_ref.at[at], part_in.at[at], c_send.at[index], c_recv.at[index],
               partner).wait_recv()
        summed = partial_ref[at, :].astype(jnp.float32) + part_in[at, :].astype(jnp.float32)
        total = (residual_ref[at, :].astype(jnp.float32) + summed).astype(jnp.bfloat16)
        stream[at, :] = total
        gathered[row, at, :] = normalize(total, gain_ref[...])

    def part(offset, index, which):
        return gathered.at[ring_row(place + offset, chips, which), piece_rows(index, size)]

    def offset_of(way, distance):
        return -distance if way == 0 else distance

    def hop(way, distance, index, sending):
        at = part(offset_of(way, distance - 1 if sending else distance), index, core)
        return remote(at, at, send.at[way, distance - 1, index], recv.at[way, distance - 1, index],
                      ways[way])

    def over(way, distance, sending):
        at = part(offset_of(way, distance), 0 if sending else PIECES - 1, core)
        return remote(at, at, over_send.at[way, distance - 1], over_recv.at[way, distance - 1],
                      partner)

    def pass_on(way, distance, index, which):
        at = part(offset_of(way, distance), index, which)
        return remote(at, at, sib_send.at[way, distance, index], sib_recv.at[way, distance, index],
                      sibling)

    def routing_hop(way, distance, sending):
        back = offset_of(way, distance - 1 if sending else distance)
        at = metas.at[ring_row(place + back, chips, core)]
        return remote(at, at, m_send.at[way, distance - 1], m_recv.at[way, distance - 1], ways[way])

    def routing_on(way, distance, which):
        at = metas.at[ring_row(place + offset_of(way, distance), chips, which)]
        return remote(at, at, n_send.at[way, distance], n_recv.at[way, distance], sibling)

    sent = []

    def go(copy):
        copy.start()
        sent.append(copy)

    reach = [half_way, half_way - 1]
    theirs = gathered.at[other]

    def offsets(distances):
        found = []
        for distance in reversed(distances):
            found += sorted({distance, (chips - distance) % chips})
        return found

    def blocks_of(distances):
        return [(offset, which) for which in range(2) for offset in offsets(distances)]

    def wait_for(distances):
        for distance in distances:
            if distance == 0:
                remote(theirs, theirs, x_sem.at[0], x_sem.at[1], sibling).wait_recv()
                routing_on(0, 0, 1 - core).wait_recv()
                continue
            for way in range(2):
                if distance <= reach[way]:
                    routing_on(way, distance, 1 - core).wait_recv()
                indices = list(ring_pieces(distance, half_way, way))
                for index in indices + ([PIECES - 1] if 0 in indices else []):
                    pass_on(way, distance, index, 1 - core).wait_recv()

    def pack(distances):
        blocks = blocks_of(distances)
        not_after = lax.broadcasted_iota(jnp.int32, (tokens, tokens), 0) <= lax.broadcasted_iota(
            jnp.int32, (tokens, tokens), 1
        )
        not_after = jnp.where(not_after, 1.0, 0.0).astype(jnp.bfloat16)
        numbers = lax.broadcasted_iota(jnp.int32, (cap, tokens), 0).astype(jnp.float32)
        named, weights = [], []
        wanted = [(offset, which, row) for offset, which in blocks]
        wanted += [(offset, 0, other) for offset, which in blocks if which == 0]
        for offset, which, expert in wanted:
            meta = metas[ring_row(place + offset, chips, core if which == 0 else 1 - core)]
            hit = jnp.where(meta[:TOP] == expert.astype(jnp.float32), 1.0, 0.0)
            named.append(jnp.max(hit, axis=0, keepdims=True))
            weights.append(jnp.sum(hit * meta[TOP:], axis=0, keepdims=True))
        hits = jnp.concatenate(named, 0)
        order = jnp.dot(hits.astype(jnp.bfloat16), not_after, preferred_element_type=jnp.float32)
        chosen = [
            jnp.where(order[at:at + 1] == numbers + 1.0, 1.0, 0.0) * named[at]
            for at in range(len(wanted))
        ]
        for at, (offset, which) in enumerate(blocks):
            here = pl.ds(at * cap, cap)
            weight = jnp.sum(chosen[at] * weights[at], axis=1, keepdims=True)
            slot_weight[here, :] = jnp.broadcast_to(weight, (cap, slot_weight.shape[1]))
            source = ring_row(place + offset, chips, core if which == 0 else 1 - core)
            packed[here, :] = jnp.dot(
                chosen[at].astype(jnp.bfloat16), gathered[source],
                preferred_element_type=jnp.float32,
            ).astype(jnp.bfloat16)
        for at, (offset, which) in enumerate(blocks[:len(blocks) // 2]):
            both = jnp.concatenate([chosen[at], chosen[len(blocks) + at]], 0)
            select[offset] = both.T.astype(jnp.bfloat16)

    def gate_and_up(distances, start, width):
        count = cap * len(blocks_of(distances))
        values = packed[:count, :]
        lanes = pl.ds(start, width)
        gate = jnp.dot(values, gate_up[0, :, lanes], preferred_element_type=jnp.float32)
        up = jnp.dot(values, gate_up[1, :, lanes], preferred_element_type=jnp.float32)
        active[:count, lanes] = ((up + 1.0) * gate * jax.nn.sigmoid(1.702 * gate)).astype(jnp.bfloat16)

    def go_down(distances, start, width):
        blocks = blocks_of(distances)
        count = cap * len(blocks)
        lanes = pl.ds(start, width)
        result = jnp.dot(active[:count, :], down[:, lanes], preferred_element_type=jnp.float32)
        result = (result * slot_weight[:count, :1]).astype(jnp.bfloat16)
        for at, (offset, which) in enumerate(blocks):
            piece = result[at * cap:(at + 1) * cap]
            if which == 0:
                slots[offset, :cap, lanes] = piece
            else:
                sib_slots[offset, :, lanes] = piece

    def slot_copy(offset):
        return remote(sib_slots.at[offset], slots.at[offset, pl.ds(cap, cap)], slot_sem.at[0, offset],
                      slot_sem.at[1, offset], sibling)

    queue = []

    def work(count):
        for _ in range(min(count, len(queue))):
            queue.pop(0)()

    def enqueue(distances, first):
        queue.append(lambda: wait_for(distances))
        queue.append(lambda: pack(distances))
        if first:
            queue.append(lambda: loads[0].wait())
        for start, width in tiles(gate_up.shape[2], 256):
            queue.append(lambda start=start, width=width: gate_and_up(distances, start, width))
        if first:
            queue.append(lambda: loads[1].wait())
        for start, width in tiles(down.shape[1], 512):
            queue.append(lambda start=start, width=width: go_down(distances, start, width))
        queue.append(lambda: [go(slot_copy(offset)) for offset in offsets(distances)])

    near, mid = half_way // 4, half_way // 2
    batches = [range(near + 1), range(near + 1, mid + 1), range(mid + 1, half_way + 1)]
    for index in [1, 2, 0]:
        ready(index)
        for way in range(2):
            if index in ring_pieces(1, half_way, way):
                go(hop(way, 1, index, True))
    ready(PIECES - 1)
    local_meta.wait()
    for way in range(2):
        go(routing_hop(way, 1, True))
    go(routing_on(0, 0, core))
    mine = gathered.at[row]
    go(remote(mine, mine, x_sem.at[0], x_sem.at[1], sibling))

    def take_over(distance):
        for way in range(2):
            if distance > 0 and 0 in ring_pieces(distance, half_way, way):
                over(way, distance, False).wait_recv()
                go(pass_on(way, distance, PIECES - 1, core))

    for distance in range(1, half_way + 1):
        for index in [1, 2, 0]:
            for way in range(2):
                if index not in ring_pieces(distance, half_way, way):
                    continue
                hop(way, distance, index, False).wait_recv()
                if distance < half_way and index in ring_pieces(distance + 1, half_way, way):
                    go(hop(way, distance + 1, index, True))
                if index == 0:
                    go(over(way, distance, True))
                go(pass_on(way, distance, index, core))
            if index == 2:
                take_over(distance - 1)
            work(5)
        for way in range(2):
            if distance <= reach[way]:
                routing_hop(way, distance, False).wait_recv()
                if distance < reach[way]:
                    go(routing_hop(way, distance + 1, True))
                go(routing_on(way, distance, core))
        if distance == near + 1:
            enqueue(batches[0], True)
            work(4)
        if distance == mid + 1:
            work(len(queue))
            enqueue(batches[1], False)
    work(3)
    take_over(half_way)
    work(len(queue))
    enqueue(batches[2], False)
    work(len(queue))

    def combine(offset):
        slot_copy(offset).wait_recv()
        mix[offset] = jnp.dot(
            select[offset], slots[offset], preferred_element_type=jnp.float32
        ).astype(jnp.bfloat16)

    def fold_hop(way, distance, index):
        at = pl.ds(index * size, size)
        return remote(ring_out.at[way, distance - 1, at], ring_in.at[way, distance - 1, at],
                      f_send.at[way, distance - 1, index], f_recv.at[way, distance - 1, index],
                      ways[way])

    def arrived(way, distance, index):
        fold_hop(way, distance, index).wait_recv()
        return ring_in[way, distance - 1, pl.ds(index * size, size), :].astype(jnp.float32)

    def fold_over(offset):
        return remote(mix.at[offset, piece_rows(PIECES - 1, size)], over_in.at[offset],
                      fo_send.at[offset], fo_recv.at[offset], partner)

    for distance in range(half_way, 0, -1):
        for offset in offsets([distance]):
            combine(offset)
            go(fold_over(offset))
        for index in [1, 2, 0]:
            for way in range(2):
                if index not in ring_pieces(distance, half_way, way):
                    continue
                offset = distance if way == 0 else chips - distance
                value = mix[offset, piece_rows(index, size), :].astype(jnp.float32)
                if index == 0:
                    fold_over(offset).wait_recv()
                    value = value + over_in[offset].astype(jnp.float32)
                if distance < half_way and index in ring_pieces(distance + 1, half_way, way):
                    value = value + arrived(way, distance + 1, index)
                ring_out[way, distance - 1, pl.ds(index * size, size), :] = value.astype(
                    jnp.bfloat16
                )
                go(fold_hop(way, distance, index))
    combine(0)
    width = out_ref.shape[1]
    for index in [3, 1, 2, 0]:
        at = piece_rows(index, size)
        value = mix[0, at, :].astype(jnp.float32)
        for way in range(2):
            if index in ring_pieces(1, half_way, way):
                value = value + arrived(way, 1, index)
        low, high = value[:, :width], value[:, width:]
        x_out[at, :] = jnp.where(col == 0, high, low).astype(jnp.bfloat16)
        go(remote(x_out.at[at], x_in.at[at], fx_sem.at[0, index], fx_sem.at[1, index], partner))
        base = stream[at, :].astype(jnp.float32)
        keep[at, :] = jnp.where(col == 0, low, high) + jnp.where(
            col == 0, base[:, :width], base[:, width:]
        )
    for index in [0, 2, 1, 3]:
        at = piece_rows(index, size)
        named = PIECES - 1 - index
        remote(x_out.at[at], x_in.at[at], fx_sem.at[0, named], fx_sem.at[1, named],
               partner).wait_recv()
        out_ref[at, :] = (keep[at, :] + x_in[at, :].astype(jnp.float32)).astype(jnp.bfloat16)
    for index in range(PIECES):
        crosses[index].wait_send()
    for copy in sent:
        copy.wait_send()


def expert_layer(partial, residual, gain, meta, w_gate_up, w_down, rows, cap, width):
    half_way = rows // 4
    chips = rows // 2
    tokens, features = residual.shape
    hidden = w_gate_up.shape[3]
    near, mid = half_way // 4, half_way // 2
    most = cap * 2 * max(2 * near + 1, 2 * (mid - near), 2 * (half_way - mid) - 1)
    bf16, f32, dma = jnp.bfloat16, jnp.float32, pltpu.SemaphoreType.DMA
    hbm = pl.BlockSpec(memory_space=pl.ANY)
    return pl.pallas_call(
        lambda *refs: expert_kernel(rows, cap, *refs),
        out_shape=jax.ShapeDtypeStruct((tokens, width), bf16),
        in_specs=[VMEM] * 4 + [hbm] * 2,
        out_specs=VMEM,
        scratch_shapes=[
            pltpu.VMEM(w_gate_up.shape[1:], bf16),
            pltpu.VMEM(w_down.shape[1:], bf16),
            pltpu.VMEM((rows, tokens, features), bf16),
            pltpu.VMEM((rows, *meta.shape), meta.dtype),
            pltpu.VMEM((tokens, features), bf16),
            pltpu.VMEM((tokens, features), bf16),
            pltpu.VMEM((most, features), bf16),
            pltpu.VMEM((most, hidden), bf16),
            pltpu.VMEM((most, 128), f32),
            pltpu.VMEM((chips, tokens, 2 * cap), bf16),
            pltpu.VMEM((chips, 2 * cap, features), bf16),
            pltpu.VMEM((chips, cap, features), bf16),
            pltpu.VMEM((chips, tokens, features), bf16),
            pltpu.VMEM((2, half_way, tokens, features), bf16),
            pltpu.VMEM((2, half_way, tokens, features), bf16),
            pltpu.VMEM((chips, tokens // PIECES, features), bf16),
            pltpu.VMEM((tokens, width), f32),
            pltpu.VMEM((tokens, width), bf16),
            pltpu.VMEM((tokens, width), bf16),
            dma((2,)),
            dma((2,)),
            dma((PIECES,)),
            dma((PIECES,)),
            dma((2, half_way)),
            dma((2, half_way)),
            dma((2, half_way + 1)),
            dma((2, half_way + 1)),
            dma,
            dma((2, half_way, PIECES)),
            dma((2, half_way, PIECES)),
            dma((2, half_way)),
            dma((2, half_way)),
            dma((2, half_way + 1, PIECES)),
            dma((2, half_way + 1, PIECES)),
            dma((2, chips)),
            dma((2, half_way, PIECES)),
            dma((2, half_way, PIECES)),
            dma((chips,)),
            dma((chips,)),
            dma((2, PIECES)),
        ],
        compiler_params=pltpu.CompilerParams(
            collective_id=2, has_side_effects=True, vmem_limit_bytes=VMEM_BYTES
        ),
        name="experts",
    )(partial, residual, gain.reshape(1, -1), meta, w_gate_up, w_down)


def local(
    residual,
    query_states,
    key_states,
    value_states,
    segment_ids,
    sink_logits,
    w_out,
    norm_gain,
    expert_ids,
    route_weight,
    w_gate_up,
    w_down,
):
    tok_rows = query_states.shape[0]
    row_count = lax.axis_size("row")
    col_count = lax.axis_size("col")
    row_index = lax.axis_index("row")
    col_index = lax.axis_index("col")
    local_heads = sink_logits.shape[0]
    group_size = HEADS // KV_HEADS
    if local_heads >= group_size:
        kv_count = local_heads // group_size
        kv_first = col_index * kv_count
    else:
        kv_count = 1
        kv_first = col_index * local_heads // group_size
    kv_width = kv_count * HEAD_DIM
    own_keys = lax.dynamic_slice_in_dim(key_states, kv_first * HEAD_DIM, kv_width, 1)
    own_values = lax.dynamic_slice_in_dim(value_states, kv_first * HEAD_DIM, kv_width, 1)
    shift_count = (WINDOW + tok_rows - 2) // tok_rows
    block_bytes = 2 * residual.shape[0] * residual.shape[1]
    experts_all = w_gate_up.shape[0] * row_count
    slot_cap = max(2, 2 * TOP * tok_rows // experts_all)
    weight_bytes = 2 * (w_gate_up.size + w_down.size)
    in_kernels = (
        col_count == 2 and row_count % 4 == 0 and row_count >= 8 and tok_rows % 64 == 0
        and kv_width % 128 == 0 and kv_width * col_count == key_states.shape[1]
        and slot_cap % 16 == 0 and weight_bytes + 4 * row_count * block_bytes < VMEM_BYTES
    )
    routing = jnp.concatenate([expert_ids.astype(jnp.float32), route_weight], 1).T
    key_parts = []
    value_parts = []
    segment_parts = []
    start_parts = []
    if in_kernels:
        keys_before, values_before, segments_before = halo(
            key_states, value_states, segment_ids, row_count, shift_count, kv_width
        )
    for offset in range(shift_count, 0, -1):
        if in_kernels:
            arrived = (
                keys_before[offset - 1],
                values_before[offset - 1],
                segments_before[offset - 1, 0],
            )
        else:
            arrived = shifted((own_keys, own_values, segment_ids), "row", offset)
        key_parts.append(arrived[0])
        value_parts.append(arrived[1])
        segment_parts.append(arrived[2])
        start_parts.append((row_index - offset) * tok_rows)
    key_parts.append(own_keys)
    value_parts.append(own_values)
    segment_parts.append(segment_ids)
    start_parts.append(row_index * tok_rows)
    key_groups = jnp.concatenate(key_parts, 0).reshape(-1, kv_count, HEAD_DIM)
    value_groups = jnp.concatenate(value_parts, 0).reshape(-1, kv_count, HEAD_DIM)
    key_segments = jnp.concatenate(segment_parts, 0)
    positions = jnp.arange(tok_rows, dtype=jnp.int32)
    key_position = jnp.concatenate([start + positions for start in start_parts], 0)
    query_position = row_index * tok_rows + positions
    allowed = (key_position[None, :] >= 0) & (key_position[None, :] <= query_position[:, None])
    allowed = allowed & (key_position[None, :] > query_position[:, None] - WINDOW)
    allowed = allowed & (key_segments[None, :] == segment_ids[:, None])
    query_groups = query_states.reshape(tok_rows, kv_count, local_heads // kv_count, HEAD_DIM)
    sink_groups = sink_logits.reshape(kv_count, local_heads // kv_count, 1, 1)
    attended = attend(query_groups, key_groups, value_groups, allowed, sink_groups).reshape(
        tok_rows, local_heads * HEAD_DIM
    )
    partial_value = jnp.dot(attended, w_out, preferred_element_type=jnp.float32)
    feature_count = residual.shape[1] // col_count
    expert_gate_up = w_gate_up[0]
    expert_down = w_down[0]
    partial_value = partial_value.astype(jnp.bfloat16)
    if in_kernels:
        return expert_layer(
            partial_value, residual, norm_gain, routing, w_gate_up, w_down, row_count, slot_cap,
            feature_count,
        )
    summed = lax.psum(partial_value, "col").astype(jnp.float32)
    stream = (residual.astype(jnp.float32) + summed).astype(jnp.bfloat16)
    gathered = lax.all_gather(normalize(stream, norm_gain), "row", axis=0, tiled=False)
    routing = lax.all_gather(routing, "row", axis=0, tiled=False)
    stream_part = lax.dynamic_slice_in_dim(stream, col_index * feature_count, feature_count, 1)
    names_mine = routing[:, :TOP] == row_index.astype(jnp.float32)
    mine = jnp.any(names_mine, axis=1)
    weight = jnp.sum(jnp.where(names_mine, routing[:, TOP:], 0.0), axis=1)
    token_order = jnp.arange(tok_rows, dtype=jnp.int32)
    not_after = (token_order[:, None] <= token_order[None, :]).astype(jnp.bfloat16)
    slot_of = jnp.dot(
        mine.astype(jnp.bfloat16), not_after, preferred_element_type=jnp.float32
    ).astype(jnp.int32) - 1
    slots = jnp.arange(slot_cap, dtype=jnp.int32)
    chosen = mine[:, None, :] & (slot_of[:, None, :] == slots[None, :, None])
    selector = chosen.astype(jnp.bfloat16)
    combine = jnp.where(chosen, weight[:, None, :], 0.0)
    packed = jnp.einsum(
        "nst,ntd->nsd", selector, gathered, preferred_element_type=jnp.float32
    ).astype(jnp.bfloat16).reshape(row_count * slot_cap, -1)
    gate = jnp.dot(packed, expert_gate_up[0], preferred_element_type=jnp.float32)
    up = jnp.dot(packed, expert_gate_up[1], preferred_element_type=jnp.float32)
    active = ((up + 1.0) * gate * jax.nn.sigmoid(1.702 * gate)).astype(jnp.bfloat16)
    expert_partial = jnp.dot(active, expert_down, preferred_element_type=jnp.float32)
    scaled = expert_partial.reshape(row_count, slot_cap, -1) * jnp.sum(combine, 2)[:, :, None]
    mixed = jnp.einsum(
        "nst,nsd->ntd", selector, scaled.astype(jnp.bfloat16), preferred_element_type=jnp.float32
    ).astype(jnp.bfloat16)
    mixed = mixed.reshape(row_count * tok_rows, -1)
    mixed = lax.psum_scatter(mixed, "row", scatter_dimension=0, tiled=True)
    mixed = lax.psum_scatter(mixed, "col", scatter_dimension=1, tiled=True)
    return (stream_part.astype(jnp.float32) + mixed.astype(jnp.float32)).astype(jnp.bfloat16)


def solution(mesh):
    in_specs = (
        P("row", None),
        P("row", "col"),
        P("row", None),
        P("row", None),
        P("row"),
        P("col"),
        P("col", None),
        P(),
        P("row", None),
        P("row", None),
        P("row", None, None, "col"),
        P("row", "col", None),
    )
    out_specs = P("row", "col")
    return jax.shard_map(local, mesh=mesh, in_specs=in_specs, out_specs=out_specs, check_vma=False)
```

```python
import jax
import jax.numpy as jnp
from jax import lax
from jax.experimental import pallas as pl
from jax.experimental.pallas import tpu as pltpu
from jax.sharding import PartitionSpec as P

HEADS = 64
KV_HEADS = 8
HEAD_DIM = 64
WINDOW = 128
TOP = 4


epsilon = 1e-05
masked_score = -1e30


def shifted(shard, axis, by):
    size = lax.axis_size(axis)
    pairs = [(i, i + by) for i in range(size) if 0 <= i + by < size]
    return lax.ppermute(shard, axis, pairs)


def normalize(stream_rows, norm_gain):
    values32 = stream_rows.astype(jnp.float32)
    square_mean = jnp.mean(values32 * values32, axis=-1, keepdims=True)
    return (values32 * lax.rsqrt(square_mean + epsilon) * norm_gain).astype(jnp.bfloat16)


def attend(query_groups, key_groups, value_groups, allowed, sink_groups):
    scores = jnp.einsum(
        "tgjd,lgd->gjtl", query_groups, key_groups, preferred_element_type=jnp.float32
    )
    scores = scores * query_groups.shape[-1] ** (-0.5)
    scores = jnp.where(allowed[None, None], scores, masked_score)
    peak_score = jnp.maximum(jnp.max(scores, axis=-1, keepdims=True), sink_groups)
    numerator = jnp.exp(scores - peak_score)
    denominator = jnp.exp(sink_groups - peak_score) + jnp.sum(numerator, axis=-1, keepdims=True)
    weights = (numerator / denominator).astype(jnp.bfloat16)
    return jnp.einsum(
        "gjtl,lgd->tgjd", weights, value_groups, preferred_element_type=jnp.float32
    ).astype(jnp.bfloat16)


MESH = pl.DeviceIdType.MESH
VMEM = pl.BlockSpec(memory_space=pltpu.VMEM)
PIECES = 4
VMEM_BYTES = 60 * 1024 * 1024


def ring_place(row, chips):
    chip = lax.div(row, 2)
    along = lax.div(chip, 2)
    return jnp.where(lax.rem(chip, 2) == 0, along, chips - 1 - along)


def ring_row(place, chips, core):
    place = lax.rem(place + chips, chips)
    chip = jnp.where(place < chips // 2, 2 * place, 2 * (chips - 1 - place) + 1)
    return 2 * chip + core


def greet(devices):
    barrier = pltpu.get_barrier_semaphore()
    for device in devices:
        pl.semaphore_signal(barrier, inc=1, device_id=device, device_id_type=MESH)
    pl.semaphore_wait(barrier, len(devices))


def remote(src, dst, send, recv, device):
    return pltpu.make_async_remote_copy(
        src_ref=src, dst_ref=dst, send_sem=send, recv_sem=recv, device_id=device,
        device_id_type=MESH,
    )


def halo_kernel(rows, shifts, key_ref, value_ref, segment_ref, key_out, value_out, segment_out, send, recv):
    row = lax.axis_index("row")
    col = lax.axis_index("col")
    after = [{"row": lax.rem(row + shift, rows)} for shift in range(1, shifts + 1)]
    before = [{"row": lax.rem(row + rows - shift, rows)} for shift in range(1, shifts + 1)]
    greet(after + before)
    width = key_out.shape[2]
    lanes = pl.ds(pl.multiple_of(col * width, width), width)
    copies = []
    for at in range(shifts):
        for which, (src, dst) in enumerate([
            (segment_ref, segment_out.at[at]),
            (key_ref.at[:, lanes], key_out.at[at]),
            (value_ref.at[:, lanes], value_out.at[at]),
        ]):
            copies.append(remote(src, dst, send.at[at, which], recv.at[at, which], after[at]))
    for copy in copies:
        copy.start()
    for copy in copies:
        copy.wait()


def halo(keys, values, segments, rows, shifts, width):
    tokens = keys.shape[0]
    return pl.pallas_call(
        lambda *refs: halo_kernel(rows, shifts, *refs),
        out_shape=(
            jax.ShapeDtypeStruct((shifts, tokens, width), keys.dtype),
            jax.ShapeDtypeStruct((shifts, tokens, width), values.dtype),
            jax.ShapeDtypeStruct((shifts, 1, tokens), segments.dtype),
        ),
        in_specs=[VMEM] * 3,
        out_specs=(VMEM,) * 3,
        scratch_shapes=[
            pltpu.SemaphoreType.DMA((shifts, 3)),
            pltpu.SemaphoreType.DMA((shifts, 3)),
        ],
        compiler_params=pltpu.CompilerParams(
            collective_id=1, has_side_effects=True, vmem_limit_bytes=16 * 1024 * 1024
        ),
        name="halo",
    )(keys, values, segments.reshape(1, -1))


def ring_pieces(distance, half_way, way):
    if distance < half_way:
        return [1, 2, 0]
    return [1, 0] if way == 0 else [2]


def piece_rows(index, size):
    col = lax.axis_index("col")
    start = (index + col * (PIECES - 1 - 2 * index)) * size
    return pl.ds(pl.multiple_of(start, size), size)


def tiles(total, step):
    return [(start, min(step, total - start)) for start in range(0, total, step)]


def expert_kernel(rows, cap, partial_ref, residual_ref, gain_ref, meta_ref, gate_up_hbm, down_hbm, out_ref,
                  gate_up, down, gathered, metas, part_in, stream, packed, active, slot_weight, select,
                  slots, sib_slots, mix, ring_in, ring_out, over_in, keep, x_out, x_in,
                  w_sem, x_sem, c_send, c_recv, m_send, m_recv, n_send, n_recv, l_sem, send, recv,
                  over_send, over_recv, sib_send, sib_recv, slot_sem, f_send, f_recv, fo_send, fo_recv, fx_sem):
    chips = rows // 2
    half_way = chips // 2
    row = lax.axis_index("row")
    col = lax.axis_index("col")
    core = lax.rem(row, 2)
    place = ring_place(row, chips)
    other = row + 1 - 2 * core
    sibling = {"row": other}
    partner = {"col": 1 - col}
    ways = [{"row": ring_row(place + 1, chips, core)}, {"row": ring_row(place - 1, chips, core)}]
    loads = [
        pltpu.make_async_copy(gate_up_hbm.at[0], gate_up, w_sem.at[0]),
        pltpu.make_async_copy(down_hbm.at[0], down, w_sem.at[1]),
    ]
    for load in loads:
        load.start()
    greet([sibling, partner] + ways)
    tokens = partial_ref.shape[0]
    size = tokens // PIECES
    crosses = {}
    for index in [2, 1, 3, 0]:
        at = piece_rows(index, size)
        named = PIECES - 1 - index
        crosses[index] = remote(partial_ref.at[at], part_in.at[at], c_send.at[named],
                                c_recv.at[named], partner)
        crosses[index].start()
    local_meta = pltpu.make_async_copy(meta_ref, metas.at[row], l_sem)
    local_meta.start()

    def ready(index):
        at = piece_rows(index, size)
        remote(partial_ref.at[at], part_in.at[at], c_send.at[index], c_recv.at[index],
               partner).wait_recv()
        summed = partial_ref[at, :].astype(jnp.float32) + part_in[at, :].astype(jnp.float32)
        total = (residual_ref[at, :].astype(jnp.float32) + summed).astype(jnp.bfloat16)
        stream[at, :] = total
        gathered[row, at, :] = normalize(total, gain_ref[...])

    def part(offset, index, which):
        return gathered.at[ring_row(place + offset, chips, which), piece_rows(index, size)]

    def offset_of(way, distance):
        return -distance if way == 0 else distance

    def hop(way, distance, index, sending):
        at = part(offset_of(way, distance - 1 if sending else distance), index, core)
        return remote(at, at, send.at[way, distance - 1, index], recv.at[way, distance - 1, index],
                      ways[way])

    def over(way, distance, sending):
        at = part(offset_of(way, distance), 0 if sending else PIECES - 1, core)
        return remote(at, at, over_send.at[way, distance - 1], over_recv.at[way, distance - 1],
                      partner)

    def pass_on(way, distance, index, which):
        at = part(offset_of(way, distance), index, which)
        return remote(at, at, sib_send.at[way, distance, index], sib_recv.at[way, distance, index],
                      sibling)

    def routing_hop(way, distance, sending):
        back = offset_of(way, distance - 1 if sending else distance)
        at = metas.at[ring_row(place + back, chips, core)]
        return remote(at, at, m_send.at[way, distance - 1], m_recv.at[way, distance - 1], ways[way])

    def routing_on(way, distance, which):
        at = metas.at[ring_row(place + offset_of(way, distance), chips, which)]
        return remote(at, at, n_send.at[way, distance], n_recv.at[way, distance], sibling)

    sent = []

    def go(copy):
        copy.start()
        sent.append(copy)

    reach = [half_way, half_way - 1]
    theirs = gathered.at[other]

    def offsets(distances):
        found = []
        for distance in reversed(distances):
            found += sorted({distance, (chips - distance) % chips})
        return found

    def blocks_of(distances):
        return [(offset, which) for which in range(2) for offset in offsets(distances)]

    def wait_for(distances):
        for distance in distances:
            if distance == 0:
                remote(theirs, theirs, x_sem.at[0], x_sem.at[1], sibling).wait_recv()
                routing_on(0, 0, 1 - core).wait_recv()
                continue
            for way in range(2):
                if distance <= reach[way]:
                    routing_on(way, distance, 1 - core).wait_recv()
                indices = list(ring_pieces(distance, half_way, way))
                for index in indices + ([PIECES - 1] if 0 in indices else []):
                    pass_on(way, distance, index, 1 - core).wait_recv()

    def pack(distances):
        blocks = blocks_of(distances)
        not_after = lax.broadcasted_iota(jnp.int32, (tokens, tokens), 0) <= lax.broadcasted_iota(
            jnp.int32, (tokens, tokens), 1
        )
        not_after = jnp.where(not_after, 1.0, 0.0).astype(jnp.bfloat16)
        numbers = lax.broadcasted_iota(jnp.int32, (cap, tokens), 0).astype(jnp.float32)
        named, weights = [], []
        wanted = [(offset, which, row) for offset, which in blocks]
        wanted += [(offset, 0, other) for offset, which in blocks if which == 0]
        for offset, which, expert in wanted:
            meta = metas[ring_row(place + offset, chips, core if which == 0 else 1 - core)]
            hit = jnp.where(meta[:TOP] == expert.astype(jnp.float32), 1.0, 0.0)
            named.append(jnp.max(hit, axis=0, keepdims=True))
            weights.append(jnp.sum(hit * meta[TOP:], axis=0, keepdims=True))
        hits = jnp.concatenate(named, 0)
        order = jnp.dot(hits.astype(jnp.bfloat16), not_after, preferred_element_type=jnp.float32)
        chosen = [
            jnp.where(order[at:at + 1] == numbers + 1.0, 1.0, 0.0) * named[at]
            for at in range(len(wanted))
        ]
        for at, (offset, which) in enumerate(blocks):
            here = pl.ds(at * cap, cap)
            weight = jnp.sum(chosen[at] * weights[at], axis=1, keepdims=True)
            slot_weight[here, :] = jnp.broadcast_to(weight, (cap, slot_weight.shape[1]))
            source = ring_row(place + offset, chips, core if which == 0 else 1 - core)
            packed[here, :] = jnp.dot(
                chosen[at].astype(jnp.bfloat16), gathered[source],
                preferred_element_type=jnp.float32,
            ).astype(jnp.bfloat16)
        for at, (offset, which) in enumerate(blocks[:len(blocks) // 2]):
            both = jnp.concatenate([chosen[at], chosen[len(blocks) + at]], 0)
            select[offset] = both.T.astype(jnp.bfloat16)

    def gate_and_up(distances, start, width):
        count = cap * len(blocks_of(distances))
        values = packed[:count, :]
        lanes = pl.ds(start, width)
        last = (((1,), (1,)), ((), ()))
        gate = lax.dot_general(values, gate_up[0, lanes, :], last, preferred_element_type=jnp.float32)
        up = lax.dot_general(values, gate_up[1, lanes, :], last, preferred_element_type=jnp.float32)
        active[:count, lanes] = ((up + 1.0) * gate * jax.nn.sigmoid(1.702 * gate)).astype(jnp.bfloat16)

    def go_down(distances, start, width):
        blocks = blocks_of(distances)
        count = cap * len(blocks)
        lanes = pl.ds(start, width)
        result = jnp.dot(active[:count, :], down[:, lanes], preferred_element_type=jnp.float32)
        result = (result * slot_weight[:count, :1]).astype(jnp.bfloat16)
        for at, (offset, which) in enumerate(blocks):
            piece = result[at * cap:(at + 1) * cap]
            if which == 0:
                slots[offset, :cap, lanes] = piece
            else:
                sib_slots[offset, :, lanes] = piece

    def slot_copy(offset):
        return remote(sib_slots.at[offset], slots.at[offset, pl.ds(cap, cap)], slot_sem.at[0, offset],
                      slot_sem.at[1, offset], sibling)

    queue = []

    def work(count):
        for _ in range(min(count, len(queue))):
            queue.pop(0)()

    def enqueue(distances, first):
        queue.append(lambda: wait_for(distances))
        queue.append(lambda: pack(distances))
        if first:
            queue.append(lambda: loads[0].wait())
        for start, width in tiles(gate_up.shape[1], 256):
            queue.append(lambda start=start, width=width: gate_and_up(distances, start, width))
        if first:
            queue.append(lambda: loads[1].wait())
        for start, width in tiles(down.shape[1], 512):
            queue.append(lambda start=start, width=width: go_down(distances, start, width))
        queue.append(lambda: [go(slot_copy(offset)) for offset in offsets(distances)])

    near, mid = half_way // 4, half_way // 2
    batches = [range(near + 1), range(near + 1, mid + 1), range(mid + 1, half_way + 1)]
    for index in [1, 2, 0]:
        ready(index)
        for way in range(2):
            if index in ring_pieces(1, half_way, way):
                go(hop(way, 1, index, True))
    ready(PIECES - 1)
    local_meta.wait()
    for way in range(2):
        go(routing_hop(way, 1, True))
    go(routing_on(0, 0, core))
    mine = gathered.at[row]
    go(remote(mine, mine, x_sem.at[0], x_sem.at[1], sibling))

    def take_over(distance):
        for way in range(2):
            if distance > 0 and 0 in ring_pieces(distance, half_way, way):
                over(way, distance, False).wait_recv()
                go(pass_on(way, distance, PIECES - 1, core))

    for distance in range(1, half_way + 1):
        for index in [1, 2, 0]:
            for way in range(2):
                if index not in ring_pieces(distance, half_way, way):
                    continue
                hop(way, distance, index, False).wait_recv()
                if distance < half_way and index in ring_pieces(distance + 1, half_way, way):
                    go(hop(way, distance + 1, index, True))
                if index == 0:
                    go(over(way, distance, True))
                go(pass_on(way, distance, index, core))
            if index == 2:
                take_over(distance - 1)
            work(5)
        for way in range(2):
            if distance <= reach[way]:
                routing_hop(way, distance, False).wait_recv()
                if distance < reach[way]:
                    go(routing_hop(way, distance + 1, True))
                go(routing_on(way, distance, core))
        if distance == near + 1:
            enqueue(batches[0], True)
            work(4)
        if distance == mid + 1:
            work(len(queue))
            enqueue(batches[1], False)
    work(3)
    take_over(half_way)
    work(len(queue))
    enqueue(batches[2], False)
    work(len(queue))

    def combine(offset):
        slot_copy(offset).wait_recv()
        mix[offset] = jnp.dot(
            select[offset], slots[offset], preferred_element_type=jnp.float32
        ).astype(jnp.bfloat16)

    def fold_hop(way, distance, index):
        at = pl.ds(index * size, size)
        return remote(ring_out.at[way, distance - 1, at], ring_in.at[way, distance - 1, at],
                      f_send.at[way, distance - 1, index], f_recv.at[way, distance - 1, index],
                      ways[way])

    def arrived(way, distance, index):
        fold_hop(way, distance, index).wait_recv()
        return ring_in[way, distance - 1, pl.ds(index * size, size), :].astype(jnp.float32)

    def fold_over(offset):
        return remote(mix.at[offset, piece_rows(PIECES - 1, size)], over_in.at[offset],
                      fo_send.at[offset], fo_recv.at[offset], partner)

    for distance in range(half_way, 0, -1):
        for offset in offsets([distance]):
            combine(offset)
            go(fold_over(offset))
        for index in [1, 2, 0]:
            for way in range(2):
                if index not in ring_pieces(distance, half_way, way):
                    continue
                offset = distance if way == 0 else chips - distance
                value = mix[offset, piece_rows(index, size), :].astype(jnp.float32)
                if index == 0:
                    fold_over(offset).wait_recv()
                    value = value + over_in[offset].astype(jnp.float32)
                if distance < half_way and index in ring_pieces(distance + 1, half_way, way):
                    value = value + arrived(way, distance + 1, index)
                ring_out[way, distance - 1, pl.ds(index * size, size), :] = value.astype(
                    jnp.bfloat16
                )
                go(fold_hop(way, distance, index))
    combine(0)
    width = out_ref.shape[1]
    for index in [3, 1, 2, 0]:
        at = piece_rows(index, size)
        value = mix[0, at, :].astype(jnp.float32)
        for way in range(2):
            if index in ring_pieces(1, half_way, way):
                value = value + arrived(way, 1, index)
        low, high = value[:, :width], value[:, width:]
        x_out[at, :] = jnp.where(col == 0, high, low).astype(jnp.bfloat16)
        go(remote(x_out.at[at], x_in.at[at], fx_sem.at[0, index], fx_sem.at[1, index], partner))
        base = stream[at, :].astype(jnp.float32)
        keep[at, :] = jnp.where(col == 0, low, high) + jnp.where(
            col == 0, base[:, :width], base[:, width:]
        )
    for index in [0, 2, 1, 3]:
        at = piece_rows(index, size)
        named = PIECES - 1 - index
        remote(x_out.at[at], x_in.at[at], fx_sem.at[0, named], fx_sem.at[1, named],
               partner).wait_recv()
        out_ref[at, :] = (keep[at, :] + x_in[at, :].astype(jnp.float32)).astype(jnp.bfloat16)
    for index in range(PIECES):
        crosses[index].wait_send()
    for copy in sent:
        copy.wait_send()


def expert_layer(partial, residual, gain, meta, w_gate_up, w_down, rows, cap, width):
    w_gate_up = jnp.swapaxes(w_gate_up, 2, 3)
    half_way = rows // 4
    chips = rows // 2
    tokens, features = residual.shape
    hidden = w_gate_up.shape[2]
    near, mid = half_way // 4, half_way // 2
    most = cap * 2 * max(2 * near + 1, 2 * (mid - near), 2 * (half_way - mid) - 1)
    bf16, f32, dma = jnp.bfloat16, jnp.float32, pltpu.SemaphoreType.DMA
    hbm = pl.BlockSpec(memory_space=pl.ANY)
    return pl.pallas_call(
        lambda *refs: expert_kernel(rows, cap, *refs),
        out_shape=jax.ShapeDtypeStruct((tokens, width), bf16),
        in_specs=[VMEM] * 4 + [hbm] * 2,
        out_specs=VMEM,
        scratch_shapes=[
            pltpu.VMEM(w_gate_up.shape[1:], bf16),
            pltpu.VMEM(w_down.shape[1:], bf16),
            pltpu.VMEM((rows, tokens, features), bf16),
            pltpu.VMEM((rows, *meta.shape), meta.dtype),
            pltpu.VMEM((tokens, features), bf16),
            pltpu.VMEM((tokens, features), bf16),
            pltpu.VMEM((most, features), bf16),
            pltpu.VMEM((most, hidden), bf16),
            pltpu.VMEM((most, 128), f32),
            pltpu.VMEM((chips, tokens, 2 * cap), bf16),
            pltpu.VMEM((chips, 2 * cap, features), bf16),
            pltpu.VMEM((chips, cap, features), bf16),
            pltpu.VMEM((chips, tokens, features), bf16),
            pltpu.VMEM((2, half_way, tokens, features), bf16),
            pltpu.VMEM((2, half_way, tokens, features), bf16),
            pltpu.VMEM((chips, tokens // PIECES, features), bf16),
            pltpu.VMEM((tokens, width), f32),
            pltpu.VMEM((tokens, width), bf16),
            pltpu.VMEM((tokens, width), bf16),
            dma((2,)),
            dma((2,)),
            dma((PIECES,)),
            dma((PIECES,)),
            dma((2, half_way)),
            dma((2, half_way)),
            dma((2, half_way + 1)),
            dma((2, half_way + 1)),
            dma,
            dma((2, half_way, PIECES)),
            dma((2, half_way, PIECES)),
            dma((2, half_way)),
            dma((2, half_way)),
            dma((2, half_way + 1, PIECES)),
            dma((2, half_way + 1, PIECES)),
            dma((2, chips)),
            dma((2, half_way, PIECES)),
            dma((2, half_way, PIECES)),
            dma((chips,)),
            dma((chips,)),
            dma((2, PIECES)),
        ],
        compiler_params=pltpu.CompilerParams(
            collective_id=2, has_side_effects=True, vmem_limit_bytes=VMEM_BYTES
        ),
        name="experts",
    )(partial, residual, gain.reshape(1, -1), meta, w_gate_up, w_down)


def local(
    residual,
    query_states,
    key_states,
    value_states,
    segment_ids,
    sink_logits,
    w_out,
    norm_gain,
    expert_ids,
    route_weight,
    w_gate_up,
    w_down,
):
    tok_rows = query_states.shape[0]
    row_count = lax.axis_size("row")
    col_count = lax.axis_size("col")
    row_index = lax.axis_index("row")
    col_index = lax.axis_index("col")
    local_heads = sink_logits.shape[0]
    group_size = HEADS // KV_HEADS
    if local_heads >= group_size:
        kv_count = local_heads // group_size
        kv_first = col_index * kv_count
    else:
        kv_count = 1
        kv_first = col_index * local_heads // group_size
    kv_width = kv_count * HEAD_DIM
    own_keys = lax.dynamic_slice_in_dim(key_states, kv_first * HEAD_DIM, kv_width, 1)
    own_values = lax.dynamic_slice_in_dim(value_states, kv_first * HEAD_DIM, kv_width, 1)
    shift_count = (WINDOW + tok_rows - 2) // tok_rows
    block_bytes = 2 * residual.shape[0] * residual.shape[1]
    experts_all = w_gate_up.shape[0] * row_count
    slot_cap = max(2, 2 * TOP * tok_rows // experts_all)
    weight_bytes = 2 * (w_gate_up.size + w_down.size)
    in_kernels = (
        col_count == 2 and row_count % 4 == 0 and row_count >= 8 and tok_rows % 64 == 0
        and kv_width % 128 == 0 and kv_width * col_count == key_states.shape[1]
        and slot_cap % 16 == 0 and weight_bytes + 4 * row_count * block_bytes < VMEM_BYTES
    )
    routing = jnp.concatenate([expert_ids.astype(jnp.float32), route_weight], 1).T
    key_parts = []
    value_parts = []
    segment_parts = []
    start_parts = []
    if in_kernels:
        keys_before, values_before, segments_before = halo(
            key_states, value_states, segment_ids, row_count, shift_count, kv_width
        )
    for offset in range(shift_count, 0, -1):
        if in_kernels:
            arrived = (
                keys_before[offset - 1],
                values_before[offset - 1],
                segments_before[offset - 1, 0],
            )
        else:
            arrived = shifted((own_keys, own_values, segment_ids), "row", offset)
        key_parts.append(arrived[0])
        value_parts.append(arrived[1])
        segment_parts.append(arrived[2])
        start_parts.append((row_index - offset) * tok_rows)
    key_parts.append(own_keys)
    value_parts.append(own_values)
    segment_parts.append(segment_ids)
    start_parts.append(row_index * tok_rows)
    key_groups = jnp.concatenate(key_parts, 0).reshape(-1, kv_count, HEAD_DIM)
    value_groups = jnp.concatenate(value_parts, 0).reshape(-1, kv_count, HEAD_DIM)
    key_segments = jnp.concatenate(segment_parts, 0)
    positions = jnp.arange(tok_rows, dtype=jnp.int32)
    key_position = jnp.concatenate([start + positions for start in start_parts], 0)
    query_position = row_index * tok_rows + positions
    allowed = (key_position[None, :] >= 0) & (key_position[None, :] <= query_position[:, None])
    allowed = allowed & (key_position[None, :] > query_position[:, None] - WINDOW)
    allowed = allowed & (key_segments[None, :] == segment_ids[:, None])
    query_groups = query_states.reshape(tok_rows, kv_count, local_heads // kv_count, HEAD_DIM)
    sink_groups = sink_logits.reshape(kv_count, local_heads // kv_count, 1, 1)
    attended = attend(query_groups, key_groups, value_groups, allowed, sink_groups).reshape(
        tok_rows, local_heads * HEAD_DIM
    )
    partial_value = jnp.dot(attended, w_out, preferred_element_type=jnp.float32)
    feature_count = residual.shape[1] // col_count
    expert_gate_up = w_gate_up[0]
    expert_down = w_down[0]
    partial_value = partial_value.astype(jnp.bfloat16)
    if in_kernels:
        return expert_layer(
            partial_value, residual, norm_gain, routing, w_gate_up, w_down, row_count, slot_cap,
            feature_count,
        )
    summed = lax.psum(partial_value, "col").astype(jnp.float32)
    stream = (residual.astype(jnp.float32) + summed).astype(jnp.bfloat16)
    gathered = lax.all_gather(normalize(stream, norm_gain), "row", axis=0, tiled=False)
    routing = lax.all_gather(routing, "row", axis=0, tiled=False)
    stream_part = lax.dynamic_slice_in_dim(stream, col_index * feature_count, feature_count, 1)
    names_mine = routing[:, :TOP] == row_index.astype(jnp.float32)
    mine = jnp.any(names_mine, axis=1)
    weight = jnp.sum(jnp.where(names_mine, routing[:, TOP:], 0.0), axis=1)
    token_order = jnp.arange(tok_rows, dtype=jnp.int32)
    not_after = (token_order[:, None] <= token_order[None, :]).astype(jnp.bfloat16)
    slot_of = jnp.dot(
        mine.astype(jnp.bfloat16), not_after, preferred_element_type=jnp.float32
    ).astype(jnp.int32) - 1
    slots = jnp.arange(slot_cap, dtype=jnp.int32)
    chosen = mine[:, None, :] & (slot_of[:, None, :] == slots[None, :, None])
    selector = chosen.astype(jnp.bfloat16)
    combine = jnp.where(chosen, weight[:, None, :], 0.0)
    packed = jnp.einsum(
        "nst,ntd->nsd", selector, gathered, preferred_element_type=jnp.float32
    ).astype(jnp.bfloat16).reshape(row_count * slot_cap, -1)
    gate = jnp.dot(packed, expert_gate_up[0], preferred_element_type=jnp.float32)
    up = jnp.dot(packed, expert_gate_up[1], preferred_element_type=jnp.float32)
    active = ((up + 1.0) * gate * jax.nn.sigmoid(1.702 * gate)).astype(jnp.bfloat16)
    expert_partial = jnp.dot(active, expert_down, preferred_element_type=jnp.float32)
    scaled = expert_partial.reshape(row_count, slot_cap, -1) * jnp.sum(combine, 2)[:, :, None]
    mixed = jnp.einsum(
        "nst,nsd->ntd", selector, scaled.astype(jnp.bfloat16), preferred_element_type=jnp.float32
    ).astype(jnp.bfloat16)
    mixed = mixed.reshape(row_count * tok_rows, -1)
    mixed = lax.psum_scatter(mixed, "row", scatter_dimension=0, tiled=True)
    mixed = lax.psum_scatter(mixed, "col", scatter_dimension=1, tiled=True)
    return (stream_part.astype(jnp.float32) + mixed.astype(jnp.float32)).astype(jnp.bfloat16)


def solution(mesh):
    in_specs = (
        P("row", None),
        P("row", "col"),
        P("row", None),
        P("row", None),
        P("row"),
        P("col"),
        P("col", None),
        P(),
        P("row", None),
        P("row", None),
        P("row", None, None, "col"),
        P("row", "col", None),
    )
    out_specs = P("row", "col")
    return jax.shard_map(local, mesh=mesh, in_specs=in_specs, out_specs=out_specs, check_vma=False)
```

```python
import jax
import jax.numpy as jnp
from jax import lax
from jax.experimental import pallas as pl
from jax.experimental.pallas import tpu as pltpu
from jax.sharding import PartitionSpec as P

HEADS = 64
KV_HEADS = 8
HEAD_DIM = 64
WINDOW = 128
TOP = 4


epsilon = 1e-05
masked_score = -1e30


def shifted(shard, axis, by):
    size = lax.axis_size(axis)
    pairs = [(i, i + by) for i in range(size) if 0 <= i + by < size]
    return lax.ppermute(shard, axis, pairs)


def normalize(stream_rows, norm_gain):
    values32 = stream_rows.astype(jnp.float32)
    square_mean = jnp.mean(values32 * values32, axis=-1, keepdims=True)
    return (values32 * lax.rsqrt(square_mean + epsilon) * norm_gain).astype(jnp.bfloat16)


def attend(query_groups, key_groups, value_groups, allowed, sink_groups):
    scores = jnp.einsum(
        "tgjd,lgd->gjtl", query_groups, key_groups, preferred_element_type=jnp.float32
    )
    scores = scores * query_groups.shape[-1] ** (-0.5)
    scores = jnp.where(allowed[None, None], scores, masked_score)
    peak_score = jnp.maximum(jnp.max(scores, axis=-1, keepdims=True), sink_groups)
    numerator = jnp.exp(scores - peak_score)
    denominator = jnp.exp(sink_groups - peak_score) + jnp.sum(numerator, axis=-1, keepdims=True)
    weights = (numerator / denominator).astype(jnp.bfloat16)
    return jnp.einsum(
        "gjtl,lgd->tgjd", weights, value_groups, preferred_element_type=jnp.float32
    ).astype(jnp.bfloat16)


MESH = pl.DeviceIdType.MESH
VMEM = pl.BlockSpec(memory_space=pltpu.VMEM)
PIECES = 4
VMEM_BYTES = 61 * 1024 * 1024


def ring_place(row, chips):
    chip = lax.div(row, 2)
    along = lax.div(chip, 2)
    return jnp.where(lax.rem(chip, 2) == 0, along, chips - 1 - along)


def ring_row(place, chips, core):
    place = lax.rem(place + chips, chips)
    chip = jnp.where(place < chips // 2, 2 * place, 2 * (chips - 1 - place) + 1)
    return 2 * chip + core


def greet(devices):
    barrier = pltpu.get_barrier_semaphore()
    for device in devices:
        pl.semaphore_signal(barrier, inc=1, device_id=device, device_id_type=MESH)
    pl.semaphore_wait(barrier, len(devices))


def remote(src, dst, send, recv, device):
    return pltpu.make_async_remote_copy(
        src_ref=src, dst_ref=dst, send_sem=send, recv_sem=recv, device_id=device,
        device_id_type=MESH,
    )


def ring_pieces(distance, half_way, way):
    if distance < half_way:
        return [1, 2, 0]
    return [1, 0] if way == 0 else [2]


def piece_rows(index, size):
    col = lax.axis_index("col")
    start = (index + col * (PIECES - 1 - 2 * index)) * size
    return pl.ds(pl.multiple_of(start, size), size)


OUT_TILE = 512
BUDGET = 2.0


def attend_all(row, shifts, query_ref, key_all, value_all, segment_ref, segment_all, sink_ref, attended):
    tokens = query_ref.shape[0]
    keys = key_all.shape[0]
    groups = key_all.shape[1] // HEAD_DIM
    heads = sink_ref.shape[1] // groups
    pairs = heads // 2
    lanes = 2 * HEAD_DIM
    segments = [segment_all[at] for at in range(shifts - 1, -1, -1)] + [segment_ref[...]]
    rest = keys - (shifts + 1) * tokens
    if rest:
        segments.append(jnp.full((1, rest), -1, jnp.int32))
    key_segment = jnp.concatenate(segments, 1).astype(jnp.float32)
    diagonal = lax.broadcasted_iota(jnp.int32, (tokens, tokens), 0) == lax.broadcasted_iota(
        jnp.int32, (tokens, tokens), 1
    )
    query_segment = jnp.sum(
        jnp.where(diagonal, segment_ref[...].astype(jnp.float32), 0.0), axis=1, keepdims=True
    )
    query_at = shifts * tokens + lax.broadcasted_iota(jnp.int32, (tokens, keys), 0)
    key_at = lax.broadcasted_iota(jnp.int32, (tokens, keys), 1)
    allowed = (key_at <= query_at) & (key_at > query_at - WINDOW) & (key_at + row * tokens >= shifts * tokens)
    allowed = allowed & (key_segment == query_segment)
    bias = jnp.where(allowed, 0.0, masked_score)
    bias = jnp.concatenate([bias] * pairs, 0).T
    values_turned = value_all[...].astype(jnp.float32).T.astype(jnp.bfloat16)
    lower = lax.broadcasted_iota(jnp.int32, (keys, lanes), 1) < HEAD_DIM
    pair_of = lax.broadcasted_iota(jnp.int32, (1, pairs * tokens), 1)
    nothing = jnp.zeros((HEAD_DIM, keys), jnp.bfloat16)
    for group in range(groups):
        tile = group // 2 * lanes
        straight = key_all[:, tile:tile + lanes]
        turned = jnp.concatenate([straight[:, HEAD_DIM:], straight[:, :HEAD_DIM]], 1)
        first, second = (straight, turned) if group % 2 == 0 else (turned, straight)
        zero = jnp.zeros_like(straight)
        both_keys = jnp.concatenate([jnp.where(lower, first, zero), jnp.where(lower, zero, second)], 0)
        value = values_turned[group * HEAD_DIM:(group + 1) * HEAD_DIM]
        both_values = jnp.concatenate(
            [jnp.concatenate([value, nothing], 1), jnp.concatenate([nothing, value], 1)], 0
        )
        first_lane = group * heads * HEAD_DIM
        queries = jnp.concatenate(
            [query_ref[:, first_lane + pair * lanes:first_lane + (pair + 1) * lanes] for pair in range(pairs)], 0
        )
        scores = lax.dot_general(
            both_keys, queries, (((1,), (1,)), ((), ())), preferred_element_type=jnp.float32
        )
        halves = []
        for half in range(2):
            sink = jnp.full(pair_of.shape, sink_ref[0, group * heads + half])
            for pair in range(1, pairs):
                sink = jnp.where(
                    pair_of >= pair * tokens, sink_ref[0, group * heads + 2 * pair + half], sink
                )
            block = scores[half * keys:(half + 1) * keys] * HEAD_DIM ** (-0.5) + bias
            peak = jnp.maximum(jnp.max(block, axis=0, keepdims=True), sink)
            numerator = jnp.exp(block - peak)
            denominator = jnp.exp(sink - peak) + jnp.sum(numerator, axis=0, keepdims=True)
            halves.append((numerator * (1.0 / denominator)).astype(jnp.bfloat16))
        mixed = jnp.dot(
            both_values, jnp.concatenate(halves, 0), preferred_element_type=jnp.float32
        ).T.astype(jnp.bfloat16)
        for pair in range(pairs):
            attended[:, first_lane + pair * lanes:first_lane + (pair + 1) * lanes] = mixed[
                pair * tokens:(pair + 1) * tokens
            ]


def tiles(total, step):
    return [(start, min(step, total - start)) for start in range(0, total, step)]


def expert_kernel(rows, cap, shifts, residual_ref, query_ref, key_ref, value_ref, segment_ref, sink_ref, gain_ref,
                  ids_ref, weight_ref, w_out_hbm, gate_up_hbm, down_hbm, out_ref,
                  w_out, key_all, value_all, segment_all, attended, partial_ref, meta_ref,
                  gate_up, down, gathered, metas, part_in, stream, packed, active, slot_weight, select,
                  slots, sib_slots, mix, ring_in, ring_out, over_in, keep, x_out, x_in,
                  o_sem, h_send, h_recv, w_sem, x_sem, c_send, c_recv, m_send, m_recv, n_send, n_recv, l_sem, send, recv,
                  over_send, over_recv, sib_send, sib_recv, slot_sem, f_send, f_recv, fo_send, fo_recv, fx_sem):
    chips = rows // 2
    half_way = chips // 2
    row = lax.axis_index("row")
    col = lax.axis_index("col")
    core = lax.rem(row, 2)
    place = ring_place(row, chips)
    other = row + 1 - 2 * core
    sibling = {"row": other}
    partner = {"col": 1 - col}
    ways = [{"row": ring_row(place + 1, chips, core)}, {"row": ring_row(place - 1, chips, core)}]
    tokens, features = residual_ref.shape
    size = tokens // PIECES
    out_tiles = tiles(features, OUT_TILE)
    out_loads = [
        pltpu.make_async_copy(w_out_hbm.at[pl.ds(start, width)], w_out.at[pl.ds(start, width)], o_sem.at[at])
        for at, (start, width) in enumerate(out_tiles)
    ]
    for load in out_loads:
        load.start()
    loads = [
        pltpu.make_async_copy(gate_up_hbm.at[0], gate_up, w_sem.at[0]),
        pltpu.make_async_copy(down_hbm.at[0], down, w_sem.at[1]),
    ]
    after = [{"row": lax.rem(row + shift, rows)} for shift in range(1, shifts + 1)]
    before = [{"row": lax.rem(row + rows - shift, rows)} for shift in range(1, shifts + 1)]
    greet(after + before + [sibling, partner] + ways)
    kv_width = key_all.shape[1]
    own_lanes = pl.ds(pl.multiple_of(col * kv_width, kv_width), kv_width)
    halos = []
    for at in range(shifts):
        there = pl.ds((shifts - 1 - at) * tokens, tokens)
        for which, (src, dst) in enumerate([
            (segment_ref, segment_all.at[at]),
            (key_ref.at[:, own_lanes], key_all.at[there]),
            (value_ref.at[:, own_lanes], value_all.at[there]),
        ]):
            halos.append(remote(src, dst, h_send.at[at, which], h_recv.at[at, which], after[at]))
            halos[-1].start()
    here = pl.ds(shifts * tokens, tokens)
    rest = key_all.shape[0] - (shifts + 1) * tokens
    for ref, every in [(key_ref, key_all), (value_ref, value_all)]:
        every[here, :] = ref[:, own_lanes]
        if rest:
            every[pl.ds((shifts + 1) * tokens, rest), :] = jnp.zeros((rest, kv_width), every.dtype)
    meta_ref[:TOP, :] = ids_ref[...].astype(jnp.float32)
    meta_ref[TOP:, :] = weight_ref[...]
    local_meta = pltpu.make_async_copy(meta_ref, metas.at[row], l_sem)
    local_meta.start()
    for halo in halos:
        halo.wait_recv()
    for load in loads:
        load.start()
    attend_all(row, shifts, query_ref, key_all, value_all, segment_ref, segment_all, sink_ref, attended)

    middle = pl.ds(size, 2 * size)
    early = []
    for at, (start, width) in enumerate(out_tiles):
        out_loads[at].wait()
        lanes = pl.ds(start, width)
        partial_ref[:, lanes] = lax.dot_general(
            attended[...], w_out[lanes, :], (((1,), (1,)), ((), ())), preferred_element_type=jnp.float32
        ).astype(jnp.bfloat16)
        early.append(remote(partial_ref.at[middle, lanes], part_in.at[middle, lanes], c_send.at[PIECES + at],
                            c_recv.at[PIECES + at], partner))
        early[-1].start()
    crosses = {}
    for index in [3, 0]:
        at = piece_rows(index, size)
        named = PIECES - 1 - index
        crosses[index] = remote(partial_ref.at[at], part_in.at[at], c_send.at[named],
                                c_recv.at[named], partner)
        crosses[index].start()
    for copy in early:
        copy.wait_recv()

    def ready(index):
        at = piece_rows(index, size)
        if index in (0, PIECES - 1):
            remote(partial_ref.at[at], part_in.at[at], c_send.at[index], c_recv.at[index],
                   partner).wait_recv()
        summed = partial_ref[at, :].astype(jnp.float32) + part_in[at, :].astype(jnp.float32)
        total = (residual_ref[at, :].astype(jnp.float32) + summed).astype(jnp.bfloat16)
        stream[at, :] = total
        gathered[row, at, :] = normalize(total, gain_ref[...])

    def part(offset, index, which):
        return gathered.at[ring_row(place + offset, chips, which), piece_rows(index, size)]

    def offset_of(way, distance):
        return -distance if way == 0 else distance

    def hop(way, distance, index, sending):
        at = part(offset_of(way, distance - 1 if sending else distance), index, core)
        return remote(at, at, send.at[way, distance - 1, index], recv.at[way, distance - 1, index],
                      ways[way])

    def over(way, distance, sending):
        at = part(offset_of(way, distance), 0 if sending else PIECES - 1, core)
        return remote(at, at, over_send.at[way, distance - 1], over_recv.at[way, distance - 1],
                      partner)

    def pass_on(way, distance, index, which):
        at = part(offset_of(way, distance), index, which)
        return remote(at, at, sib_send.at[way, distance, index], sib_recv.at[way, distance, index],
                      sibling)

    def routing_hop(way, distance, sending):
        back = offset_of(way, distance - 1 if sending else distance)
        at = metas.at[ring_row(place + back, chips, core)]
        return remote(at, at, m_send.at[way, distance - 1], m_recv.at[way, distance - 1], ways[way])

    def routing_on(way, distance, which):
        at = metas.at[ring_row(place + offset_of(way, distance), chips, which)]
        return remote(at, at, n_send.at[way, distance], n_recv.at[way, distance], sibling)

    sent = []

    def go(copy):
        copy.start()
        sent.append(copy)

    reach = [half_way, half_way - 1]
    theirs = gathered.at[other]

    def offsets(distances):
        found = []
        for distance in reversed(distances):
            found += sorted({distance, (chips - distance) % chips})
        return found

    def blocks_of(distances):
        return [(offset, which) for which in range(2) for offset in offsets(distances)]

    def wait_for(distances):
        for distance in distances:
            if distance == 0:
                remote(theirs, theirs, x_sem.at[0], x_sem.at[1], sibling).wait_recv()
                routing_on(0, 0, 1 - core).wait_recv()
                continue
            for way in range(2):
                if distance <= reach[way]:
                    routing_on(way, distance, 1 - core).wait_recv()
                indices = list(ring_pieces(distance, half_way, way))
                for index in indices + ([PIECES - 1] if 0 in indices else []):
                    pass_on(way, distance, index, 1 - core).wait_recv()

    def pack(distances):
        blocks = blocks_of(distances)
        not_after = lax.broadcasted_iota(jnp.int32, (tokens, tokens), 0) <= lax.broadcasted_iota(
            jnp.int32, (tokens, tokens), 1
        )
        not_after = jnp.where(not_after, 1.0, 0.0).astype(jnp.bfloat16)
        numbers = lax.broadcasted_iota(jnp.int32, (cap, tokens), 0).astype(jnp.float32)
        named, weights = [], []
        wanted = [(offset, which, row) for offset, which in blocks]
        wanted += [(offset, 0, other) for offset, which in blocks if which == 0]
        for offset, which, expert in wanted:
            meta = metas[ring_row(place + offset, chips, core if which == 0 else 1 - core)]
            hit = jnp.where(meta[:TOP] == expert.astype(jnp.float32), 1.0, 0.0)
            named.append(jnp.max(hit, axis=0, keepdims=True))
            weights.append(jnp.sum(hit * meta[TOP:], axis=0, keepdims=True))
        hits = jnp.concatenate(named, 0)
        order = jnp.dot(hits.astype(jnp.bfloat16), not_after, preferred_element_type=jnp.float32)
        chosen = [
            jnp.where(order[at:at + 1] == numbers + 1.0, 1.0, 0.0) * named[at]
            for at in range(len(wanted))
        ]
        for at, (offset, which) in enumerate(blocks):
            here = pl.ds(at * cap, cap)
            weight = jnp.sum(chosen[at] * weights[at], axis=1, keepdims=True)
            slot_weight[here, :] = jnp.broadcast_to(weight, (cap, slot_weight.shape[1]))
            source = ring_row(place + offset, chips, core if which == 0 else 1 - core)
            packed[here, :] = jnp.dot(
                chosen[at].astype(jnp.bfloat16), gathered[source],
                preferred_element_type=jnp.float32,
            ).astype(jnp.bfloat16)
        for at, (offset, which) in enumerate(blocks[:len(blocks) // 2]):
            both = jnp.concatenate([chosen[at], chosen[len(blocks) + at]], 0)
            select[offset] = both.T.astype(jnp.bfloat16)

    def gate_and_up(distances, start, width):
        count = cap * len(blocks_of(distances))
        values = packed[:count, :]
        lanes = pl.ds(start, width)
        last = (((1,), (1,)), ((), ()))
        gate = lax.dot_general(values, gate_up[0, lanes, :], last, preferred_element_type=jnp.float32)
        up = lax.dot_general(values, gate_up[1, lanes, :], last, preferred_element_type=jnp.float32)
        active[:count, lanes] = ((up + 1.0) * gate * jax.nn.sigmoid(1.702 * gate)).astype(jnp.bfloat16)

    def go_down(distances, start, width):
        blocks = blocks_of(distances)
        count = cap * len(blocks)
        lanes = pl.ds(start, width)
        result = jnp.dot(active[:count, :], down[:, lanes], preferred_element_type=jnp.float32)
        result = (result * slot_weight[:count, :1]).astype(jnp.bfloat16)
        for at, (offset, which) in enumerate(blocks):
            piece = result[at * cap:(at + 1) * cap]
            if which == 0:
                slots[offset, :cap, lanes] = piece
            else:
                sib_slots[offset, :, lanes] = piece

    def slot_copy(offset):
        return remote(sib_slots.at[offset], slots.at[offset, pl.ds(cap, cap)], slot_sem.at[0, offset],
                      slot_sem.at[1, offset], sibling)

    queue = []

    def work(budget):
        while queue and budget > 0:
            cost, step = queue.pop(0)
            step()
            budget -= cost

    def enqueue(distances, first):
        queue.append((0.3, lambda: wait_for(distances)))
        queue.append((0.8, lambda: pack(distances)))
        if first:
            queue.append((0.0, lambda: loads[0].wait()))
        for start, width in tiles(gate_up.shape[1], 256):
            queue.append((1.0, lambda start=start, width=width: gate_and_up(distances, start, width)))
        if first:
            queue.append((0.0, lambda: loads[1].wait()))
        for start, width in tiles(down.shape[1], 512):
            queue.append((0.4, lambda start=start, width=width: go_down(distances, start, width)))
        queue.append((0.2, lambda: [go(slot_copy(offset)) for offset in offsets(distances)]))

    near, mid = half_way // 4, half_way // 2
    batches = [range(near + 1), range(near + 1, mid + 1), range(mid + 1, half_way + 1)]
    for index in [1, 2, 0]:
        ready(index)
        for way in range(2):
            if index in ring_pieces(1, half_way, way):
                go(hop(way, 1, index, True))
    ready(PIECES - 1)
    local_meta.wait()
    for way in range(2):
        go(routing_hop(way, 1, True))
    go(routing_on(0, 0, core))
    mine = gathered.at[row]
    go(remote(mine, mine, x_sem.at[0], x_sem.at[1], sibling))

    def take_over(distance):
        for way in range(2):
            if distance > 0 and 0 in ring_pieces(distance, half_way, way):
                over(way, distance, False).wait_recv()
                go(pass_on(way, distance, PIECES - 1, core))

    for distance in range(1, half_way + 1):
        for index in [1, 2, 0]:
            for way in range(2):
                if index not in ring_pieces(distance, half_way, way):
                    continue
                hop(way, distance, index, False).wait_recv()
                if distance < half_way and index in ring_pieces(distance + 1, half_way, way):
                    go(hop(way, distance + 1, index, True))
                if index == 0:
                    go(over(way, distance, True))
                go(pass_on(way, distance, index, core))
            if index == 2:
                take_over(distance - 1)
                if distance == near + 1:
                    enqueue(batches[0], True)
                if distance == mid + 1:
                    enqueue(batches[1], False)
            work(BUDGET)
        for way in range(2):
            if distance <= reach[way]:
                routing_hop(way, distance, False).wait_recv()
                if distance < reach[way]:
                    go(routing_hop(way, distance + 1, True))
                go(routing_on(way, distance, core))
    work(BUDGET)
    take_over(half_way)
    work(100)
    enqueue(batches[2], False)
    work(100)

    def combine(offset):
        slot_copy(offset).wait_recv()
        mix[offset] = jnp.dot(
            select[offset], slots[offset], preferred_element_type=jnp.float32
        ).astype(jnp.bfloat16)

    def fold_hop(way, distance, index):
        at = pl.ds(index * size, size)
        return remote(ring_out.at[way, distance - 1, at], ring_in.at[way, distance - 1, at],
                      f_send.at[way, distance - 1, index], f_recv.at[way, distance - 1, index],
                      ways[way])

    def arrived(way, distance, index):
        fold_hop(way, distance, index).wait_recv()
        return ring_in[way, distance - 1, pl.ds(index * size, size), :].astype(jnp.float32)

    def fold_over(offset):
        return remote(mix.at[offset, piece_rows(PIECES - 1, size)], over_in.at[offset],
                      fo_send.at[offset], fo_recv.at[offset], partner)

    for distance in range(half_way, 0, -1):
        for offset in offsets([distance]):
            combine(offset)
            go(fold_over(offset))
        for index in [1, 2, 0]:
            for way in range(2):
                if index not in ring_pieces(distance, half_way, way):
                    continue
                offset = distance if way == 0 else chips - distance
                value = mix[offset, piece_rows(index, size), :].astype(jnp.float32)
                if index == 0:
                    fold_over(offset).wait_recv()
                    value = value + over_in[offset].astype(jnp.float32)
                if distance < half_way and index in ring_pieces(distance + 1, half_way, way):
                    value = value + arrived(way, distance + 1, index)
                ring_out[way, distance - 1, pl.ds(index * size, size), :] = value.astype(
                    jnp.bfloat16
                )
                go(fold_hop(way, distance, index))
    combine(0)
    width = out_ref.shape[1]
    for index in [3, 1, 2, 0]:
        at = piece_rows(index, size)
        value = mix[0, at, :].astype(jnp.float32)
        for way in range(2):
            if index in ring_pieces(1, half_way, way):
                value = value + arrived(way, 1, index)
        low, high = value[:, :width], value[:, width:]
        x_out[at, :] = jnp.where(col == 0, high, low).astype(jnp.bfloat16)
        go(remote(x_out.at[at], x_in.at[at], fx_sem.at[0, index], fx_sem.at[1, index], partner))
        base = stream[at, :].astype(jnp.float32)
        keep[at, :] = jnp.where(col == 0, low, high) + jnp.where(
            col == 0, base[:, :width], base[:, width:]
        )
    for index in [0, 2, 1, 3]:
        at = piece_rows(index, size)
        named = PIECES - 1 - index
        remote(x_out.at[at], x_in.at[at], fx_sem.at[0, named], fx_sem.at[1, named],
               partner).wait_recv()
        out_ref[at, :] = keep[at, :] + x_in[at, :].astype(jnp.float32)
    for copy in early + halos + list(crosses.values()) + sent:
        copy.wait_send()


def layer(residual, queries, keys, values, segments, sinks, w_out, gain, expert_ids, route_weight, w_gate_up,
          w_down, rows, cap, shifts, kv_width, width):
    w_gate_up = jnp.swapaxes(w_gate_up, 2, 3)
    w_out = w_out.T
    half_way = rows // 4
    chips = rows // 2
    tokens, features = residual.shape
    hidden = w_gate_up.shape[2]
    near, mid = half_way // 4, half_way // 2
    most = cap * 2 * max(2 * near + 1, 2 * (mid - near), 2 * (half_way - mid) - 1)
    key_rows = -(-(shifts + 1) * tokens // 128) * 128
    out_tiles = len(tiles(features, OUT_TILE))
    meta = (2 * TOP, tokens)
    bf16, f32, dma = jnp.bfloat16, jnp.float32, pltpu.SemaphoreType.DMA
    hbm = pl.BlockSpec(memory_space=pl.ANY)
    return pl.pallas_call(
        lambda *refs: expert_kernel(rows, cap, shifts, *refs),
        out_shape=jax.ShapeDtypeStruct((tokens, width), f32),
        in_specs=[VMEM] * 5 + [pl.BlockSpec(memory_space=pltpu.SMEM)] + [VMEM] * 3 + [hbm] * 3,
        out_specs=VMEM,
        scratch_shapes=[
            pltpu.VMEM(w_out.shape, bf16),
            pltpu.VMEM((key_rows, kv_width), bf16),
            pltpu.VMEM((key_rows, kv_width), bf16),
            pltpu.VMEM((shifts, 1, tokens), jnp.int32),
            pltpu.VMEM(queries.shape, bf16),
            pltpu.VMEM((tokens, features), bf16),
            pltpu.VMEM(meta, f32),
            pltpu.VMEM(w_gate_up.shape[1:], bf16),
            pltpu.VMEM(w_down.shape[1:], bf16),
            pltpu.VMEM((rows, tokens, features), bf16),
            pltpu.VMEM((rows, *meta), f32),
            pltpu.VMEM((tokens, features), bf16),
            pltpu.VMEM((tokens, features), bf16),
            pltpu.VMEM((most, features), bf16),
            pltpu.VMEM((most, hidden), bf16),
            pltpu.VMEM((most, 128), f32),
            pltpu.VMEM((chips, tokens, 2 * cap), bf16),
            pltpu.VMEM((chips, 2 * cap, features), bf16),
            pltpu.VMEM((chips, cap, features), bf16),
            pltpu.VMEM((chips, tokens, features), bf16),
            pltpu.VMEM((2, half_way, tokens // PIECES * (PIECES - 1), features), bf16),
            pltpu.VMEM((2, half_way, tokens // PIECES * (PIECES - 1), features), bf16),
            pltpu.VMEM((chips, tokens // PIECES, features), bf16),
            pltpu.VMEM((tokens, width), f32),
            pltpu.VMEM((tokens, width), bf16),
            pltpu.VMEM((tokens, width), bf16),
            dma((out_tiles,)),
            dma((shifts, 3)),
            dma((shifts, 3)),
            dma((2,)),
            dma((2,)),
            dma((PIECES + out_tiles,)),
            dma((PIECES + out_tiles,)),
            dma((2, half_way)),
            dma((2, half_way)),
            dma((2, half_way + 1)),
            dma((2, half_way + 1)),
            dma,
            dma((2, half_way, PIECES)),
            dma((2, half_way, PIECES)),
            dma((2, half_way)),
            dma((2, half_way)),
            dma((2, half_way + 1, PIECES)),
            dma((2, half_way + 1, PIECES)),
            dma((2, chips)),
            dma((2, half_way, PIECES)),
            dma((2, half_way, PIECES)),
            dma((chips,)),
            dma((chips,)),
            dma((2, PIECES)),
        ],
        compiler_params=pltpu.CompilerParams(
            collective_id=2, has_side_effects=True, vmem_limit_bytes=VMEM_BYTES
        ),
        name="layer",
    )(residual, queries, keys, values, segments.reshape(1, -1), sinks.reshape(1, -1), gain.reshape(1, -1),
      expert_ids.T, route_weight.T, w_out, w_gate_up, w_down).astype(bf16)


def local(
    residual,
    query_states,
    key_states,
    value_states,
    segment_ids,
    sink_logits,
    w_out,
    norm_gain,
    expert_ids,
    route_weight,
    w_gate_up,
    w_down,
):
    tok_rows = query_states.shape[0]
    row_count = lax.axis_size("row")
    col_count = lax.axis_size("col")
    row_index = lax.axis_index("row")
    col_index = lax.axis_index("col")
    local_heads = sink_logits.shape[0]
    group_size = HEADS // KV_HEADS
    if local_heads >= group_size:
        kv_count = local_heads // group_size
        kv_first = col_index * kv_count
    else:
        kv_count = 1
        kv_first = col_index * local_heads // group_size
    kv_width = kv_count * HEAD_DIM
    own_keys = lax.dynamic_slice_in_dim(key_states, kv_first * HEAD_DIM, kv_width, 1)
    own_values = lax.dynamic_slice_in_dim(value_states, kv_first * HEAD_DIM, kv_width, 1)
    shift_count = (WINDOW + tok_rows - 2) // tok_rows
    block_bytes = 2 * residual.shape[0] * residual.shape[1]
    experts_all = w_gate_up.shape[0] * row_count
    slot_cap = max(2, 2 * TOP * tok_rows // experts_all)
    weight_bytes = 2 * (w_out.size + w_gate_up.size + w_down.size)
    in_kernels = (
        col_count == 2 and row_count % 4 == 0 and row_count >= 8 and tok_rows % 64 == 0
        and kv_width % 128 == 0 and kv_width * col_count == key_states.shape[1]
        and slot_cap % 16 == 0 and 2 * slot_cap == tok_rows and 2 * HEAD_DIM == 128
        and local_heads % (2 * kv_count) == 0 and weight_bytes + 3 * row_count * block_bytes < VMEM_BYTES
    )
    feature_count = residual.shape[1] // col_count
    if in_kernels:
        return layer(
            residual, query_states, key_states, value_states, segment_ids, sink_logits, w_out, norm_gain,
            expert_ids, route_weight, w_gate_up, w_down, row_count, slot_cap, shift_count, kv_width,
            feature_count,
        )
    routing = jnp.concatenate([expert_ids.astype(jnp.float32), route_weight], 1).T
    key_parts = []
    value_parts = []
    segment_parts = []
    start_parts = []
    for offset in range(shift_count, 0, -1):
        arrived = shifted((own_keys, own_values, segment_ids), "row", offset)
        key_parts.append(arrived[0])
        value_parts.append(arrived[1])
        segment_parts.append(arrived[2])
        start_parts.append((row_index - offset) * tok_rows)
    key_parts.append(own_keys)
    value_parts.append(own_values)
    segment_parts.append(segment_ids)
    start_parts.append(row_index * tok_rows)
    key_groups = jnp.concatenate(key_parts, 0).reshape(-1, kv_count, HEAD_DIM)
    value_groups = jnp.concatenate(value_parts, 0).reshape(-1, kv_count, HEAD_DIM)
    key_segments = jnp.concatenate(segment_parts, 0)
    positions = jnp.arange(tok_rows, dtype=jnp.int32)
    key_position = jnp.concatenate([start + positions for start in start_parts], 0)
    query_position = row_index * tok_rows + positions
    allowed = (key_position[None, :] >= 0) & (key_position[None, :] <= query_position[:, None])
    allowed = allowed & (key_position[None, :] > query_position[:, None] - WINDOW)
    allowed = allowed & (key_segments[None, :] == segment_ids[:, None])
    query_groups = query_states.reshape(tok_rows, kv_count, local_heads // kv_count, HEAD_DIM)
    sink_groups = sink_logits.reshape(kv_count, local_heads // kv_count, 1, 1)
    attended = attend(query_groups, key_groups, value_groups, allowed, sink_groups).reshape(
        tok_rows, local_heads * HEAD_DIM
    )
    partial_value = jnp.dot(attended, w_out, preferred_element_type=jnp.float32)
    expert_gate_up = w_gate_up[0]
    expert_down = w_down[0]
    partial_value = partial_value.astype(jnp.bfloat16)
    summed = lax.psum(partial_value, "col").astype(jnp.float32)
    stream = (residual.astype(jnp.float32) + summed).astype(jnp.bfloat16)
    gathered = lax.all_gather(normalize(stream, norm_gain), "row", axis=0, tiled=False)
    routing = lax.all_gather(routing, "row", axis=0, tiled=False)
    stream_part = lax.dynamic_slice_in_dim(stream, col_index * feature_count, feature_count, 1)
    names_mine = routing[:, :TOP] == row_index.astype(jnp.float32)
    mine = jnp.any(names_mine, axis=1)
    weight = jnp.sum(jnp.where(names_mine, routing[:, TOP:], 0.0), axis=1)
    token_order = jnp.arange(tok_rows, dtype=jnp.int32)
    not_after = (token_order[:, None] <= token_order[None, :]).astype(jnp.bfloat16)
    slot_of = jnp.dot(
        mine.astype(jnp.bfloat16), not_after, preferred_element_type=jnp.float32
    ).astype(jnp.int32) - 1
    slots = jnp.arange(slot_cap, dtype=jnp.int32)
    chosen = mine[:, None, :] & (slot_of[:, None, :] == slots[None, :, None])
    selector = chosen.astype(jnp.bfloat16)
    combine = jnp.where(chosen, weight[:, None, :], 0.0)
    packed = jnp.einsum(
        "nst,ntd->nsd", selector, gathered, preferred_element_type=jnp.float32
    ).astype(jnp.bfloat16).reshape(row_count * slot_cap, -1)
    gate = jnp.dot(packed, expert_gate_up[0], preferred_element_type=jnp.float32)
    up = jnp.dot(packed, expert_gate_up[1], preferred_element_type=jnp.float32)
    active = ((up + 1.0) * gate * jax.nn.sigmoid(1.702 * gate)).astype(jnp.bfloat16)
    expert_partial = jnp.dot(active, expert_down, preferred_element_type=jnp.float32)
    scaled = expert_partial.reshape(row_count, slot_cap, -1) * jnp.sum(combine, 2)[:, :, None]
    mixed = jnp.einsum(
        "nst,nsd->ntd", selector, scaled.astype(jnp.bfloat16), preferred_element_type=jnp.float32
    ).astype(jnp.bfloat16)
    mixed = mixed.reshape(row_count * tok_rows, -1)
    mixed = lax.psum_scatter(mixed, "row", scatter_dimension=0, tiled=True)
    mixed = lax.psum_scatter(mixed, "col", scatter_dimension=1, tiled=True)
    return (stream_part.astype(jnp.float32) + mixed.astype(jnp.float32)).astype(jnp.bfloat16)


def solution(mesh):
    in_specs = (
        P("row", None),
        P("row", "col"),
        P("row", None),
        P("row", None),
        P("row"),
        P("col"),
        P("col", None),
        P(),
        P("row", None),
        P("row", None),
        P("row", None, None, "col"),
        P("row", "col", None),
    )
    out_specs = P("row", "col")
    return jax.shard_map(local, mesh=mesh, in_specs=in_specs, out_specs=out_specs, check_vma=False)
```

```python
import jax
import jax.numpy as jnp
from jax import lax
from jax.experimental import pallas as pl
from jax.experimental.pallas import tpu as pltpu
from jax.sharding import PartitionSpec as P

HEADS = 64
KV_HEADS = 8
HEAD_DIM = 64
WINDOW = 128
TOP = 4


epsilon = 1e-05
masked_score = -1e30


def shifted(shard, axis, by):
    size = lax.axis_size(axis)
    pairs = [(i, i + by) for i in range(size) if 0 <= i + by < size]
    return lax.ppermute(shard, axis, pairs)


def normalize(stream_rows, norm_gain):
    values32 = stream_rows.astype(jnp.float32)
    square_mean = jnp.mean(values32 * values32, axis=-1, keepdims=True)
    return (values32 * lax.rsqrt(square_mean + epsilon) * norm_gain).astype(jnp.bfloat16)


def attend(query_groups, key_groups, value_groups, allowed, sink_groups):
    scores = jnp.einsum(
        "tgjd,lgd->gjtl", query_groups, key_groups, preferred_element_type=jnp.float32
    )
    scores = scores * query_groups.shape[-1] ** (-0.5)
    scores = jnp.where(allowed[None, None], scores, masked_score)
    peak_score = jnp.maximum(jnp.max(scores, axis=-1, keepdims=True), sink_groups)
    numerator = jnp.exp(scores - peak_score)
    denominator = jnp.exp(sink_groups - peak_score) + jnp.sum(numerator, axis=-1, keepdims=True)
    weights = (numerator / denominator).astype(jnp.bfloat16)
    return jnp.einsum(
        "gjtl,lgd->tgjd", weights, value_groups, preferred_element_type=jnp.float32
    ).astype(jnp.bfloat16)


MESH = pl.DeviceIdType.MESH
VMEM = pl.BlockSpec(memory_space=pltpu.VMEM)
PIECES = 4
VMEM_BYTES = 61 * 1024 * 1024


def ring_place(row, chips):
    chip = lax.div(row, 2)
    along = lax.div(chip, 2)
    return jnp.where(lax.rem(chip, 2) == 0, along, chips - 1 - along)


def ring_row(place, chips, core):
    place = lax.rem(place + chips, chips)
    chip = jnp.where(place < chips // 2, 2 * place, 2 * (chips - 1 - place) + 1)
    return 2 * chip + core


def greet(devices):
    barrier = pltpu.get_barrier_semaphore()
    for device in devices:
        pl.semaphore_signal(barrier, inc=1, device_id=device, device_id_type=MESH)
    pl.semaphore_wait(barrier, len(devices))


def remote(src, dst, send, recv, device):
    return pltpu.make_async_remote_copy(
        src_ref=src, dst_ref=dst, send_sem=send, recv_sem=recv, device_id=device,
        device_id_type=MESH,
    )


def ring_pieces(distance, half_way, way):
    if distance < half_way:
        return [0, 1, 2]
    return [0, 1] if way == 0 else [2, 3]


def piece_rows(index, size):
    col = lax.axis_index("col")
    start = (index + col * (PIECES - 1 - 2 * index)) * size
    return pl.ds(pl.multiple_of(start, size), size)


OUT_TILE = 512
BUDGET = 2.0


def attend_all(row, shifts, query_ref, key_all, value_all, segment_ref, segment_all, sink_ref, attended):
    tokens = query_ref.shape[0]
    keys = key_all.shape[0]
    groups = key_all.shape[1] // HEAD_DIM
    heads = sink_ref.shape[1] // groups
    pairs = heads // 2
    lanes = 2 * HEAD_DIM
    segments = [segment_all[at] for at in range(shifts - 1, -1, -1)] + [segment_ref[...]]
    rest = keys - (shifts + 1) * tokens
    if rest:
        segments.append(jnp.full((1, rest), -1, jnp.int32))
    key_segment = jnp.concatenate(segments, 1).astype(jnp.float32)
    diagonal = lax.broadcasted_iota(jnp.int32, (tokens, tokens), 0) == lax.broadcasted_iota(
        jnp.int32, (tokens, tokens), 1
    )
    query_segment = jnp.sum(
        jnp.where(diagonal, segment_ref[...].astype(jnp.float32), 0.0), axis=1, keepdims=True
    )
    query_at = shifts * tokens + lax.broadcasted_iota(jnp.int32, (tokens, keys), 0)
    key_at = lax.broadcasted_iota(jnp.int32, (tokens, keys), 1)
    allowed = (key_at <= query_at) & (key_at > query_at - WINDOW) & (key_at + row * tokens >= shifts * tokens)
    allowed = allowed & (key_segment == query_segment)
    bias = jnp.where(allowed, 0.0, masked_score)
    bias = jnp.concatenate([bias] * pairs, 0).T
    values_turned = value_all[...].astype(jnp.float32).T.astype(jnp.bfloat16)
    lower = lax.broadcasted_iota(jnp.int32, (keys, lanes), 1) < HEAD_DIM
    pair_of = lax.broadcasted_iota(jnp.int32, (1, pairs * tokens), 1)
    nothing = jnp.zeros((HEAD_DIM, keys), jnp.bfloat16)
    for group in range(groups):
        tile = group // 2 * lanes
        straight = key_all[:, tile:tile + lanes]
        turned = jnp.concatenate([straight[:, HEAD_DIM:], straight[:, :HEAD_DIM]], 1)
        first, second = (straight, turned) if group % 2 == 0 else (turned, straight)
        zero = jnp.zeros_like(straight)
        both_keys = jnp.concatenate([jnp.where(lower, first, zero), jnp.where(lower, zero, second)], 0)
        value = values_turned[group * HEAD_DIM:(group + 1) * HEAD_DIM]
        both_values = jnp.concatenate(
            [jnp.concatenate([value, nothing], 1), jnp.concatenate([nothing, value], 1)], 0
        )
        first_lane = group * heads * HEAD_DIM
        queries = jnp.concatenate(
            [query_ref[:, first_lane + pair * lanes:first_lane + (pair + 1) * lanes] for pair in range(pairs)], 0
        )
        scores = lax.dot_general(
            both_keys, queries, (((1,), (1,)), ((), ())), preferred_element_type=jnp.float32
        )
        halves = []
        for half in range(2):
            sink = jnp.full(pair_of.shape, sink_ref[0, group * heads + half])
            for pair in range(1, pairs):
                sink = jnp.where(
                    pair_of >= pair * tokens, sink_ref[0, group * heads + 2 * pair + half], sink
                )
            block = scores[half * keys:(half + 1) * keys] * HEAD_DIM ** (-0.5) + bias
            peak = jnp.maximum(jnp.max(block, axis=0, keepdims=True), sink)
            numerator = jnp.exp(block - peak)
            denominator = jnp.exp(sink - peak) + jnp.sum(numerator, axis=0, keepdims=True)
            halves.append((numerator * (1.0 / denominator)).astype(jnp.bfloat16))
        mixed = jnp.dot(
            both_values, jnp.concatenate(halves, 0), preferred_element_type=jnp.float32
        ).T.astype(jnp.bfloat16)
        for pair in range(pairs):
            attended[:, first_lane + pair * lanes:first_lane + (pair + 1) * lanes] = mixed[
                pair * tokens:(pair + 1) * tokens
            ]


def tiles(total, step):
    return [(start, min(step, total - start)) for start in range(0, total, step)]


def expert_kernel(rows, cap, shifts, residual_ref, query_ref, key_ref, value_ref, segment_ref, sink_ref, gain_ref,
                  ids_ref, weight_ref, w_out_hbm, gate_up_hbm, down_hbm, out_ref,
                  w_out, key_all, value_all, segment_all, attended, partial_ref, meta_ref,
                  gate_up, down, gathered, metas, part_in, stream, packed, active, slot_weight, select,
                  slots, sib_slots, mix, ring_in, ring_out, over_in, keep, x_out, x_in,
                  o_sem, h_send, h_recv, w_sem, x_sem, c_send, c_recv, m_send, m_recv, n_send, n_recv, l_sem, send, recv,
                  over_send, over_recv, sib_send, sib_recv, slot_sem, f_send, f_recv, fo_send, fo_recv, fx_sem):
    chips = rows // 2
    half_way = chips // 2
    row = lax.axis_index("row")
    col = lax.axis_index("col")
    core = lax.rem(row, 2)
    place = ring_place(row, chips)
    other = row + 1 - 2 * core
    sibling = {"row": other}
    partner = {"col": 1 - col}
    ways = [{"row": ring_row(place + 1, chips, core)}, {"row": ring_row(place - 1, chips, core)}]
    tokens, features = residual_ref.shape
    size = tokens // PIECES
    out_tiles = tiles(features, OUT_TILE)
    out_loads = [
        pltpu.make_async_copy(w_out_hbm.at[pl.ds(start, width)], w_out.at[pl.ds(start, width)], o_sem.at[at])
        for at, (start, width) in enumerate(out_tiles)
    ]
    for load in out_loads:
        load.start()
    loads = [
        pltpu.make_async_copy(gate_up_hbm.at[0], gate_up, w_sem.at[0]),
        pltpu.make_async_copy(down_hbm.at[0], down, w_sem.at[1]),
    ]
    after = [{"row": lax.rem(row + shift, rows)} for shift in range(1, shifts + 1)]
    before = [{"row": lax.rem(row + rows - shift, rows)} for shift in range(1, shifts + 1)]
    greet(after + before + [sibling, partner] + ways)
    kv_width = key_all.shape[1]
    own_lanes = pl.ds(pl.multiple_of(col * kv_width, kv_width), kv_width)
    halos = []
    for at in range(shifts):
        there = pl.ds((shifts - 1 - at) * tokens, tokens)
        for which, (src, dst) in enumerate([
            (segment_ref, segment_all.at[at]),
            (key_ref.at[:, own_lanes], key_all.at[there]),
            (value_ref.at[:, own_lanes], value_all.at[there]),
        ]):
            halos.append(remote(src, dst, h_send.at[at, which], h_recv.at[at, which], after[at]))
            halos[-1].start()
    here = pl.ds(shifts * tokens, tokens)
    rest = key_all.shape[0] - (shifts + 1) * tokens
    for ref, every in [(key_ref, key_all), (value_ref, value_all)]:
        every[here, :] = ref[:, own_lanes]
        if rest:
            every[pl.ds((shifts + 1) * tokens, rest), :] = jnp.zeros((rest, kv_width), every.dtype)
    meta_ref[:TOP, :] = ids_ref[...].astype(jnp.float32)
    meta_ref[TOP:, :] = weight_ref[...]
    local_meta = pltpu.make_async_copy(meta_ref, metas.at[row], l_sem)
    local_meta.start()
    for halo in halos:
        halo.wait_recv()
    for load in loads:
        load.start()
    attend_all(row, shifts, query_ref, key_all, value_all, segment_ref, segment_all, sink_ref, attended)

    first_rows = pl.ds(pl.multiple_of((1 - col) * 2 * size, 2 * size), 2 * size)
    early = []
    for at, (start, width) in enumerate(out_tiles):
        out_loads[at].wait()
        lanes = pl.ds(start, width)
        partial_ref[:, lanes] = lax.dot_general(
            attended[...], w_out[lanes, :], (((1,), (1,)), ((), ())), preferred_element_type=jnp.float32
        ).astype(jnp.bfloat16)
        early.append(remote(partial_ref.at[first_rows, lanes], part_in.at[first_rows, lanes], c_send.at[PIECES + at],
                            c_recv.at[PIECES + at], partner))
        early[-1].start()
    crosses = {}
    for index in [1, 0]:
        at = piece_rows(index, size)
        named = PIECES - 1 - index
        crosses[index] = remote(partial_ref.at[at], part_in.at[at], c_send.at[named],
                                c_recv.at[named], partner)
        crosses[index].start()
    for copy in early:
        copy.wait_recv()

    def ready(index):
        at = piece_rows(index, size)
        if index >= 2:
            remote(partial_ref.at[at], part_in.at[at], c_send.at[index], c_recv.at[index],
                   partner).wait_recv()
        summed = partial_ref[at, :].astype(jnp.float32) + part_in[at, :].astype(jnp.float32)
        total = (residual_ref[at, :].astype(jnp.float32) + summed).astype(jnp.bfloat16)
        stream[at, :] = total
        gathered[row, at, :] = normalize(total, gain_ref[...])

    def part(offset, index, which):
        return gathered.at[ring_row(place + offset, chips, which), piece_rows(index, size)]

    def offset_of(way, distance):
        return -distance if way == 0 else distance

    def hop(way, distance, index, sending):
        at = part(offset_of(way, distance - 1 if sending else distance), index, core)
        return remote(at, at, send.at[way, distance - 1, index], recv.at[way, distance - 1, index],
                      ways[way])

    def over(way, distance, sending):
        at = part(offset_of(way, distance), 0 if sending else PIECES - 1, core)
        return remote(at, at, over_send.at[way, distance - 1], over_recv.at[way, distance - 1],
                      partner)

    def pass_on(way, distance, index, which):
        at = part(offset_of(way, distance), index, which)
        return remote(at, at, sib_send.at[way, distance, index], sib_recv.at[way, distance, index],
                      sibling)

    def routing_hop(way, distance, sending):
        back = offset_of(way, distance - 1 if sending else distance)
        at = metas.at[ring_row(place + back, chips, core)]
        return remote(at, at, m_send.at[way, distance - 1], m_recv.at[way, distance - 1], ways[way])

    def routing_on(way, distance, which):
        at = metas.at[ring_row(place + offset_of(way, distance), chips, which)]
        return remote(at, at, n_send.at[way, distance], n_recv.at[way, distance], sibling)

    sent = []

    def go(copy):
        copy.start()
        sent.append(copy)

    reach = [half_way, half_way - 1]
    theirs = gathered.at[other]

    def offsets(distances):
        found = []
        for distance in reversed(distances):
            found += sorted({distance, (chips - distance) % chips})
        return found

    def blocks_of(distances):
        return [(offset, which) for which in range(2) for offset in offsets(distances)]

    def wait_for(distances):
        for distance in distances:
            if distance == 0:
                remote(theirs, theirs, x_sem.at[0], x_sem.at[1], sibling).wait_recv()
                routing_on(0, 0, 1 - core).wait_recv()
                continue
            for way in range(2):
                if distance <= reach[way]:
                    routing_on(way, distance, 1 - core).wait_recv()
                indices = list(ring_pieces(distance, half_way, way))
                for index in indices + ([PIECES - 1] if distance < half_way else []):
                    pass_on(way, distance, index, 1 - core).wait_recv()

    def pack(distances):
        blocks = blocks_of(distances)
        not_after = lax.broadcasted_iota(jnp.int32, (tokens, tokens), 0) <= lax.broadcasted_iota(
            jnp.int32, (tokens, tokens), 1
        )
        not_after = jnp.where(not_after, 1.0, 0.0).astype(jnp.bfloat16)
        numbers = lax.broadcasted_iota(jnp.int32, (cap, tokens), 0).astype(jnp.float32)
        named, weights = [], []
        wanted = [(offset, which, row) for offset, which in blocks]
        wanted += [(offset, 0, other) for offset, which in blocks if which == 0]
        for offset, which, expert in wanted:
            meta = metas[ring_row(place + offset, chips, core if which == 0 else 1 - core)]
            hit = jnp.where(meta[:TOP] == expert.astype(jnp.float32), 1.0, 0.0)
            named.append(jnp.max(hit, axis=0, keepdims=True))
            weights.append(jnp.sum(hit * meta[TOP:], axis=0, keepdims=True))
        hits = jnp.concatenate(named, 0)
        order = jnp.dot(hits.astype(jnp.bfloat16), not_after, preferred_element_type=jnp.float32)
        chosen = [
            jnp.where(order[at:at + 1] == numbers + 1.0, 1.0, 0.0) * named[at]
            for at in range(len(wanted))
        ]
        for at, (offset, which) in enumerate(blocks):
            here = pl.ds(at * cap, cap)
            weight = jnp.sum(chosen[at] * weights[at], axis=1, keepdims=True)
            slot_weight[here, :] = jnp.broadcast_to(weight, (cap, slot_weight.shape[1]))
            source = ring_row(place + offset, chips, core if which == 0 else 1 - core)
            packed[here, :] = jnp.dot(
                chosen[at].astype(jnp.bfloat16), gathered[source],
                preferred_element_type=jnp.float32,
            ).astype(jnp.bfloat16)
        for at, (offset, which) in enumerate(blocks[:len(blocks) // 2]):
            both = jnp.concatenate([chosen[at], chosen[len(blocks) + at]], 0)
            select[offset] = both.T.astype(jnp.bfloat16)

    def gate_and_up(distances, start, width):
        count = cap * len(blocks_of(distances))
        values = packed[:count, :]
        lanes = pl.ds(start, width)
        last = (((1,), (1,)), ((), ()))
        gate = lax.dot_general(values, gate_up[0, lanes, :], last, preferred_element_type=jnp.float32)
        up = lax.dot_general(values, gate_up[1, lanes, :], last, preferred_element_type=jnp.float32)
        active[:count, lanes] = ((up + 1.0) * gate * jax.nn.sigmoid(1.702 * gate)).astype(jnp.bfloat16)

    def go_down(distances, start, width):
        blocks = blocks_of(distances)
        count = cap * len(blocks)
        lanes = pl.ds(start, width)
        result = jnp.dot(active[:count, :], down[:, lanes], preferred_element_type=jnp.float32)
        result = (result * slot_weight[:count, :1]).astype(jnp.bfloat16)
        for at, (offset, which) in enumerate(blocks):
            piece = result[at * cap:(at + 1) * cap]
            if which == 0:
                slots[offset, :cap, lanes] = piece
            else:
                sib_slots[offset, :, lanes] = piece

    def slot_copy(offset):
        return remote(sib_slots.at[offset], slots.at[offset, pl.ds(cap, cap)], slot_sem.at[0, offset],
                      slot_sem.at[1, offset], sibling)

    queue = []

    def work(budget):
        while queue and budget > 0:
            cost, step = queue.pop(0)
            step()
            budget -= cost

    def enqueue(distances, first):
        queue.append((0.3, lambda: wait_for(distances)))
        queue.append((0.8, lambda: pack(distances)))
        if first:
            queue.append((0.0, lambda: loads[0].wait()))
        for start, width in tiles(gate_up.shape[1], 256):
            queue.append((1.0, lambda start=start, width=width: gate_and_up(distances, start, width)))
        if first:
            queue.append((0.0, lambda: loads[1].wait()))
        for start, width in tiles(down.shape[1], 512):
            queue.append((0.4, lambda start=start, width=width: go_down(distances, start, width)))
        queue.append((0.2, lambda: [go(slot_copy(offset)) for offset in offsets(distances)]))

    near, mid = half_way // 4, half_way // 2
    batches = [range(near + 1), range(near + 1, mid + 1), range(mid + 1, half_way + 1)]
    for index in [0, 1, 2]:
        ready(index)
        for way in range(2):
            if index in ring_pieces(1, half_way, way):
                go(hop(way, 1, index, True))
    ready(PIECES - 1)
    local_meta.wait()
    for way in range(2):
        go(routing_hop(way, 1, True))
    go(routing_on(0, 0, core))
    mine = gathered.at[row]
    go(remote(mine, mine, x_sem.at[0], x_sem.at[1], sibling))

    def take_over(distance):
        for way in range(2):
            over(way, distance, False).wait_recv()
            if distance + 1 == half_way and way == 1:
                go(hop(way, half_way, PIECES - 1, True))
            go(pass_on(way, distance, PIECES - 1, core))

    for distance in range(1, half_way + 1):
        for step, index in enumerate([0, 1, 2] if distance < half_way else [0, 2, 1, 3]):
            for way in range(2):
                if index not in ring_pieces(distance, half_way, way):
                    continue
                hop(way, distance, index, False).wait_recv()
                if distance < half_way and index in ring_pieces(distance + 1, half_way, way):
                    go(hop(way, distance + 1, index, True))
                if index == 0 and distance < half_way:
                    go(over(way, distance, True))
                go(pass_on(way, distance, index, core))
            if step == 0:
                if distance == near + 1:
                    enqueue(batches[0], True)
                if distance == mid + 1:
                    work(100)
                    enqueue(batches[1], False)
            work(BUDGET)
        for way in range(2):
            if distance <= reach[way]:
                routing_hop(way, distance, False).wait_recv()
                if distance < reach[way]:
                    go(routing_hop(way, distance + 1, True))
                go(routing_on(way, distance, core))
        if distance < half_way:
            take_over(distance)
    work(100)
    enqueue(batches[2], False)
    work(100)

    def combine(offset):
        slot_copy(offset).wait_recv()
        mix[offset] = jnp.dot(
            select[offset], slots[offset], preferred_element_type=jnp.float32
        ).astype(jnp.bfloat16)

    def fold_hop(way, distance, index):
        at = pl.ds(index % (PIECES - 1) * size, size)
        return remote(ring_out.at[way, distance - 1, at], ring_in.at[way, distance - 1, at],
                      f_send.at[way, distance - 1, index], f_recv.at[way, distance - 1, index],
                      ways[way])

    def arrived(way, distance, index):
        fold_hop(way, distance, index).wait_recv()
        return ring_in[way, distance - 1, pl.ds(index % (PIECES - 1) * size, size), :].astype(jnp.float32)

    def fold_over(offset):
        return remote(mix.at[offset, piece_rows(PIECES - 1, size)], over_in.at[offset],
                      fo_send.at[offset], fo_recv.at[offset], partner)

    def fold_step(way, distance, index):
        offset = distance if way == 0 else chips - distance
        at = piece_rows(index, size)
        value = mix[offset, at, :].astype(jnp.float32)
        if distance < half_way and index in ring_pieces(distance + 1, half_way, way):
            value = value + arrived(way, distance + 1, index)
        if distance < half_way and index == PIECES - 1:
            mix[offset, at, :] = value.astype(jnp.bfloat16)
            go(fold_over(offset))
            return
        if index == 0 and distance < half_way:
            fold_over(offset).wait_recv()
            value = value + over_in[offset].astype(jnp.float32)
        ring_out[way, distance - 1, pl.ds(index % (PIECES - 1) * size, size), :] = value.astype(
            jnp.bfloat16
        )
        go(fold_hop(way, distance, index))

    for distance in range(half_way, 0, -1):
        for offset in offsets([distance]):
            combine(offset)
        if distance == half_way:
            steps = [(1, 3), (0, 1), (1, 2), (0, 0)]
        elif distance == half_way - 1:
            steps = [(0, 3), (0, 2), (1, 1), (1, 3), (0, 1), (1, 2), (0, 0), (1, 0)]
        else:
            steps = [(0, 3), (1, 3), (0, 1), (1, 1), (0, 2), (1, 2), (0, 0), (1, 0)]
        for way, index in steps:
            fold_step(way, distance, index)
    combine(0)
    width = out_ref.shape[1]
    for index in [3, 1, 2, 0]:
        at = piece_rows(index, size)
        value = mix[0, at, :].astype(jnp.float32)
        for way in range(2):
            if index in ring_pieces(1, half_way, way):
                value = value + arrived(way, 1, index)
        low, high = value[:, :width], value[:, width:]
        x_out[at, :] = jnp.where(col == 0, high, low).astype(jnp.bfloat16)
        go(remote(x_out.at[at], x_in.at[at], fx_sem.at[0, index], fx_sem.at[1, index], partner))
        base = stream[at, :].astype(jnp.float32)
        keep[at, :] = jnp.where(col == 0, low, high) + jnp.where(
            col == 0, base[:, :width], base[:, width:]
        )
    for index in [0, 2, 1, 3]:
        at = piece_rows(index, size)
        named = PIECES - 1 - index
        remote(x_out.at[at], x_in.at[at], fx_sem.at[0, named], fx_sem.at[1, named],
               partner).wait_recv()
        out_ref[at, :] = keep[at, :] + x_in[at, :].astype(jnp.float32)
    for copy in early + halos + list(crosses.values()) + sent:
        copy.wait_send()


def layer(residual, queries, keys, values, segments, sinks, w_out, gain, expert_ids, route_weight, w_gate_up,
          w_down, rows, cap, shifts, kv_width, width):
    w_gate_up = jnp.swapaxes(w_gate_up, 2, 3)
    w_out = w_out.T
    half_way = rows // 4
    chips = rows // 2
    tokens, features = residual.shape
    hidden = w_gate_up.shape[2]
    near, mid = half_way // 4, half_way // 2
    most = cap * 2 * max(2 * near + 1, 2 * (mid - near), 2 * (half_way - mid) - 1)
    key_rows = -(-(shifts + 1) * tokens // 128) * 128
    out_tiles = len(tiles(features, OUT_TILE))
    meta = (2 * TOP, tokens)
    bf16, f32, dma = jnp.bfloat16, jnp.float32, pltpu.SemaphoreType.DMA
    hbm = pl.BlockSpec(memory_space=pl.ANY)
    return pl.pallas_call(
        lambda *refs: expert_kernel(rows, cap, shifts, *refs),
        out_shape=jax.ShapeDtypeStruct((tokens, width), f32),
        in_specs=[VMEM] * 5 + [pl.BlockSpec(memory_space=pltpu.SMEM)] + [VMEM] * 3 + [hbm] * 3,
        out_specs=VMEM,
        scratch_shapes=[
            pltpu.VMEM(w_out.shape, bf16),
            pltpu.VMEM((key_rows, kv_width), bf16),
            pltpu.VMEM((key_rows, kv_width), bf16),
            pltpu.VMEM((shifts, 1, tokens), jnp.int32),
            pltpu.VMEM(queries.shape, bf16),
            pltpu.VMEM((tokens, features), bf16),
            pltpu.VMEM(meta, f32),
            pltpu.VMEM(w_gate_up.shape[1:], bf16),
            pltpu.VMEM(w_down.shape[1:], bf16),
            pltpu.VMEM((rows, tokens, features), bf16),
            pltpu.VMEM((rows, *meta), f32),
            pltpu.VMEM((tokens, features), bf16),
            pltpu.VMEM((tokens, features), bf16),
            pltpu.VMEM((most, features), bf16),
            pltpu.VMEM((most, hidden), bf16),
            pltpu.VMEM((most, 128), f32),
            pltpu.VMEM((chips, tokens, 2 * cap), bf16),
            pltpu.VMEM((chips, 2 * cap, features), bf16),
            pltpu.VMEM((chips, cap, features), bf16),
            pltpu.VMEM((chips, tokens, features), bf16),
            pltpu.VMEM((2, half_way, tokens // PIECES * (PIECES - 1), features), bf16),
            pltpu.VMEM((2, half_way, tokens // PIECES * (PIECES - 1), features), bf16),
            pltpu.VMEM((chips, tokens // PIECES, features), bf16),
            pltpu.VMEM((tokens, width), f32),
            pltpu.VMEM((tokens, width), bf16),
            pltpu.VMEM((tokens, width), bf16),
            dma((out_tiles,)),
            dma((shifts, 3)),
            dma((shifts, 3)),
            dma((2,)),
            dma((2,)),
            dma((PIECES + out_tiles,)),
            dma((PIECES + out_tiles,)),
            dma((2, half_way)),
            dma((2, half_way)),
            dma((2, half_way + 1)),
            dma((2, half_way + 1)),
            dma,
            dma((2, half_way, PIECES)),
            dma((2, half_way, PIECES)),
            dma((2, half_way)),
            dma((2, half_way)),
            dma((2, half_way + 1, PIECES)),
            dma((2, half_way + 1, PIECES)),
            dma((2, chips)),
            dma((2, half_way, PIECES)),
            dma((2, half_way, PIECES)),
            dma((chips,)),
            dma((chips,)),
            dma((2, PIECES)),
        ],
        compiler_params=pltpu.CompilerParams(
            collective_id=2, has_side_effects=True, vmem_limit_bytes=VMEM_BYTES
        ),
        name="layer",
    )(residual, queries, keys, values, segments.reshape(1, -1), sinks.reshape(1, -1), gain.reshape(1, -1),
      expert_ids.T, route_weight.T, w_out, w_gate_up, w_down).astype(bf16)


def local(
    residual,
    query_states,
    key_states,
    value_states,
    segment_ids,
    sink_logits,
    w_out,
    norm_gain,
    expert_ids,
    route_weight,
    w_gate_up,
    w_down,
):
    tok_rows = query_states.shape[0]
    row_count = lax.axis_size("row")
    col_count = lax.axis_size("col")
    row_index = lax.axis_index("row")
    col_index = lax.axis_index("col")
    local_heads = sink_logits.shape[0]
    group_size = HEADS // KV_HEADS
    if local_heads >= group_size:
        kv_count = local_heads // group_size
        kv_first = col_index * kv_count
    else:
        kv_count = 1
        kv_first = col_index * local_heads // group_size
    kv_width = kv_count * HEAD_DIM
    own_keys = lax.dynamic_slice_in_dim(key_states, kv_first * HEAD_DIM, kv_width, 1)
    own_values = lax.dynamic_slice_in_dim(value_states, kv_first * HEAD_DIM, kv_width, 1)
    shift_count = (WINDOW + tok_rows - 2) // tok_rows
    block_bytes = 2 * residual.shape[0] * residual.shape[1]
    experts_all = w_gate_up.shape[0] * row_count
    slot_cap = max(2, 2 * TOP * tok_rows // experts_all)
    weight_bytes = 2 * (w_out.size + w_gate_up.size + w_down.size)
    in_kernels = (
        col_count == 2 and row_count % 4 == 0 and row_count >= 8 and tok_rows % 64 == 0
        and kv_width % 128 == 0 and kv_width * col_count == key_states.shape[1]
        and slot_cap % 16 == 0 and 2 * slot_cap == tok_rows and 2 * HEAD_DIM == 128
        and local_heads % (2 * kv_count) == 0 and weight_bytes + 3 * row_count * block_bytes < VMEM_BYTES
    )
    feature_count = residual.shape[1] // col_count
    if in_kernels:
        return layer(
            residual, query_states, key_states, value_states, segment_ids, sink_logits, w_out, norm_gain,
            expert_ids, route_weight, w_gate_up, w_down, row_count, slot_cap, shift_count, kv_width,
            feature_count,
        )
    routing = jnp.concatenate([expert_ids.astype(jnp.float32), route_weight], 1).T
    key_parts = []
    value_parts = []
    segment_parts = []
    start_parts = []
    for offset in range(shift_count, 0, -1):
        arrived = shifted((own_keys, own_values, segment_ids), "row", offset)
        key_parts.append(arrived[0])
        value_parts.append(arrived[1])
        segment_parts.append(arrived[2])
        start_parts.append((row_index - offset) * tok_rows)
    key_parts.append(own_keys)
    value_parts.append(own_values)
    segment_parts.append(segment_ids)
    start_parts.append(row_index * tok_rows)
    key_groups = jnp.concatenate(key_parts, 0).reshape(-1, kv_count, HEAD_DIM)
    value_groups = jnp.concatenate(value_parts, 0).reshape(-1, kv_count, HEAD_DIM)
    key_segments = jnp.concatenate(segment_parts, 0)
    positions = jnp.arange(tok_rows, dtype=jnp.int32)
    key_position = jnp.concatenate([start + positions for start in start_parts], 0)
    query_position = row_index * tok_rows + positions
    allowed = (key_position[None, :] >= 0) & (key_position[None, :] <= query_position[:, None])
    allowed = allowed & (key_position[None, :] > query_position[:, None] - WINDOW)
    allowed = allowed & (key_segments[None, :] == segment_ids[:, None])
    query_groups = query_states.reshape(tok_rows, kv_count, local_heads // kv_count, HEAD_DIM)
    sink_groups = sink_logits.reshape(kv_count, local_heads // kv_count, 1, 1)
    attended = attend(query_groups, key_groups, value_groups, allowed, sink_groups).reshape(
        tok_rows, local_heads * HEAD_DIM
    )
    partial_value = jnp.dot(attended, w_out, preferred_element_type=jnp.float32)
    expert_gate_up = w_gate_up[0]
    expert_down = w_down[0]
    partial_value = partial_value.astype(jnp.bfloat16)
    summed = lax.psum(partial_value, "col").astype(jnp.float32)
    stream = (residual.astype(jnp.float32) + summed).astype(jnp.bfloat16)
    gathered = lax.all_gather(normalize(stream, norm_gain), "row", axis=0, tiled=False)
    routing = lax.all_gather(routing, "row", axis=0, tiled=False)
    stream_part = lax.dynamic_slice_in_dim(stream, col_index * feature_count, feature_count, 1)
    names_mine = routing[:, :TOP] == row_index.astype(jnp.float32)
    mine = jnp.any(names_mine, axis=1)
    weight = jnp.sum(jnp.where(names_mine, routing[:, TOP:], 0.0), axis=1)
    token_order = jnp.arange(tok_rows, dtype=jnp.int32)
    not_after = (token_order[:, None] <= token_order[None, :]).astype(jnp.bfloat16)
    slot_of = jnp.dot(
        mine.astype(jnp.bfloat16), not_after, preferred_element_type=jnp.float32
    ).astype(jnp.int32) - 1
    slots = jnp.arange(slot_cap, dtype=jnp.int32)
    chosen = mine[:, None, :] & (slot_of[:, None, :] == slots[None, :, None])
    selector = chosen.astype(jnp.bfloat16)
    combine = jnp.where(chosen, weight[:, None, :], 0.0)
    packed = jnp.einsum(
        "nst,ntd->nsd", selector, gathered, preferred_element_type=jnp.float32
    ).astype(jnp.bfloat16).reshape(row_count * slot_cap, -1)
    gate = jnp.dot(packed, expert_gate_up[0], preferred_element_type=jnp.float32)
    up = jnp.dot(packed, expert_gate_up[1], preferred_element_type=jnp.float32)
    active = ((up + 1.0) * gate * jax.nn.sigmoid(1.702 * gate)).astype(jnp.bfloat16)
    expert_partial = jnp.dot(active, expert_down, preferred_element_type=jnp.float32)
    scaled = expert_partial.reshape(row_count, slot_cap, -1) * jnp.sum(combine, 2)[:, :, None]
    mixed = jnp.einsum(
        "nst,nsd->ntd", selector, scaled.astype(jnp.bfloat16), preferred_element_type=jnp.float32
    ).astype(jnp.bfloat16)
    mixed = mixed.reshape(row_count * tok_rows, -1)
    mixed = lax.psum_scatter(mixed, "row", scatter_dimension=0, tiled=True)
    mixed = lax.psum_scatter(mixed, "col", scatter_dimension=1, tiled=True)
    return (stream_part.astype(jnp.float32) + mixed.astype(jnp.float32)).astype(jnp.bfloat16)


def solution(mesh):
    in_specs = (
        P("row", None),
        P("row", "col"),
        P("row", None),
        P("row", None),
        P("row"),
        P("col"),
        P("col", None),
        P(),
        P("row", None),
        P("row", None),
        P("row", None, None, "col"),
        P("row", "col", None),
    )
    out_specs = P("row", "col")
    return jax.shard_map(local, mesh=mesh, in_specs=in_specs, out_specs=out_specs, check_vma=False)
```

```python
import jax
import jax.numpy as jnp
from jax import lax
from jax.experimental import pallas as pl
from jax.experimental.pallas import tpu as pltpu
from jax.sharding import PartitionSpec as P

HEADS = 64
KV_HEADS = 8
HEAD_DIM = 64
WINDOW = 128
TOP = 4


epsilon = 1e-05
masked_score = -1e30


def shifted(shard, axis, by):
    size = lax.axis_size(axis)
    pairs = [(i, i + by) for i in range(size) if 0 <= i + by < size]
    return lax.ppermute(shard, axis, pairs)


def normalize(stream_rows, norm_gain):
    values32 = stream_rows.astype(jnp.float32)
    square_mean = jnp.mean(values32 * values32, axis=-1, keepdims=True)
    return (values32 * lax.rsqrt(square_mean + epsilon) * norm_gain).astype(jnp.bfloat16)


def attend(query_groups, key_groups, value_groups, allowed, sink_groups):
    scores = jnp.einsum(
        "tgjd,lgd->gjtl", query_groups, key_groups, preferred_element_type=jnp.float32
    )
    scores = scores * query_groups.shape[-1] ** (-0.5)
    scores = jnp.where(allowed[None, None], scores, masked_score)
    peak_score = jnp.maximum(jnp.max(scores, axis=-1, keepdims=True), sink_groups)
    numerator = jnp.exp(scores - peak_score)
    denominator = jnp.exp(sink_groups - peak_score) + jnp.sum(numerator, axis=-1, keepdims=True)
    weights = (numerator / denominator).astype(jnp.bfloat16)
    return jnp.einsum(
        "gjtl,lgd->tgjd", weights, value_groups, preferred_element_type=jnp.float32
    ).astype(jnp.bfloat16)


MESH = pl.DeviceIdType.MESH
VMEM = pl.BlockSpec(memory_space=pltpu.VMEM)
PIECES = 4
VMEM_BYTES = 61 * 1024 * 1024


def ring_place(row, chips):
    chip = lax.div(row, 2)
    along = lax.div(chip, 2)
    return jnp.where(lax.rem(chip, 2) == 0, along, chips - 1 - along)


def ring_row(place, chips, core):
    place = lax.rem(place + chips, chips)
    chip = jnp.where(place < chips // 2, 2 * place, 2 * (chips - 1 - place) + 1)
    return 2 * chip + core


def greet(devices):
    barrier = pltpu.get_barrier_semaphore()
    for device in devices:
        pl.semaphore_signal(barrier, inc=1, device_id=device, device_id_type=MESH)
    pl.semaphore_wait(barrier, len(devices))


def remote(src, dst, send, recv, device):
    return pltpu.make_async_remote_copy(
        src_ref=src, dst_ref=dst, send_sem=send, recv_sem=recv, device_id=device,
        device_id_type=MESH,
    )


def ring_pieces(distance, half_way, way):
    if distance < half_way:
        return [0, 1, 2]
    return [0, 1] if way == 0 else [2, 3]


def piece_rows(index, size):
    col = lax.axis_index("col")
    start = (index + col * (PIECES - 1 - 2 * index)) * size
    return pl.ds(pl.multiple_of(start, size), size)


BUDGET = 2.0


def attend_all(row, shifts, query_ref, key_all, value_all, segment_ref, segment_all, sink_ref, attended):
    tokens = query_ref.shape[0]
    keys = key_all.shape[0]
    groups = key_all.shape[1] // HEAD_DIM
    heads = sink_ref.shape[1] // groups
    pairs = heads // 2
    lanes = 2 * HEAD_DIM
    segments = [segment_all[at] for at in range(shifts - 1, -1, -1)] + [segment_ref[...]]
    rest = keys - (shifts + 1) * tokens
    if rest:
        segments.append(jnp.full((1, rest), -1, jnp.int32))
    key_segment = jnp.concatenate(segments, 1).astype(jnp.float32)
    diagonal = lax.broadcasted_iota(jnp.int32, (tokens, tokens), 0) == lax.broadcasted_iota(
        jnp.int32, (tokens, tokens), 1
    )
    query_segment = jnp.sum(
        jnp.where(diagonal, segment_ref[...].astype(jnp.float32), 0.0), axis=1, keepdims=True
    )
    query_at = shifts * tokens + lax.broadcasted_iota(jnp.int32, (tokens, keys), 0)
    key_at = lax.broadcasted_iota(jnp.int32, (tokens, keys), 1)
    allowed = (key_at <= query_at) & (key_at > query_at - WINDOW) & (key_at + row * tokens >= shifts * tokens)
    allowed = allowed & (key_segment == query_segment)
    bias = jnp.where(allowed, 0.0, masked_score)
    bias = jnp.concatenate([bias] * pairs, 0).T
    values_turned = value_all[...].astype(jnp.float32).T.astype(jnp.bfloat16)
    lower = lax.broadcasted_iota(jnp.int32, (keys, lanes), 1) < HEAD_DIM
    pair_of = lax.broadcasted_iota(jnp.int32, (1, pairs * tokens), 1)
    nothing = jnp.zeros((HEAD_DIM, keys), jnp.bfloat16)
    for group in range(groups):
        tile = group // 2 * lanes
        straight = key_all[:, tile:tile + lanes]
        turned = jnp.concatenate([straight[:, HEAD_DIM:], straight[:, :HEAD_DIM]], 1)
        first, second = (straight, turned) if group % 2 == 0 else (turned, straight)
        zero = jnp.zeros_like(straight)
        both_keys = jnp.concatenate([jnp.where(lower, first, zero), jnp.where(lower, zero, second)], 0)
        value = values_turned[group * HEAD_DIM:(group + 1) * HEAD_DIM]
        both_values = jnp.concatenate(
            [jnp.concatenate([value, nothing], 1), jnp.concatenate([nothing, value], 1)], 0
        )
        first_lane = group * heads * HEAD_DIM
        queries = jnp.concatenate(
            [query_ref[:, first_lane + pair * lanes:first_lane + (pair + 1) * lanes] for pair in range(pairs)], 0
        )
        scores = lax.dot_general(
            both_keys, queries, (((1,), (1,)), ((), ())), preferred_element_type=jnp.float32
        )
        halves = []
        for half in range(2):
            sink = jnp.full(pair_of.shape, sink_ref[0, group * heads + half])
            for pair in range(1, pairs):
                sink = jnp.where(
                    pair_of >= pair * tokens, sink_ref[0, group * heads + 2 * pair + half], sink
                )
            block = scores[half * keys:(half + 1) * keys] * HEAD_DIM ** (-0.5) + bias
            peak = jnp.maximum(jnp.max(block, axis=0, keepdims=True), sink)
            numerator = jnp.exp(block - peak)
            denominator = jnp.exp(sink - peak) + jnp.sum(numerator, axis=0, keepdims=True)
            halves.append((numerator * (1.0 / denominator)).astype(jnp.bfloat16))
        mixed = jnp.dot(
            both_values, jnp.concatenate(halves, 0), preferred_element_type=jnp.float32
        ).T.astype(jnp.bfloat16)
        for pair in range(pairs):
            attended[:, first_lane + pair * lanes:first_lane + (pair + 1) * lanes] = mixed[
                pair * tokens:(pair + 1) * tokens
            ]


def tiles(total, step):
    return [(start, min(step, total - start)) for start in range(0, total, step)]


def expert_kernel(rows, cap, shifts, residual_hbm, query_hbm, key_ref, value_ref, segment_ref, sink_ref, gain_hbm,
                  ids_ref, weight_ref, w_out_hbm, gate_up_hbm, down_hbm, out_ref,
                  residual_ref, query_ref, gain_ref, i_sem, w_out, key_all, value_all, segment_all, attended, partial_ref, meta_ref,
                  gate_up, down, gathered, metas, part_in, stream, packed, active, slot_weight, select,
                  slots, sib_slots, mix, ring_in, ring_out, over_in, keep, x_out, x_in,
                  o_sem, h_send, h_recv, w_sem, x_sem, c_send, c_recv, m_send, m_recv, n_send, n_recv, l_sem, send, recv,
                  over_send, over_recv, sib_send, sib_recv, slot_sem, f_send, f_recv, fo_send, fo_recv, fx_sem):
    chips = rows // 2
    half_way = chips // 2
    row = lax.axis_index("row")
    col = lax.axis_index("col")
    core = lax.rem(row, 2)
    place = ring_place(row, chips)
    other = row + 1 - 2 * core
    sibling = {"row": other}
    partner = {"col": 1 - col}
    ways = [{"row": ring_row(place + 1, chips, core)}, {"row": ring_row(place - 1, chips, core)}]
    tokens, features = residual_ref.shape
    size = tokens // PIECES
    held = chips * tokens
    depth = w_out.shape[1]
    out_tiles = tiles(features, held)
    out_loads = [
        pltpu.make_async_copy(
            w_out_hbm.at[pl.ds(at * tokens, tokens)], mix.at[at, :, pl.ds(0, depth)],
            o_sem.at[len(out_tiles) + at],
        )
        for at in range(chips)
    ] + [
        pltpu.make_async_copy(w_out_hbm.at[pl.ds(start, width)], w_out.at[pl.ds(start - held, width)], o_sem.at[at])
        for at, (start, width) in enumerate(out_tiles) if at
    ]
    kv_width = key_all.shape[1]
    own_lanes = pl.ds(pl.multiple_of(col * kv_width, kv_width), kv_width)
    here = pl.ds(shifts * tokens, tokens)
    inputs = [
        pltpu.make_async_copy(key_ref.at[:, own_lanes], key_all.at[here], i_sem.at[0]),
        pltpu.make_async_copy(value_ref.at[:, own_lanes], value_all.at[here], i_sem.at[1]),
        pltpu.make_async_copy(query_hbm, query_ref, i_sem.at[2]),
        pltpu.make_async_copy(residual_hbm, residual_ref, i_sem.at[3]),
        pltpu.make_async_copy(gain_hbm, gain_ref.at[0], i_sem.at[4]),
    ]
    for load in inputs + out_loads:
        load.start()
    loads = [
        pltpu.make_async_copy(gate_up_hbm.at[0], gate_up, w_sem.at[0]),
        pltpu.make_async_copy(down_hbm.at[0], down, w_sem.at[1]),
    ]
    after = [{"row": lax.rem(row + shift, rows)} for shift in range(1, shifts + 1)]
    before = [{"row": lax.rem(row + rows - shift, rows)} for shift in range(1, shifts + 1)]
    greet(after + before + [sibling, partner] + ways)
    halos = []
    for at in range(shifts):
        there = pl.ds((shifts - 1 - at) * tokens, tokens)
        for which, (src, dst) in enumerate([
            (segment_ref, segment_all.at[at]),
            (key_ref.at[:, own_lanes], key_all.at[there]),
            (value_ref.at[:, own_lanes], value_all.at[there]),
        ]):
            halos.append(remote(src, dst, h_send.at[at, which], h_recv.at[at, which], after[at]))
            halos[-1].start()
    rest = key_all.shape[0] - (shifts + 1) * tokens
    for every in [key_all, value_all]:
        if rest:
            every[pl.ds((shifts + 1) * tokens, rest), :] = jnp.zeros((rest, kv_width), every.dtype)
    meta_ref[:TOP, :] = ids_ref[...].astype(jnp.float32)
    meta_ref[TOP:, :] = weight_ref[...]
    local_meta = pltpu.make_async_copy(meta_ref, metas.at[row], l_sem)
    local_meta.start()
    for load in inputs[:3]:
        load.wait()
    for halo in halos:
        halo.wait_recv()
    for load in loads:
        load.start()
    attend_all(row, shifts, query_ref, key_all, value_all, segment_ref, segment_all, sink_ref, attended)

    first_rows = pl.ds(pl.multiple_of((1 - col) * 2 * size, 2 * size), 2 * size)
    early = []
    for at, (start, width) in enumerate(out_tiles):
        for load in out_loads[:chips] if at == 0 else [out_loads[chips - 1 + at]]:
            load.wait()
        lanes = pl.ds(start, width)
        rows_out = (
            mix[:, :, :depth].reshape(held, depth) if at == 0 else w_out[pl.ds(start - held, width), :]
        )
        partial_ref[:, lanes] = lax.dot_general(
            attended[...], rows_out, (((1,), (1,)), ((), ())), preferred_element_type=jnp.float32
        ).astype(jnp.bfloat16)
        early.append(remote(partial_ref.at[first_rows, lanes], part_in.at[first_rows, lanes], c_send.at[PIECES + at],
                            c_recv.at[PIECES + at], partner))
        early[-1].start()
    crosses = {}
    for index in [1, 0]:
        at = piece_rows(index, size)
        named = PIECES - 1 - index
        crosses[index] = remote(partial_ref.at[at], part_in.at[at], c_send.at[named],
                                c_recv.at[named], partner)
        crosses[index].start()
    for load in inputs[3:]:
        load.wait()
    for copy in early:
        copy.wait_recv()

    def ready(index):
        at = piece_rows(index, size)
        if index >= 2:
            remote(partial_ref.at[at], part_in.at[at], c_send.at[index], c_recv.at[index],
                   partner).wait_recv()
        summed = partial_ref[at, :].astype(jnp.float32) + part_in[at, :].astype(jnp.float32)
        total = (residual_ref[at, :].astype(jnp.float32) + summed).astype(jnp.bfloat16)
        stream[at, :] = total
        gathered[row, at, :] = normalize(total, gain_ref[...])

    def part(offset, index, which):
        return gathered.at[ring_row(place + offset, chips, which), piece_rows(index, size)]

    def offset_of(way, distance):
        return -distance if way == 0 else distance

    def hop(way, distance, index, sending):
        at = part(offset_of(way, distance - 1 if sending else distance), index, core)
        return remote(at, at, send.at[way, distance - 1, index], recv.at[way, distance - 1, index],
                      ways[way])

    def over(way, distance, sending):
        at = part(offset_of(way, distance), 0 if sending else PIECES - 1, core)
        return remote(at, at, over_send.at[way, distance - 1], over_recv.at[way, distance - 1],
                      partner)

    def pass_on(way, distance, index, which):
        at = part(offset_of(way, distance), index, which)
        return remote(at, at, sib_send.at[way, distance, index], sib_recv.at[way, distance, index],
                      sibling)

    def routing_hop(way, distance, sending):
        back = offset_of(way, distance - 1 if sending else distance)
        at = metas.at[ring_row(place + back, chips, core)]
        return remote(at, at, m_send.at[way, distance - 1], m_recv.at[way, distance - 1], ways[way])

    def routing_on(way, distance, which):
        at = metas.at[ring_row(place + offset_of(way, distance), chips, which)]
        return remote(at, at, n_send.at[way, distance], n_recv.at[way, distance], sibling)

    sent = []

    def go(copy):
        copy.start()
        sent.append(copy)

    reach = [half_way, half_way - 1]
    theirs = gathered.at[other]

    def offsets(distances):
        return [
            offset for distance in distances for offset in sorted({distance, (chips - distance) % chips})
        ]

    def blocks_of(distances):
        return [(offset, which) for offset in offsets(distances) for which in range(2)]

    def first_slot(distance):
        return cap * len(blocks_of(range(distance)))

    def wait_for(distances):
        for distance in distances:
            if distance == 0:
                remote(theirs, theirs, x_sem.at[0], x_sem.at[1], sibling).wait_recv()
                routing_on(0, 0, 1 - core).wait_recv()
                continue
            for way in range(2):
                if distance <= reach[way]:
                    routing_on(way, distance, 1 - core).wait_recv()
                indices = list(ring_pieces(distance, half_way, way))
                for index in indices + ([PIECES - 1] if distance < half_way else []):
                    pass_on(way, distance, index, 1 - core).wait_recv()

    def pack(distance):
        blocks = blocks_of([distance])
        not_after = lax.broadcasted_iota(jnp.int32, (tokens, tokens), 0) <= lax.broadcasted_iota(
            jnp.int32, (tokens, tokens), 1
        )
        not_after = jnp.where(not_after, 1.0, 0.0).astype(jnp.bfloat16)
        numbers = lax.broadcasted_iota(jnp.int32, (cap, tokens), 0).astype(jnp.float32)
        named, weights = [], []
        wanted = [(offset, which, row) for offset, which in blocks]
        wanted += [(offset, 0, other) for offset, which in blocks if which == 0]
        for offset, which, expert in wanted:
            meta = metas[ring_row(place + offset, chips, core if which == 0 else 1 - core)]
            hit = jnp.where(meta[:TOP] == expert.astype(jnp.float32), 1.0, 0.0)
            named.append(jnp.max(hit, axis=0, keepdims=True))
            weights.append(jnp.sum(hit * meta[TOP:], axis=0, keepdims=True))
        hits = jnp.concatenate(named, 0)
        order = jnp.dot(hits.astype(jnp.bfloat16), not_after, preferred_element_type=jnp.float32)
        chosen = [
            jnp.where(order[at:at + 1] == numbers + 1.0, 1.0, 0.0) * named[at]
            for at in range(len(wanted))
        ]
        for at, (offset, which) in enumerate(blocks):
            here = pl.ds(first_slot(distance) + at * cap, cap)
            weight = jnp.sum(chosen[at] * weights[at], axis=1, keepdims=True)
            slot_weight[here, :] = jnp.broadcast_to(weight, (cap, slot_weight.shape[1]))
            source = ring_row(place + offset, chips, core if which == 0 else 1 - core)
            packed[here, :] = jnp.dot(
                chosen[at].astype(jnp.bfloat16), gathered[source],
                preferred_element_type=jnp.float32,
            ).astype(jnp.bfloat16)
        for at, (offset, which) in enumerate(blocks[::2]):
            both = jnp.concatenate([chosen[2 * at], chosen[len(blocks) + at]], 0)
            select[offset] = both.T.astype(jnp.bfloat16)

    def gate_and_up(distances, start, width):
        count = cap * len(blocks_of(distances))
        values = packed[pl.ds(first_slot(distances[0]), count), :]
        lanes = pl.ds(start, width)
        last = (((1,), (1,)), ((), ()))
        gate = lax.dot_general(values, gate_up[0, lanes, :], last, preferred_element_type=jnp.float32)
        up = lax.dot_general(values, gate_up[1, lanes, :], last, preferred_element_type=jnp.float32)
        active[:count, lanes] = ((up + 1.0) * gate * jax.nn.sigmoid(1.702 * gate)).astype(jnp.bfloat16)

    def go_down(distances, first, last, start, width):
        blocks = blocks_of(distances)[first:last]
        lanes = pl.ds(start, width)
        count = (last - first) * cap
        result = jnp.dot(
            active[pl.ds(first * cap, count), :], down[:, lanes], preferred_element_type=jnp.float32
        )
        scale = slot_weight[pl.ds(first_slot(distances[0]) + first * cap, count), :1]
        result = (result * scale).astype(jnp.bfloat16)
        for at, (offset, which) in enumerate(blocks):
            piece = result[at * cap:(at + 1) * cap]
            if which == 0:
                slots[offset, :cap, lanes] = piece
            else:
                sib_slots[offset, :, lanes] = piece

    def slot_copy(offset):
        return remote(sib_slots.at[offset], slots.at[offset, pl.ds(cap, cap)], slot_sem.at[0, offset],
                      slot_sem.at[1, offset], sibling)

    queue = []

    def work(budget):
        while queue and budget > 0:
            cost, step = queue.pop(0)
            step()
            budget -= cost

    def enqueue_pack(distance):
        queue.append((0.1, lambda: wait_for([distance])))
        queue.append((0.5, lambda: pack(distance)))

    def enqueue_products(distances, last_first):
        if distances[0] == 0:
            queue.append((0.0, lambda: loads[0].wait()))
        for start, width in tiles(gate_up.shape[1], 256):
            queue.append((1.0, lambda start=start, width=width: gate_and_up(distances, start, width)))
        if distances[0] == 0:
            queue.append((0.0, lambda: loads[1].wait()))
        count = len(blocks_of(distances))
        split = count - len(blocks_of(distances[-1:]))
        for begin, end in ((split, count), (0, split)) if last_first else ((0, count),):
            for start, width in tiles(down.shape[1], 512):
                queue.append((0.4, lambda start=start, width=width, begin=begin, end=end: go_down(
                    distances, begin, end, start, width)))
            queue.append((0.2, lambda begin=begin, end=end: [
                go(slot_copy(offset)) for offset in offsets(distances)[begin // 2:end // 2]]))

    near, mid = half_way // 4, half_way // 2
    batches = [range(near + 1), range(near + 1, mid + 1), range(mid + 1, half_way + 1)]
    for index in [0, 1, 2]:
        ready(index)
        for way in range(2):
            if index in ring_pieces(1, half_way, way):
                go(hop(way, 1, index, True))
    ready(PIECES - 1)
    local_meta.wait()
    for way in range(2):
        go(routing_hop(way, 1, True))
    go(routing_on(0, 0, core))
    mine = gathered.at[row]
    go(remote(mine, mine, x_sem.at[0], x_sem.at[1], sibling))

    def take_over(distance):
        for way in range(2):
            over(way, distance, False).wait_recv()
            if distance + 1 == half_way and way == 1:
                go(hop(way, half_way, PIECES - 1, True))
            go(pass_on(way, distance, PIECES - 1, core))

    for distance in range(1, half_way + 1):
        for step, index in enumerate([0, 1, 2] if distance < half_way else [0, 2, 1, 3]):
            for way in range(2):
                if index not in ring_pieces(distance, half_way, way):
                    continue
                hop(way, distance, index, False).wait_recv()
                if distance < half_way and index in ring_pieces(distance + 1, half_way, way):
                    go(hop(way, distance + 1, index, True))
                if index == 0 and distance < half_way:
                    go(over(way, distance, True))
                go(pass_on(way, distance, index, core))
            if step == 0:
                enqueue_pack(distance - 1)
                for batch in batches[:-1]:
                    if batch[-1] == distance - 1:
                        enqueue_products(batch, False)
            work(BUDGET)
        for way in range(2):
            if distance <= reach[way]:
                routing_hop(way, distance, False).wait_recv()
                if distance < reach[way]:
                    go(routing_hop(way, distance + 1, True))
                go(routing_on(way, distance, core))
        if distance < half_way:
            take_over(distance)
    enqueue_pack(half_way)
    enqueue_products(batches[-1], True)
    work(100)

    def combine(offset):
        slot_copy(offset).wait_recv()
        mix[offset] = jnp.dot(
            select[offset], slots[offset], preferred_element_type=jnp.float32
        ).astype(jnp.bfloat16)

    def fold_hop(way, distance, index):
        at = pl.ds(index % (PIECES - 1) * size, size)
        return remote(ring_out.at[way, distance - 1, at], ring_in.at[way, distance - 1, at],
                      f_send.at[way, distance - 1, index], f_recv.at[way, distance - 1, index],
                      ways[way])

    def arrived(way, distance, index):
        fold_hop(way, distance, index).wait_recv()
        return ring_in[way, distance - 1, pl.ds(index % (PIECES - 1) * size, size), :].astype(jnp.float32)

    def fold_over(offset):
        return remote(mix.at[offset, piece_rows(PIECES - 1, size)], over_in.at[offset],
                      fo_send.at[offset], fo_recv.at[offset], partner)

    def fold_step(way, distance, index):
        offset = distance if way == 0 else chips - distance
        at = piece_rows(index, size)
        value = mix[offset, at, :].astype(jnp.float32)
        if distance < half_way and index in ring_pieces(distance + 1, half_way, way):
            value = value + arrived(way, distance + 1, index)
        if distance < half_way and index == PIECES - 1:
            mix[offset, at, :] = value.astype(jnp.bfloat16)
            go(fold_over(offset))
            return
        if index == 0 and distance < half_way:
            fold_over(offset).wait_recv()
            value = value + over_in[offset].astype(jnp.float32)
        ring_out[way, distance - 1, pl.ds(index % (PIECES - 1) * size, size), :] = value.astype(
            jnp.bfloat16
        )
        go(fold_hop(way, distance, index))

    for distance in range(half_way, 0, -1):
        for offset in offsets([distance]):
            combine(offset)
        if distance == half_way:
            steps = [(1, 3), (0, 1), (1, 2), (0, 0)]
        elif distance == half_way - 1:
            steps = [(0, 3), (0, 2), (1, 1), (1, 3), (0, 1), (1, 2), (0, 0), (1, 0)]
        else:
            steps = [(0, 3), (1, 3), (0, 1), (1, 1), (0, 2), (1, 2), (0, 0), (1, 0)]
        for way, index in steps:
            fold_step(way, distance, index)
    combine(0)
    width = out_ref.shape[1]
    for index in [3, 1, 2, 0]:
        at = piece_rows(index, size)
        value = mix[0, at, :].astype(jnp.float32)
        for way in range(2):
            if index in ring_pieces(1, half_way, way):
                value = value + arrived(way, 1, index)
        low, high = value[:, :width], value[:, width:]
        x_out[at, :] = jnp.where(col == 0, high, low).astype(jnp.bfloat16)
        go(remote(x_out.at[at], x_in.at[at], fx_sem.at[0, index], fx_sem.at[1, index], partner))
        base = stream[at, :].astype(jnp.float32)
        keep[at, :] = jnp.where(col == 0, low, high) + jnp.where(
            col == 0, base[:, :width], base[:, width:]
        )
    for index in [0, 2, 1, 3]:
        at = piece_rows(index, size)
        named = PIECES - 1 - index
        remote(x_out.at[at], x_in.at[at], fx_sem.at[0, named], fx_sem.at[1, named],
               partner).wait_recv()
        out_ref[at, :] = keep[at, :] + x_in[at, :].astype(jnp.float32)
    for copy in early + halos + list(crosses.values()) + sent:
        copy.wait_send()


def layer(residual, queries, keys, values, segments, sinks, w_out, gain, expert_ids, route_weight, w_gate_up,
          w_down, rows, cap, shifts, kv_width, width):
    w_gate_up = jnp.swapaxes(w_gate_up, 2, 3)
    w_out = w_out.T
    half_way = rows // 4
    chips = rows // 2
    tokens, features = residual.shape
    hidden = w_gate_up.shape[2]
    near, mid = half_way // 4, half_way // 2
    most = cap * 2 * max(2 * near + 1, 2 * (mid - near), 2 * (half_way - mid) - 1)
    key_rows = -(-(shifts + 1) * tokens // 128) * 128
    out_tiles = len(tiles(features, chips * tokens))
    meta = (2 * TOP, tokens)
    bf16, f32, dma = jnp.bfloat16, jnp.float32, pltpu.SemaphoreType.DMA
    hbm = pl.BlockSpec(memory_space=pl.ANY)
    return pl.pallas_call(
        lambda *refs: expert_kernel(rows, cap, shifts, *refs),
        out_shape=jax.ShapeDtypeStruct((tokens, width), f32),
        in_specs=[hbm] * 4 + [VMEM, pl.BlockSpec(memory_space=pltpu.SMEM), hbm, VMEM, VMEM] + [hbm] * 3,
        out_specs=VMEM,
        scratch_shapes=[
            pltpu.VMEM((tokens, features), bf16),
            pltpu.VMEM(queries.shape, bf16),
            pltpu.VMEM((1, features), f32),
            dma((5,)),
            pltpu.VMEM((features - chips * tokens, w_out.shape[1]), bf16),
            pltpu.VMEM((key_rows, kv_width), bf16),
            pltpu.VMEM((key_rows, kv_width), bf16),
            pltpu.VMEM((shifts, 1, tokens), jnp.int32),
            pltpu.VMEM(queries.shape, bf16),
            pltpu.VMEM((tokens, features), bf16),
            pltpu.VMEM(meta, f32),
            pltpu.VMEM(w_gate_up.shape[1:], bf16),
            pltpu.VMEM(w_down.shape[1:], bf16),
            pltpu.VMEM((rows, tokens, features), bf16),
            pltpu.VMEM((rows, *meta), f32),
            pltpu.VMEM((tokens, features), bf16),
            pltpu.VMEM((tokens, features), bf16),
            pltpu.VMEM((rows * cap, features), bf16),
            pltpu.VMEM((most, hidden), bf16),
            pltpu.VMEM((rows * cap, 128), f32),
            pltpu.VMEM((chips, tokens, 2 * cap), bf16),
            pltpu.VMEM((chips, 2 * cap, features), bf16),
            pltpu.VMEM((chips, cap, features), bf16),
            pltpu.VMEM((chips, tokens, features), bf16),
            pltpu.VMEM((2, half_way, tokens // PIECES * (PIECES - 1), features), bf16),
            pltpu.VMEM((2, half_way, tokens // PIECES * (PIECES - 1), features), bf16),
            pltpu.VMEM((chips, tokens // PIECES, features), bf16),
            pltpu.VMEM((tokens, width), f32),
            pltpu.VMEM((tokens, width), bf16),
            pltpu.VMEM((tokens, width), bf16),
            dma((out_tiles + chips,)),
            dma((shifts, 3)),
            dma((shifts, 3)),
            dma((2,)),
            dma((2,)),
            dma((PIECES + out_tiles,)),
            dma((PIECES + out_tiles,)),
            dma((2, half_way)),
            dma((2, half_way)),
            dma((2, half_way + 1)),
            dma((2, half_way + 1)),
            dma,
            dma((2, half_way, PIECES)),
            dma((2, half_way, PIECES)),
            dma((2, half_way)),
            dma((2, half_way)),
            dma((2, half_way + 1, PIECES)),
            dma((2, half_way + 1, PIECES)),
            dma((2, chips)),
            dma((2, half_way, PIECES)),
            dma((2, half_way, PIECES)),
            dma((chips,)),
            dma((chips,)),
            dma((2, PIECES)),
        ],
        compiler_params=pltpu.CompilerParams(
            collective_id=2, has_side_effects=True, vmem_limit_bytes=VMEM_BYTES
        ),
        name="layer",
    )(residual, queries, keys, values, segments.reshape(1, -1), sinks.reshape(1, -1), gain,
      expert_ids.T, route_weight.T, w_out, w_gate_up, w_down).astype(bf16)


def local(
    residual,
    query_states,
    key_states,
    value_states,
    segment_ids,
    sink_logits,
    w_out,
    norm_gain,
    expert_ids,
    route_weight,
    w_gate_up,
    w_down,
):
    tok_rows = query_states.shape[0]
    row_count = lax.axis_size("row")
    col_count = lax.axis_size("col")
    row_index = lax.axis_index("row")
    col_index = lax.axis_index("col")
    local_heads = sink_logits.shape[0]
    group_size = HEADS // KV_HEADS
    if local_heads >= group_size:
        kv_count = local_heads // group_size
        kv_first = col_index * kv_count
    else:
        kv_count = 1
        kv_first = col_index * local_heads // group_size
    kv_width = kv_count * HEAD_DIM
    own_keys = lax.dynamic_slice_in_dim(key_states, kv_first * HEAD_DIM, kv_width, 1)
    own_values = lax.dynamic_slice_in_dim(value_states, kv_first * HEAD_DIM, kv_width, 1)
    shift_count = (WINDOW + tok_rows - 2) // tok_rows
    block_bytes = 2 * residual.shape[0] * residual.shape[1]
    experts_all = w_gate_up.shape[0] * row_count
    slot_cap = max(2, 2 * TOP * tok_rows // experts_all)
    weight_bytes = 2 * (w_out.size + w_gate_up.size + w_down.size)
    in_kernels = (
        col_count == 2 and row_count % 4 == 0 and row_count >= 8 and tok_rows % 64 == 0
        and kv_width % 128 == 0 and kv_width * col_count == key_states.shape[1]
        and row_count // 2 * tok_rows < residual.shape[1] and w_out.shape[0] <= residual.shape[1]
        and slot_cap % 16 == 0 and 2 * slot_cap == tok_rows and 2 * HEAD_DIM == 128
        and local_heads % (2 * kv_count) == 0 and weight_bytes + 3 * row_count * block_bytes < VMEM_BYTES
    )
    feature_count = residual.shape[1] // col_count
    if in_kernels:
        return layer(
            residual, query_states, key_states, value_states, segment_ids, sink_logits, w_out, norm_gain,
            expert_ids, route_weight, w_gate_up, w_down, row_count, slot_cap, shift_count, kv_width,
            feature_count,
        )
    routing = jnp.concatenate([expert_ids.astype(jnp.float32), route_weight], 1).T
    key_parts = []
    value_parts = []
    segment_parts = []
    start_parts = []
    for offset in range(shift_count, 0, -1):
        arrived = shifted((own_keys, own_values, segment_ids), "row", offset)
        key_parts.append(arrived[0])
        value_parts.append(arrived[1])
        segment_parts.append(arrived[2])
        start_parts.append((row_index - offset) * tok_rows)
    key_parts.append(own_keys)
    value_parts.append(own_values)
    segment_parts.append(segment_ids)
    start_parts.append(row_index * tok_rows)
    key_groups = jnp.concatenate(key_parts, 0).reshape(-1, kv_count, HEAD_DIM)
    value_groups = jnp.concatenate(value_parts, 0).reshape(-1, kv_count, HEAD_DIM)
    key_segments = jnp.concatenate(segment_parts, 0)
    positions = jnp.arange(tok_rows, dtype=jnp.int32)
    key_position = jnp.concatenate([start + positions for start in start_parts], 0)
    query_position = row_index * tok_rows + positions
    allowed = (key_position[None, :] >= 0) & (key_position[None, :] <= query_position[:, None])
    allowed = allowed & (key_position[None, :] > query_position[:, None] - WINDOW)
    allowed = allowed & (key_segments[None, :] == segment_ids[:, None])
    query_groups = query_states.reshape(tok_rows, kv_count, local_heads // kv_count, HEAD_DIM)
    sink_groups = sink_logits.reshape(kv_count, local_heads // kv_count, 1, 1)
    attended = attend(query_groups, key_groups, value_groups, allowed, sink_groups).reshape(
        tok_rows, local_heads * HEAD_DIM
    )
    partial_value = jnp.dot(attended, w_out, preferred_element_type=jnp.float32)
    expert_gate_up = w_gate_up[0]
    expert_down = w_down[0]
    partial_value = partial_value.astype(jnp.bfloat16)
    summed = lax.psum(partial_value, "col").astype(jnp.float32)
    stream = (residual.astype(jnp.float32) + summed).astype(jnp.bfloat16)
    gathered = lax.all_gather(normalize(stream, norm_gain), "row", axis=0, tiled=False)
    routing = lax.all_gather(routing, "row", axis=0, tiled=False)
    stream_part = lax.dynamic_slice_in_dim(stream, col_index * feature_count, feature_count, 1)
    names_mine = routing[:, :TOP] == row_index.astype(jnp.float32)
    mine = jnp.any(names_mine, axis=1)
    weight = jnp.sum(jnp.where(names_mine, routing[:, TOP:], 0.0), axis=1)
    token_order = jnp.arange(tok_rows, dtype=jnp.int32)
    not_after = (token_order[:, None] <= token_order[None, :]).astype(jnp.bfloat16)
    slot_of = jnp.dot(
        mine.astype(jnp.bfloat16), not_after, preferred_element_type=jnp.float32
    ).astype(jnp.int32) - 1
    slots = jnp.arange(slot_cap, dtype=jnp.int32)
    chosen = mine[:, None, :] & (slot_of[:, None, :] == slots[None, :, None])
    selector = chosen.astype(jnp.bfloat16)
    combine = jnp.where(chosen, weight[:, None, :], 0.0)
    packed = jnp.einsum(
        "nst,ntd->nsd", selector, gathered, preferred_element_type=jnp.float32
    ).astype(jnp.bfloat16).reshape(row_count * slot_cap, -1)
    gate = jnp.dot(packed, expert_gate_up[0], preferred_element_type=jnp.float32)
    up = jnp.dot(packed, expert_gate_up[1], preferred_element_type=jnp.float32)
    active = ((up + 1.0) * gate * jax.nn.sigmoid(1.702 * gate)).astype(jnp.bfloat16)
    expert_partial = jnp.dot(active, expert_down, preferred_element_type=jnp.float32)
    scaled = expert_partial.reshape(row_count, slot_cap, -1) * jnp.sum(combine, 2)[:, :, None]
    mixed = jnp.einsum(
        "nst,nsd->ntd", selector, scaled.astype(jnp.bfloat16), preferred_element_type=jnp.float32
    ).astype(jnp.bfloat16)
    mixed = mixed.reshape(row_count * tok_rows, -1)
    mixed = lax.psum_scatter(mixed, "row", scatter_dimension=0, tiled=True)
    mixed = lax.psum_scatter(mixed, "col", scatter_dimension=1, tiled=True)
    return (stream_part.astype(jnp.float32) + mixed.astype(jnp.float32)).astype(jnp.bfloat16)


def solution(mesh):
    in_specs = (
        P("row", None),
        P("row", "col"),
        P("row", None),
        P("row", None),
        P("row"),
        P("col"),
        P("col", None),
        P(),
        P("row", None),
        P("row", None),
        P("row", None, None, "col"),
        P("row", "col", None),
    )
    out_specs = P("row", "col")
    return jax.shard_map(local, mesh=mesh, in_specs=in_specs, out_specs=out_specs, check_vma=False)
```

```python
import jax
import jax.numpy as jnp
from jax import lax
from jax.experimental import pallas as pl
from jax.experimental.pallas import tpu as pltpu
from jax.sharding import PartitionSpec as P

HEADS = 64
KV_HEADS = 8
HEAD_DIM = 64
WINDOW = 128
TOP = 4


epsilon = 1e-05
masked_score = -1e30


def shifted(shard, axis, by):
    size = lax.axis_size(axis)
    pairs = [(i, i + by) for i in range(size) if 0 <= i + by < size]
    return lax.ppermute(shard, axis, pairs)


def normalize(stream_rows, norm_gain):
    values32 = stream_rows.astype(jnp.float32)
    square_mean = jnp.mean(values32 * values32, axis=-1, keepdims=True)
    return (values32 * lax.rsqrt(square_mean + epsilon) * norm_gain).astype(jnp.bfloat16)


def attend(query_groups, key_groups, value_groups, allowed, sink_groups):
    scores = jnp.einsum(
        "tgjd,lgd->gjtl", query_groups, key_groups, preferred_element_type=jnp.float32
    )
    scores = scores * query_groups.shape[-1] ** (-0.5)
    scores = jnp.where(allowed[None, None], scores, masked_score)
    peak_score = jnp.maximum(jnp.max(scores, axis=-1, keepdims=True), sink_groups)
    numerator = jnp.exp(scores - peak_score)
    denominator = jnp.exp(sink_groups - peak_score) + jnp.sum(numerator, axis=-1, keepdims=True)
    weights = (numerator / denominator).astype(jnp.bfloat16)
    return jnp.einsum(
        "gjtl,lgd->tgjd", weights, value_groups, preferred_element_type=jnp.float32
    ).astype(jnp.bfloat16)


MESH = pl.DeviceIdType.MESH
VMEM = pl.BlockSpec(memory_space=pltpu.VMEM)
PIECES = 4
VMEM_BYTES = 61 * 1024 * 1024


def ring_place(row, chips):
    chip = lax.div(row, 2)
    along = lax.div(chip, 2)
    return jnp.where(lax.rem(chip, 2) == 0, along, chips - 1 - along)


def ring_row(place, chips, core):
    place = lax.rem(place + chips, chips)
    chip = jnp.where(place < chips // 2, 2 * place, 2 * (chips - 1 - place) + 1)
    return 2 * chip + core


def remote(src, dst, send, recv, device):
    return pltpu.make_async_remote_copy(
        src_ref=src, dst_ref=dst, send_sem=send, recv_sem=recv, device_id=device,
        device_id_type=MESH,
    )


def ring_pieces(distance, half_way, way):
    if distance < half_way:
        return [0, 1, 2]
    return [0, 1] if way == 0 else [2, 3]


def piece_rows(index, size):
    col = lax.axis_index("col")
    start = (index + col * (PIECES - 1 - 2 * index)) * size
    return pl.ds(pl.multiple_of(start, size), size)


BUDGET = 2.0


def attend_all(row, shifts, query_ref, key_all, value_all, segment_ref, segment_all, sink_ref, attended):
    tokens = query_ref.shape[0]
    keys = key_all.shape[0]
    groups = key_all.shape[1] // HEAD_DIM
    heads = sink_ref.shape[1] // groups
    pairs = heads // 2
    lanes = 2 * HEAD_DIM
    segments = [segment_all[at] for at in range(shifts - 1, -1, -1)] + [segment_ref[...]]
    rest = keys - (shifts + 1) * tokens
    if rest:
        segments.append(jnp.full((1, rest), -1, jnp.int32))
    key_segment = jnp.concatenate(segments, 1).astype(jnp.float32)
    diagonal = lax.broadcasted_iota(jnp.int32, (tokens, tokens), 0) == lax.broadcasted_iota(
        jnp.int32, (tokens, tokens), 1
    )
    query_segment = jnp.sum(
        jnp.where(diagonal, segment_ref[...].astype(jnp.float32), 0.0), axis=1, keepdims=True
    )
    query_at = shifts * tokens + lax.broadcasted_iota(jnp.int32, (tokens, keys), 0)
    key_at = lax.broadcasted_iota(jnp.int32, (tokens, keys), 1)
    allowed = (key_at <= query_at) & (key_at > query_at - WINDOW) & (key_at + row * tokens >= shifts * tokens)
    allowed = allowed & (key_segment == query_segment)
    bias = jnp.where(allowed, 0.0, masked_score)
    bias = jnp.concatenate([bias] * pairs, 0).T
    values_turned = value_all[...].astype(jnp.float32).T.astype(jnp.bfloat16)
    lower = lax.broadcasted_iota(jnp.int32, (keys, lanes), 1) < HEAD_DIM
    pair_of = lax.broadcasted_iota(jnp.int32, (1, pairs * tokens), 1)
    nothing = jnp.zeros((HEAD_DIM, keys), jnp.bfloat16)
    for group in range(groups):
        tile = group // 2 * lanes
        straight = key_all[:, tile:tile + lanes]
        turned = jnp.concatenate([straight[:, HEAD_DIM:], straight[:, :HEAD_DIM]], 1)
        first, second = (straight, turned) if group % 2 == 0 else (turned, straight)
        zero = jnp.zeros_like(straight)
        both_keys = jnp.concatenate([jnp.where(lower, first, zero), jnp.where(lower, zero, second)], 0)
        value = values_turned[group * HEAD_DIM:(group + 1) * HEAD_DIM]
        both_values = jnp.concatenate(
            [jnp.concatenate([value, nothing], 1), jnp.concatenate([nothing, value], 1)], 0
        )
        first_lane = group * heads * HEAD_DIM
        queries = jnp.concatenate(
            [query_ref[:, first_lane + pair * lanes:first_lane + (pair + 1) * lanes] for pair in range(pairs)], 0
        )
        scores = lax.dot_general(
            both_keys, queries, (((1,), (1,)), ((), ())), preferred_element_type=jnp.float32
        )
        halves = []
        for half in range(2):
            sink = jnp.full(pair_of.shape, sink_ref[0, group * heads + half])
            for pair in range(1, pairs):
                sink = jnp.where(
                    pair_of >= pair * tokens, sink_ref[0, group * heads + 2 * pair + half], sink
                )
            block = scores[half * keys:(half + 1) * keys] * HEAD_DIM ** (-0.5) + bias
            peak = jnp.maximum(jnp.max(block, axis=0, keepdims=True), sink)
            numerator = jnp.exp(block - peak)
            denominator = jnp.exp(sink - peak) + jnp.sum(numerator, axis=0, keepdims=True)
            halves.append((numerator * (1.0 / denominator)).astype(jnp.bfloat16))
        mixed = jnp.dot(
            both_values, jnp.concatenate(halves, 0), preferred_element_type=jnp.float32
        ).T.astype(jnp.bfloat16)
        for pair in range(pairs):
            attended[:, first_lane + pair * lanes:first_lane + (pair + 1) * lanes] = mixed[
                pair * tokens:(pair + 1) * tokens
            ]


def tiles(total, step):
    return [(start, min(step, total - start)) for start in range(0, total, step)]


def expert_kernel(rows, cap, shifts, residual_hbm, query_hbm, key_ref, value_ref, segment_hbm, sink_hbm, gain_hbm,
                  ids_hbm, weight_hbm, w_out_hbm, gate_up_hbm, down_hbm, out_hbm,
                  residual_ref, query_ref, gain_ref, segment_ref, sink_ref, ids_ref, weight_ref, out_ref, y_sem,
                  i_sem, w_out, key_all, value_all, segment_all, attended, partial_ref, meta_ref,
                  gate_up, down, gathered, metas, part_in, stream, packed, active, slot_weight, select,
                  slots, sib_slots, mix, ring_in, ring_out, over_in, x_out, x_in,
                  o_sem, h_send, h_recv, w_sem, x_sem, c_send, c_recv, m_send, m_recv, n_send, n_recv, l_sem, send, recv,
                  over_send, over_recv, sib_send, sib_recv, slot_sem, f_send, f_recv, fo_send, fo_recv, fx_sem):
    chips = rows // 2
    half_way = chips // 2
    row = lax.axis_index("row")
    col = lax.axis_index("col")
    core = lax.rem(row, 2)
    place = ring_place(row, chips)
    other = row + 1 - 2 * core
    sibling = {"row": other}
    partner = {"col": 1 - col}
    ways = [{"row": ring_row(place + 1, chips, core)}, {"row": ring_row(place - 1, chips, core)}]
    tokens, features = residual_ref.shape
    size = tokens // PIECES
    held = chips * tokens
    depth = w_out.shape[1]
    out_tiles = tiles(features, held)
    out_loads = [
        pltpu.make_async_copy(
            w_out_hbm.at[pl.ds(at * tokens, tokens)], mix.at[at, :, pl.ds(0, depth)],
            o_sem.at[len(out_tiles) + at],
        )
        for at in range(chips)
    ] + [
        pltpu.make_async_copy(w_out_hbm.at[pl.ds(start, width)], w_out.at[pl.ds(start - held, width)], o_sem.at[at])
        for at, (start, width) in enumerate(out_tiles) if at
    ]
    kv_width = key_all.shape[1]
    own_lanes = pl.ds(pl.multiple_of(col * kv_width, kv_width), kv_width)
    here = pl.ds(shifts * tokens, tokens)
    inputs = [
        pltpu.make_async_copy(segment_hbm, segment_ref, i_sem.at[5]),
        pltpu.make_async_copy(sink_hbm, sink_ref, i_sem.at[6]),
        pltpu.make_async_copy(ids_hbm, ids_ref, i_sem.at[7]),
        pltpu.make_async_copy(weight_hbm, weight_ref, i_sem.at[8]),
        pltpu.make_async_copy(key_ref.at[:, own_lanes], key_all.at[here], i_sem.at[0]),
        pltpu.make_async_copy(value_ref.at[:, own_lanes], value_all.at[here], i_sem.at[1]),
        pltpu.make_async_copy(query_hbm, query_ref, i_sem.at[2]),
        pltpu.make_async_copy(residual_hbm, residual_ref, i_sem.at[3]),
        pltpu.make_async_copy(gain_hbm, gain_ref.at[0], i_sem.at[4]),
    ]
    for load in inputs + out_loads:
        load.start()
    loads = [
        pltpu.make_async_copy(gate_up_hbm.at[0], gate_up, w_sem.at[0]),
        pltpu.make_async_copy(down_hbm.at[0], down, w_sem.at[1]),
    ]
    after = [{"row": lax.rem(row + shift, rows)} for shift in range(1, shifts + 1)]
    before = [{"row": lax.rem(row + rows - shift, rows)} for shift in range(1, shifts + 1)]
    follows = [row + shift < rows for shift in range(1, shifts + 1)]
    precedes = [row >= shift for shift in range(1, shifts + 1)]
    barrier = pltpu.get_barrier_semaphore()
    always = [sibling, partner] + ways
    for device in always:
        pl.semaphore_signal(barrier, inc=1, device_id=device, device_id_type=MESH)
    for exists, device in zip(follows + precedes, after + before):
        @pl.when(exists)
        def _(device=device):
            pl.semaphore_signal(barrier, inc=1, device_id=device, device_id_type=MESH)
    met = len(always)
    for exists in follows + precedes:
        met = met + exists.astype(jnp.int32)
    pl.semaphore_wait(barrier, met)
    halos = []
    for at in range(shifts):
        there = pl.ds((shifts - 1 - at) * tokens, tokens)
        halos.append([
            remote(src, dst, h_send.at[at, which], h_recv.at[at, which], after[at])
            for which, (src, dst) in enumerate([
                (segment_hbm, segment_all.at[at]),
                (key_ref.at[:, own_lanes], key_all.at[there]),
                (value_ref.at[:, own_lanes], value_all.at[there]),
            ])
        ])

        @pl.when(follows[at])
        def _(at=at):
            for halo in halos[at]:
                halo.start()

        @pl.when(jnp.logical_not(precedes[at]))
        def _(at=at, there=there):
            segment_all[at] = jnp.full((1, tokens), -1, jnp.int32)
            key_all[there, :] = jnp.zeros((tokens, kv_width), key_all.dtype)
            value_all[there, :] = jnp.zeros((tokens, kv_width), value_all.dtype)
    rest = key_all.shape[0] - (shifts + 1) * tokens
    for every in [key_all, value_all]:
        if rest:
            every[pl.ds((shifts + 1) * tokens, rest), :] = jnp.zeros((rest, kv_width), every.dtype)
    for load in inputs[:7]:
        load.wait()
    meta_ref[:TOP, :] = ids_ref[...].astype(jnp.float32)
    meta_ref[TOP:, :] = weight_ref[...]
    local_meta = pltpu.make_async_copy(meta_ref, metas.at[row], l_sem)
    local_meta.start()
    for at in range(shifts):
        @pl.when(precedes[at])
        def _(at=at):
            for halo in halos[at]:
                halo.wait_recv()
    for load in loads:
        load.start()
    attend_all(row, shifts, query_ref, key_all, value_all, segment_ref, segment_all, sink_ref, attended)

    first_rows = pl.ds(pl.multiple_of((1 - col) * 2 * size, 2 * size), 2 * size)
    early = []
    for at, (start, width) in enumerate(out_tiles):
        for load in out_loads[:chips] if at == 0 else [out_loads[chips - 1 + at]]:
            load.wait()
        lanes = pl.ds(start, width)
        rows_out = (
            mix[:, :, :depth].reshape(held, depth) if at == 0 else w_out[pl.ds(start - held, width), :]
        )
        partial_ref[:, lanes] = lax.dot_general(
            attended[...], rows_out, (((1,), (1,)), ((), ())), preferred_element_type=jnp.float32
        ).astype(jnp.bfloat16)
        early.append(remote(partial_ref.at[first_rows, lanes], part_in.at[first_rows, lanes], c_send.at[PIECES + at],
                            c_recv.at[PIECES + at], partner))
        early[-1].start()
    crosses = {}
    for index in [1, 0]:
        at = piece_rows(index, size)
        named = PIECES - 1 - index
        crosses[index] = remote(partial_ref.at[at], part_in.at[at], c_send.at[named],
                                c_recv.at[named], partner)
        crosses[index].start()
    for load in inputs[7:]:
        load.wait()
    for copy in early:
        copy.wait_recv()

    def ready(index):
        at = piece_rows(index, size)
        if index >= 2:
            remote(partial_ref.at[at], part_in.at[at], c_send.at[index], c_recv.at[index],
                   partner).wait_recv()
        summed = partial_ref[at, :].astype(jnp.float32) + part_in[at, :].astype(jnp.float32)
        total = (residual_ref[at, :].astype(jnp.float32) + summed).astype(jnp.bfloat16)
        stream[at, :] = total
        gathered[row, at, :] = normalize(total, gain_ref[...])

    def part(offset, index, which):
        return gathered.at[ring_row(place + offset, chips, which), piece_rows(index, size)]

    def offset_of(way, distance):
        return -distance if way == 0 else distance

    def hop(way, distance, index, sending):
        at = part(offset_of(way, distance - 1 if sending else distance), index, core)
        return remote(at, at, send.at[way, distance - 1, index], recv.at[way, distance - 1, index],
                      ways[way])

    def over(way, distance, sending):
        at = part(offset_of(way, distance), 0 if sending else PIECES - 1, core)
        return remote(at, at, over_send.at[way, distance - 1], over_recv.at[way, distance - 1],
                      partner)

    def pass_on(way, distance, index, which):
        at = part(offset_of(way, distance), index, which)
        return remote(at, at, sib_send.at[way, distance, index], sib_recv.at[way, distance, index],
                      sibling)

    def routing_hop(way, distance, sending):
        back = offset_of(way, distance - 1 if sending else distance)
        at = metas.at[ring_row(place + back, chips, core)]
        return remote(at, at, m_send.at[way, distance - 1], m_recv.at[way, distance - 1], ways[way])

    def routing_on(way, distance, which):
        at = metas.at[ring_row(place + offset_of(way, distance), chips, which)]
        return remote(at, at, n_send.at[way, distance], n_recv.at[way, distance], sibling)

    sent = []

    def go(copy):
        copy.start()
        sent.append(copy)

    reach = [half_way, half_way - 1]
    theirs = gathered.at[other]

    def offsets(distances):
        return [
            offset for distance in distances for offset in sorted({distance, (chips - distance) % chips})
        ]

    def blocks_of(distances):
        return [(offset, which) for offset in offsets(distances) for which in range(2)]

    def first_slot(distance):
        return cap * len(blocks_of(range(distance)))

    def wait_for(distances):
        for distance in distances:
            if distance == 0:
                remote(theirs, theirs, x_sem.at[0], x_sem.at[1], sibling).wait_recv()
                routing_on(0, 0, 1 - core).wait_recv()
                continue
            for way in range(2):
                if distance <= reach[way]:
                    routing_on(way, distance, 1 - core).wait_recv()
                indices = list(ring_pieces(distance, half_way, way))
                for index in indices + ([PIECES - 1] if distance < half_way else []):
                    pass_on(way, distance, index, 1 - core).wait_recv()

    def pack(distance):
        blocks = blocks_of([distance])
        not_after = lax.broadcasted_iota(jnp.int32, (tokens, tokens), 0) <= lax.broadcasted_iota(
            jnp.int32, (tokens, tokens), 1
        )
        not_after = jnp.where(not_after, 1.0, 0.0).astype(jnp.bfloat16)
        numbers = lax.broadcasted_iota(jnp.int32, (cap, tokens), 0).astype(jnp.float32)
        named, weights = [], []
        wanted = [(offset, which, row) for offset, which in blocks]
        wanted += [(offset, 0, other) for offset, which in blocks if which == 0]
        for offset, which, expert in wanted:
            meta = metas[ring_row(place + offset, chips, core if which == 0 else 1 - core)]
            hit = jnp.where(meta[:TOP] == expert.astype(jnp.float32), 1.0, 0.0)
            named.append(jnp.max(hit, axis=0, keepdims=True))
            weights.append(jnp.sum(hit * meta[TOP:], axis=0, keepdims=True))
        hits = jnp.concatenate(named, 0)
        order = jnp.dot(hits.astype(jnp.bfloat16), not_after, preferred_element_type=jnp.float32)
        chosen = [
            jnp.where(order[at:at + 1] == numbers + 1.0, 1.0, 0.0) * named[at]
            for at in range(len(wanted))
        ]
        for at, (offset, which) in enumerate(blocks):
            here = pl.ds(first_slot(distance) + at * cap, cap)
            weight = jnp.sum(chosen[at] * weights[at], axis=1, keepdims=True)
            slot_weight[here, :] = jnp.broadcast_to(weight, (cap, slot_weight.shape[1]))
            source = ring_row(place + offset, chips, core if which == 0 else 1 - core)
            packed[here, :] = jnp.dot(
                chosen[at].astype(jnp.bfloat16), gathered[source],
                preferred_element_type=jnp.float32,
            ).astype(jnp.bfloat16)
        for at, (offset, which) in enumerate(blocks[::2]):
            both = jnp.concatenate([chosen[2 * at], chosen[len(blocks) + at]], 0)
            select[offset] = both.T.astype(jnp.bfloat16)

    def gate_and_up(distances, start, width):
        count = cap * len(blocks_of(distances))
        values = packed[pl.ds(first_slot(distances[0]), count), :]
        lanes = pl.ds(start, width)
        last = (((1,), (1,)), ((), ()))
        gate = lax.dot_general(values, gate_up[0, lanes, :], last, preferred_element_type=jnp.float32)
        up = lax.dot_general(values, gate_up[1, lanes, :], last, preferred_element_type=jnp.float32)
        active[:count, lanes] = ((up + 1.0) * gate * jax.nn.sigmoid(1.702 * gate)).astype(jnp.bfloat16)

    def go_down(distances, first, last, start, width):
        blocks = blocks_of(distances)[first:last]
        lanes = pl.ds(start, width)
        count = (last - first) * cap
        result = jnp.dot(
            active[pl.ds(first * cap, count), :], down[:, lanes], preferred_element_type=jnp.float32
        )
        scale = slot_weight[pl.ds(first_slot(distances[0]) + first * cap, count), :1]
        result = (result * scale).astype(jnp.bfloat16)
        for at, (offset, which) in enumerate(blocks):
            piece = result[at * cap:(at + 1) * cap]
            if which == 0:
                slots[offset, :cap, lanes] = piece
            else:
                sib_slots[offset, :, lanes] = piece

    def slot_copy(offset):
        return remote(sib_slots.at[offset], slots.at[offset, pl.ds(cap, cap)], slot_sem.at[0, offset],
                      slot_sem.at[1, offset], sibling)

    queue = []

    def work(budget):
        while queue and budget > 0:
            cost, step = queue.pop(0)
            step()
            budget -= cost

    def enqueue_pack(distance):
        queue.append((0.1, lambda: wait_for([distance])))
        queue.append((0.5, lambda: pack(distance)))

    def enqueue_products(distances, last_first):
        if distances[0] == 0:
            queue.append((0.0, lambda: loads[0].wait()))
        for start, width in tiles(gate_up.shape[1], 256):
            queue.append((1.0, lambda start=start, width=width: gate_and_up(distances, start, width)))
        if distances[0] == 0:
            queue.append((0.0, lambda: loads[1].wait()))
        count = len(blocks_of(distances))
        split = count - len(blocks_of(distances[-1:]))
        for begin, end in ((split, count), (0, split)) if last_first else ((0, count),):
            for start, width in tiles(down.shape[1], 512):
                queue.append((0.4, lambda start=start, width=width, begin=begin, end=end: go_down(
                    distances, begin, end, start, width)))
            queue.append((0.2, lambda begin=begin, end=end: [
                go(slot_copy(offset)) for offset in offsets(distances)[begin // 2:end // 2]]))

    near, mid = half_way // 4, half_way // 2
    batches = [range(near + 1), range(near + 1, mid + 1), range(mid + 1, half_way + 1)]
    for index in [0, 1, 2]:
        ready(index)
        for way in range(2):
            if index in ring_pieces(1, half_way, way):
                go(hop(way, 1, index, True))
    ready(PIECES - 1)
    local_meta.wait()
    for way in range(2):
        go(routing_hop(way, 1, True))
    go(routing_on(0, 0, core))
    mine = gathered.at[row]
    go(remote(mine, mine, x_sem.at[0], x_sem.at[1], sibling))

    def take_over(distance):
        for way in range(2):
            over(way, distance, False).wait_recv()
            if distance + 1 == half_way and way == 1:
                go(hop(way, half_way, PIECES - 1, True))
            go(pass_on(way, distance, PIECES - 1, core))

    for distance in range(1, half_way + 1):
        for step, index in enumerate([0, 1, 2] if distance < half_way else [0, 2, 1, 3]):
            for way in range(2):
                if index not in ring_pieces(distance, half_way, way):
                    continue
                hop(way, distance, index, False).wait_recv()
                if distance < half_way and index in ring_pieces(distance + 1, half_way, way):
                    go(hop(way, distance + 1, index, True))
                if index == 0 and distance < half_way:
                    go(over(way, distance, True))
                go(pass_on(way, distance, index, core))
            if step == 0:
                enqueue_pack(distance - 1)
                for batch in batches[:-1]:
                    if batch[-1] == distance - 1:
                        enqueue_products(batch, False)
            work(BUDGET)
        for way in range(2):
            if distance <= reach[way]:
                routing_hop(way, distance, False).wait_recv()
                if distance < reach[way]:
                    go(routing_hop(way, distance + 1, True))
                go(routing_on(way, distance, core))
        if distance < half_way:
            take_over(distance)
    enqueue_pack(half_way)
    enqueue_products(batches[-1], True)
    work(100)

    def combine(offset):
        slot_copy(offset).wait_recv()
        mix[offset] = jnp.dot(
            select[offset], slots[offset], preferred_element_type=jnp.float32
        ).astype(jnp.bfloat16)

    def fold_hop(way, distance, index):
        at = pl.ds(index % (PIECES - 1) * size, size)
        return remote(ring_out.at[way, distance - 1, at], ring_in.at[way, distance - 1, at],
                      f_send.at[way, distance - 1, index], f_recv.at[way, distance - 1, index],
                      ways[way])

    def arrived(way, distance, index):
        fold_hop(way, distance, index).wait_recv()
        return ring_in[way, distance - 1, pl.ds(index % (PIECES - 1) * size, size), :].astype(jnp.float32)

    def fold_over(offset):
        return remote(mix.at[offset, piece_rows(PIECES - 1, size)], over_in.at[offset],
                      fo_send.at[offset], fo_recv.at[offset], partner)

    def fold_step(way, distance, index):
        offset = distance if way == 0 else chips - distance
        at = piece_rows(index, size)
        value = mix[offset, at, :].astype(jnp.float32)
        if distance < half_way and index in ring_pieces(distance + 1, half_way, way):
            value = value + arrived(way, distance + 1, index)
        if distance < half_way and index == PIECES - 1:
            mix[offset, at, :] = value.astype(jnp.bfloat16)
            go(fold_over(offset))
            return
        if index == 0 and distance < half_way:
            fold_over(offset).wait_recv()
            value = value + over_in[offset].astype(jnp.float32)
        ring_out[way, distance - 1, pl.ds(index % (PIECES - 1) * size, size), :] = value.astype(
            jnp.bfloat16
        )
        go(fold_hop(way, distance, index))

    for distance in range(half_way, 0, -1):
        for offset in offsets([distance]):
            combine(offset)
        if distance == half_way:
            steps = [(1, 3), (0, 1), (1, 2), (0, 0)]
        elif distance == half_way - 1:
            steps = [(0, 3), (0, 2), (1, 1), (1, 3), (0, 1), (1, 2), (0, 0), (1, 0)]
        else:
            steps = [(0, 3), (1, 3), (0, 1), (1, 1), (0, 2), (1, 2), (0, 0), (1, 0)]
        for way, index in steps:
            fold_step(way, distance, index)
    combine(0)
    width = out_hbm.shape[1]
    for index in [3, 1, 2, 0]:
        at = piece_rows(index, size)
        value = mix[0, at, :].astype(jnp.float32)
        for way in range(2):
            if index in ring_pieces(1, half_way, way):
                value = value + arrived(way, 1, index)
        low, high = value[:, :width], value[:, width:]
        x_out[at, :] = jnp.where(col == 0, high, low).astype(jnp.bfloat16)
        go(remote(x_out.at[at], x_in.at[at], fx_sem.at[0, index], fx_sem.at[1, index], partner))
        base = stream[at, :].astype(jnp.float32)
        out_ref[at, :] = jnp.where(col == 0, low, high) + jnp.where(
            col == 0, base[:, :width], base[:, width:]
        )
    results = []
    for index in [0, 2, 1, 3]:
        at = piece_rows(index, size)
        named = PIECES - 1 - index
        remote(x_out.at[at], x_in.at[at], fx_sem.at[0, named], fx_sem.at[1, named],
               partner).wait_recv()
        out_ref[at, :] = out_ref[at, :] + x_in[at, :].astype(jnp.float32)
        results.append(pltpu.make_async_copy(out_ref.at[at], out_hbm.at[at], y_sem.at[index]))
        results[-1].start()
    for copy in results:
        copy.wait()
    for copy in early + list(crosses.values()) + sent:
        copy.wait_send()
    for at in range(shifts):
        @pl.when(follows[at])
        def _(at=at):
            for halo in halos[at]:
                halo.wait_send()


def layer(residual, queries, keys, values, segments, sinks, w_out, gain, expert_ids, route_weight, w_gate_up,
          w_down, rows, cap, shifts, kv_width, width):
    w_gate_up = jnp.swapaxes(w_gate_up, 2, 3)
    w_out = w_out.T
    half_way = rows // 4
    chips = rows // 2
    tokens, features = residual.shape
    hidden = w_gate_up.shape[2]
    near, mid = half_way // 4, half_way // 2
    most = cap * 2 * max(2 * near + 1, 2 * (mid - near), 2 * (half_way - mid) - 1)
    key_rows = -(-(shifts + 1) * tokens // 128) * 128
    out_tiles = len(tiles(features, chips * tokens))
    meta = (2 * TOP, tokens)
    bf16, f32, dma = jnp.bfloat16, jnp.float32, pltpu.SemaphoreType.DMA
    hbm = pl.BlockSpec(memory_space=pl.ANY)
    return pl.pallas_call(
        lambda *refs: expert_kernel(rows, cap, shifts, *refs),
        out_shape=jax.ShapeDtypeStruct((tokens, width), f32),
        in_specs=[hbm] * 12,
        out_specs=hbm,
        scratch_shapes=[
            pltpu.VMEM((tokens, features), bf16),
            pltpu.VMEM(queries.shape, bf16),
            pltpu.VMEM((1, features), f32),
            pltpu.VMEM((1, tokens), jnp.int32),
            pltpu.SMEM((1, sinks.shape[0]), f32),
            pltpu.VMEM((TOP, tokens), jnp.int32),
            pltpu.VMEM((TOP, tokens), f32),
            pltpu.VMEM((tokens, width), f32),
            dma((PIECES,)),
            dma((9,)),
            pltpu.VMEM((features - chips * tokens, w_out.shape[1]), bf16),
            pltpu.VMEM((key_rows, kv_width), bf16),
            pltpu.VMEM((key_rows, kv_width), bf16),
            pltpu.VMEM((shifts, 1, tokens), jnp.int32),
            pltpu.VMEM(queries.shape, bf16),
            pltpu.VMEM((tokens, features), bf16),
            pltpu.VMEM(meta, f32),
            pltpu.VMEM(w_gate_up.shape[1:], bf16),
            pltpu.VMEM(w_down.shape[1:], bf16),
            pltpu.VMEM((rows, tokens, features), bf16),
            pltpu.VMEM((rows, *meta), f32),
            pltpu.VMEM((tokens, features), bf16),
            pltpu.VMEM((tokens, features), bf16),
            pltpu.VMEM((rows * cap, features), bf16),
            pltpu.VMEM((most, hidden), bf16),
            pltpu.VMEM((rows * cap, 128), f32),
            pltpu.VMEM((chips, tokens, 2 * cap), bf16),
            pltpu.VMEM((chips, 2 * cap, features), bf16),
            pltpu.VMEM((chips, cap, features), bf16),
            pltpu.VMEM((chips, tokens, features), bf16),
            pltpu.VMEM((2, half_way, tokens // PIECES * (PIECES - 1), features), bf16),
            pltpu.VMEM((2, half_way, tokens // PIECES * (PIECES - 1), features), bf16),
            pltpu.VMEM((chips, tokens // PIECES, features), bf16),
            pltpu.VMEM((tokens, width), bf16),
            pltpu.VMEM((tokens, width), bf16),
            dma((out_tiles + chips,)),
            dma((shifts, 3)),
            dma((shifts, 3)),
            dma((2,)),
            dma((2,)),
            dma((PIECES + out_tiles,)),
            dma((PIECES + out_tiles,)),
            dma((2, half_way)),
            dma((2, half_way)),
            dma((2, half_way + 1)),
            dma((2, half_way + 1)),
            dma,
            dma((2, half_way, PIECES)),
            dma((2, half_way, PIECES)),
            dma((2, half_way)),
            dma((2, half_way)),
            dma((2, half_way + 1, PIECES)),
            dma((2, half_way + 1, PIECES)),
            dma((2, chips)),
            dma((2, half_way, PIECES)),
            dma((2, half_way, PIECES)),
            dma((chips,)),
            dma((chips,)),
            dma((2, PIECES)),
        ],
        compiler_params=pltpu.CompilerParams(
            collective_id=2, has_side_effects=True, vmem_limit_bytes=VMEM_BYTES
        ),
        name="layer",
    )(residual, queries, keys, values, segments.reshape(1, -1), sinks.reshape(1, -1), gain,
      expert_ids.T, route_weight.T, w_out, w_gate_up, w_down).astype(bf16)


def local(
    residual,
    query_states,
    key_states,
    value_states,
    segment_ids,
    sink_logits,
    w_out,
    norm_gain,
    expert_ids,
    route_weight,
    w_gate_up,
    w_down,
):
    tok_rows = query_states.shape[0]
    row_count = lax.axis_size("row")
    col_count = lax.axis_size("col")
    row_index = lax.axis_index("row")
    col_index = lax.axis_index("col")
    local_heads = sink_logits.shape[0]
    group_size = HEADS // KV_HEADS
    if local_heads >= group_size:
        kv_count = local_heads // group_size
        kv_first = col_index * kv_count
    else:
        kv_count = 1
        kv_first = col_index * local_heads // group_size
    kv_width = kv_count * HEAD_DIM
    own_keys = lax.dynamic_slice_in_dim(key_states, kv_first * HEAD_DIM, kv_width, 1)
    own_values = lax.dynamic_slice_in_dim(value_states, kv_first * HEAD_DIM, kv_width, 1)
    shift_count = (WINDOW + tok_rows - 2) // tok_rows
    block_bytes = 2 * residual.shape[0] * residual.shape[1]
    experts_all = w_gate_up.shape[0] * row_count
    slot_cap = max(2, 2 * TOP * tok_rows // experts_all)
    weight_bytes = 2 * (w_out.size + w_gate_up.size + w_down.size)
    in_kernels = (
        col_count == 2 and row_count % 4 == 0 and row_count >= 8 and tok_rows % 64 == 0
        and kv_width % 128 == 0 and kv_width * col_count == key_states.shape[1]
        and row_count // 2 * tok_rows < residual.shape[1] and w_out.shape[0] <= residual.shape[1]
        and slot_cap % 16 == 0 and 2 * slot_cap == tok_rows and 2 * HEAD_DIM == 128
        and local_heads % (2 * kv_count) == 0 and weight_bytes + 3 * row_count * block_bytes < VMEM_BYTES
    )
    feature_count = residual.shape[1] // col_count
    if in_kernels:
        return layer(
            residual, query_states, key_states, value_states, segment_ids, sink_logits, w_out, norm_gain,
            expert_ids, route_weight, w_gate_up, w_down, row_count, slot_cap, shift_count, kv_width,
            feature_count,
        )
    routing = jnp.concatenate([expert_ids.astype(jnp.float32), route_weight], 1).T
    key_parts = []
    value_parts = []
    segment_parts = []
    start_parts = []
    for offset in range(shift_count, 0, -1):
        arrived = shifted((own_keys, own_values, segment_ids), "row", offset)
        key_parts.append(arrived[0])
        value_parts.append(arrived[1])
        segment_parts.append(arrived[2])
        start_parts.append((row_index - offset) * tok_rows)
    key_parts.append(own_keys)
    value_parts.append(own_values)
    segment_parts.append(segment_ids)
    start_parts.append(row_index * tok_rows)
    key_groups = jnp.concatenate(key_parts, 0).reshape(-1, kv_count, HEAD_DIM)
    value_groups = jnp.concatenate(value_parts, 0).reshape(-1, kv_count, HEAD_DIM)
    key_segments = jnp.concatenate(segment_parts, 0)
    positions = jnp.arange(tok_rows, dtype=jnp.int32)
    key_position = jnp.concatenate([start + positions for start in start_parts], 0)
    query_position = row_index * tok_rows + positions
    allowed = (key_position[None, :] >= 0) & (key_position[None, :] <= query_position[:, None])
    allowed = allowed & (key_position[None, :] > query_position[:, None] - WINDOW)
    allowed = allowed & (key_segments[None, :] == segment_ids[:, None])
    query_groups = query_states.reshape(tok_rows, kv_count, local_heads // kv_count, HEAD_DIM)
    sink_groups = sink_logits.reshape(kv_count, local_heads // kv_count, 1, 1)
    attended = attend(query_groups, key_groups, value_groups, allowed, sink_groups).reshape(
        tok_rows, local_heads * HEAD_DIM
    )
    partial_value = jnp.dot(attended, w_out, preferred_element_type=jnp.float32)
    expert_gate_up = w_gate_up[0]
    expert_down = w_down[0]
    partial_value = partial_value.astype(jnp.bfloat16)
    summed = lax.psum(partial_value, "col").astype(jnp.float32)
    stream = (residual.astype(jnp.float32) + summed).astype(jnp.bfloat16)
    gathered = lax.all_gather(normalize(stream, norm_gain), "row", axis=0, tiled=False)
    routing = lax.all_gather(routing, "row", axis=0, tiled=False)
    stream_part = lax.dynamic_slice_in_dim(stream, col_index * feature_count, feature_count, 1)
    names_mine = routing[:, :TOP] == row_index.astype(jnp.float32)
    mine = jnp.any(names_mine, axis=1)
    weight = jnp.sum(jnp.where(names_mine, routing[:, TOP:], 0.0), axis=1)
    token_order = jnp.arange(tok_rows, dtype=jnp.int32)
    not_after = (token_order[:, None] <= token_order[None, :]).astype(jnp.bfloat16)
    slot_of = jnp.dot(
        mine.astype(jnp.bfloat16), not_after, preferred_element_type=jnp.float32
    ).astype(jnp.int32) - 1
    slots = jnp.arange(slot_cap, dtype=jnp.int32)
    chosen = mine[:, None, :] & (slot_of[:, None, :] == slots[None, :, None])
    selector = chosen.astype(jnp.bfloat16)
    combine = jnp.where(chosen, weight[:, None, :], 0.0)
    packed = jnp.einsum(
        "nst,ntd->nsd", selector, gathered, preferred_element_type=jnp.float32
    ).astype(jnp.bfloat16).reshape(row_count * slot_cap, -1)
    gate = jnp.dot(packed, expert_gate_up[0], preferred_element_type=jnp.float32)
    up = jnp.dot(packed, expert_gate_up[1], preferred_element_type=jnp.float32)
    active = ((up + 1.0) * gate * jax.nn.sigmoid(1.702 * gate)).astype(jnp.bfloat16)
    expert_partial = jnp.dot(active, expert_down, preferred_element_type=jnp.float32)
    scaled = expert_partial.reshape(row_count, slot_cap, -1) * jnp.sum(combine, 2)[:, :, None]
    mixed = jnp.einsum(
        "nst,nsd->ntd", selector, scaled.astype(jnp.bfloat16), preferred_element_type=jnp.float32
    ).astype(jnp.bfloat16)
    mixed = mixed.reshape(row_count * tok_rows, -1)
    mixed = lax.psum_scatter(mixed, "row", scatter_dimension=0, tiled=True)
    mixed = lax.psum_scatter(mixed, "col", scatter_dimension=1, tiled=True)
    return (stream_part.astype(jnp.float32) + mixed.astype(jnp.float32)).astype(jnp.bfloat16)


def solution(mesh):
    in_specs = (
        P("row", None),
        P("row", "col"),
        P("row", None),
        P("row", None),
        P("row"),
        P("col"),
        P("col", None),
        P(),
        P("row", None),
        P("row", None),
        P("row", None, None, "col"),
        P("row", "col", None),
    )
    out_specs = P("row", "col")
    return jax.shard_map(local, mesh=mesh, in_specs=in_specs, out_specs=out_specs, check_vma=False)
```

```python
import jax
import jax.numpy as jnp
from jax import lax
from jax.experimental import pallas as pl
from jax.experimental.pallas import tpu as pltpu
from jax.sharding import PartitionSpec as P

HEADS = 64
KV_HEADS = 8
HEAD_DIM = 64
WINDOW = 128
TOP = 4


epsilon = 1e-05
masked_score = -1e30


def shifted(shard, axis, by):
    size = lax.axis_size(axis)
    pairs = [(i, i + by) for i in range(size) if 0 <= i + by < size]
    return lax.ppermute(shard, axis, pairs)


def normalize(stream_rows, norm_gain):
    values32 = stream_rows.astype(jnp.float32)
    square_mean = jnp.mean(values32 * values32, axis=-1, keepdims=True)
    return (values32 * lax.rsqrt(square_mean + epsilon) * norm_gain).astype(jnp.bfloat16)


def attend(query_groups, key_groups, value_groups, allowed, sink_groups):
    scores = jnp.einsum(
        "tgjd,lgd->gjtl", query_groups, key_groups, preferred_element_type=jnp.float32
    )
    scores = scores * query_groups.shape[-1] ** (-0.5)
    scores = jnp.where(allowed[None, None], scores, masked_score)
    peak_score = jnp.maximum(jnp.max(scores, axis=-1, keepdims=True), sink_groups)
    numerator = jnp.exp(scores - peak_score)
    denominator = jnp.exp(sink_groups - peak_score) + jnp.sum(numerator, axis=-1, keepdims=True)
    weights = (numerator / denominator).astype(jnp.bfloat16)
    return jnp.einsum(
        "gjtl,lgd->tgjd", weights, value_groups, preferred_element_type=jnp.float32
    ).astype(jnp.bfloat16)


MESH = pl.DeviceIdType.MESH
VMEM = pl.BlockSpec(memory_space=pltpu.VMEM)
PIECES = 4
VMEM_BYTES = 61 * 1024 * 1024


def ring_place(row, chips):
    chip = lax.div(row, 2)
    along = lax.div(chip, 2)
    return jnp.where(lax.rem(chip, 2) == 0, along, chips - 1 - along)


def ring_row(place, chips, core):
    place = lax.rem(place + chips, chips)
    chip = jnp.where(place < chips // 2, 2 * place, 2 * (chips - 1 - place) + 1)
    return 2 * chip + core


def remote(src, dst, send, recv, device):
    return pltpu.make_async_remote_copy(
        src_ref=src, dst_ref=dst, send_sem=send, recv_sem=recv, device_id=device,
        device_id_type=MESH,
    )


def ring_pieces(distance, half_way, way):
    if distance < half_way:
        return [0, 1, 2]
    return [0, 1] if way == 0 else [2, 3]


def piece_rows(index, size):
    col = lax.axis_index("col")
    start = (index + col * (PIECES - 1 - 2 * index)) * size
    return pl.ds(pl.multiple_of(start, size), size)


BUDGET = 2.0


def attend_all(row, shifts, query_ref, key_all, value_all, segment_ref, segment_all, sink_ref, attended):
    tokens = query_ref.shape[0]
    keys = key_all.shape[0]
    groups = key_all.shape[1] // HEAD_DIM
    heads = sink_ref.shape[1] // groups
    pairs = heads // 2
    lanes = 2 * HEAD_DIM
    segments = [segment_all[at] for at in range(shifts - 1, -1, -1)] + [segment_ref[...]]
    rest = keys - (shifts + 1) * tokens
    if rest:
        segments.append(jnp.full((1, rest), -1, jnp.int32))
    key_segment = jnp.concatenate(segments, 1).astype(jnp.float32)
    diagonal = lax.broadcasted_iota(jnp.int32, (tokens, tokens), 0) == lax.broadcasted_iota(
        jnp.int32, (tokens, tokens), 1
    )
    query_segment = jnp.sum(
        jnp.where(diagonal, segment_ref[...].astype(jnp.float32), 0.0), axis=1, keepdims=True
    )
    query_at = shifts * tokens + lax.broadcasted_iota(jnp.int32, (tokens, keys), 0)
    key_at = lax.broadcasted_iota(jnp.int32, (tokens, keys), 1)
    allowed = (key_at <= query_at) & (key_at > query_at - WINDOW) & (key_at + row * tokens >= shifts * tokens)
    allowed = allowed & (key_segment == query_segment)
    bias = jnp.where(allowed, 0.0, masked_score)
    bias = jnp.concatenate([bias] * pairs, 0).T
    values_turned = value_all[...].astype(jnp.float32).T.astype(jnp.bfloat16)
    lower = lax.broadcasted_iota(jnp.int32, (keys, lanes), 1) < HEAD_DIM
    pair_of = lax.broadcasted_iota(jnp.int32, (1, pairs * tokens), 1)
    nothing = jnp.zeros((HEAD_DIM, keys), jnp.bfloat16)
    for group in range(groups):
        tile = group // 2 * lanes
        straight = key_all[:, tile:tile + lanes]
        turned = jnp.concatenate([straight[:, HEAD_DIM:], straight[:, :HEAD_DIM]], 1)
        first, second = (straight, turned) if group % 2 == 0 else (turned, straight)
        zero = jnp.zeros_like(straight)
        both_keys = jnp.concatenate([jnp.where(lower, first, zero), jnp.where(lower, zero, second)], 0)
        value = values_turned[group * HEAD_DIM:(group + 1) * HEAD_DIM]
        both_values = jnp.concatenate(
            [jnp.concatenate([value, nothing], 1), jnp.concatenate([nothing, value], 1)], 0
        )
        first_lane = group * heads * HEAD_DIM
        queries = jnp.concatenate(
            [query_ref[:, first_lane + pair * lanes:first_lane + (pair + 1) * lanes] for pair in range(pairs)], 0
        )
        scores = lax.dot_general(
            both_keys, queries, (((1,), (1,)), ((), ())), preferred_element_type=jnp.float32
        )
        halves = []
        for half in range(2):
            sink = jnp.full(pair_of.shape, sink_ref[0, group * heads + half])
            for pair in range(1, pairs):
                sink = jnp.where(
                    pair_of >= pair * tokens, sink_ref[0, group * heads + 2 * pair + half], sink
                )
            block = scores[half * keys:(half + 1) * keys] * HEAD_DIM ** (-0.5) + bias
            peak = jnp.maximum(jnp.max(block, axis=0, keepdims=True), sink)
            numerator = jnp.exp(block - peak)
            denominator = jnp.exp(sink - peak) + jnp.sum(numerator, axis=0, keepdims=True)
            halves.append((numerator * (1.0 / denominator)).astype(jnp.bfloat16))
        mixed = jnp.dot(
            both_values, jnp.concatenate(halves, 0), preferred_element_type=jnp.float32
        ).T.astype(jnp.bfloat16)
        for pair in range(pairs):
            attended[:, first_lane + pair * lanes:first_lane + (pair + 1) * lanes] = mixed[
                pair * tokens:(pair + 1) * tokens
            ]


def tiles(total, step):
    return [(start, min(step, total - start)) for start in range(0, total, step)]


def expert_kernel(rows, cap, shifts, residual_hbm, query_hbm, key_ref, value_ref, segment_hbm, sink_hbm, gain_hbm,
                  ids_hbm, weight_hbm, w_out_hbm, gate_up_hbm, down_hbm, out_hbm,
                  residual_ref, query_ref, gain_ref, segment_ref, sink_ref, ids_ref, weight_ref, out_ref, result, y_sem,
                  i_sem, w_out, key_all, value_all, segment_all, attended, partial_ref, meta_ref,
                  gate_up, down, gathered, metas, part_in, stream, packed, active, slot_weight, select,
                  slots, sib_slots, mix, ring_in, ring_out, over_in, x_out, x_in,
                  o_sem, h_send, h_recv, w_sem, x_sem, c_send, c_recv, m_send, m_recv, n_send, n_recv, l_sem, send, recv,
                  over_send, over_recv, sib_send, sib_recv, slot_sem, f_send, f_recv, fo_send, fo_recv, fx_sem):
    chips = rows // 2
    half_way = chips // 2
    row = lax.axis_index("row")
    col = lax.axis_index("col")
    core = lax.rem(row, 2)
    place = ring_place(row, chips)
    other = row + 1 - 2 * core
    sibling = {"row": other}
    partner = {"col": 1 - col}
    ways = [{"row": ring_row(place + 1, chips, core)}, {"row": ring_row(place - 1, chips, core)}]
    tokens, features = residual_ref.shape
    size = tokens // PIECES
    held = chips * tokens
    depth = w_out.shape[1]
    out_tiles = tiles(features, held)
    out_loads = [
        pltpu.make_async_copy(
            w_out_hbm.at[pl.ds(at * tokens, tokens)], mix.at[at, :, pl.ds(0, depth)],
            o_sem.at[len(out_tiles) + at],
        )
        for at in range(chips)
    ] + [
        pltpu.make_async_copy(w_out_hbm.at[pl.ds(start, width)], w_out.at[pl.ds(start - held, width)], o_sem.at[at])
        for at, (start, width) in enumerate(out_tiles) if at
    ]
    kv_width = key_all.shape[1]
    own_lanes = pl.ds(pl.multiple_of(col * kv_width, kv_width), kv_width)
    here = pl.ds(shifts * tokens, tokens)
    inputs = [
        pltpu.make_async_copy(segment_hbm, segment_ref, i_sem.at[5]),
        pltpu.make_async_copy(sink_hbm, sink_ref, i_sem.at[6]),
        pltpu.make_async_copy(ids_hbm, ids_ref, i_sem.at[7]),
        pltpu.make_async_copy(weight_hbm, weight_ref, i_sem.at[8]),
        pltpu.make_async_copy(key_ref.at[:, own_lanes], key_all.at[here], i_sem.at[0]),
        pltpu.make_async_copy(value_ref.at[:, own_lanes], value_all.at[here], i_sem.at[1]),
        pltpu.make_async_copy(query_hbm, query_ref, i_sem.at[2]),
        pltpu.make_async_copy(residual_hbm, residual_ref, i_sem.at[3]),
        pltpu.make_async_copy(gain_hbm, gain_ref.at[0], i_sem.at[4]),
    ]
    for load in inputs + out_loads:
        load.start()
    loads = [
        pltpu.make_async_copy(gate_up_hbm.at[0], gate_up, w_sem.at[0]),
        pltpu.make_async_copy(down_hbm.at[0], down, w_sem.at[1]),
    ]
    after = [{"row": lax.rem(row + shift, rows)} for shift in range(1, shifts + 1)]
    before = [{"row": lax.rem(row + rows - shift, rows)} for shift in range(1, shifts + 1)]
    follows = [row + shift < rows for shift in range(1, shifts + 1)]
    precedes = [row >= shift for shift in range(1, shifts + 1)]
    barrier = pltpu.get_barrier_semaphore()
    always = [sibling, partner] + ways
    for device in always:
        pl.semaphore_signal(barrier, inc=1, device_id=device, device_id_type=MESH)
    for exists, device in zip(follows + precedes, after + before):
        @pl.when(exists)
        def _(device=device):
            pl.semaphore_signal(barrier, inc=1, device_id=device, device_id_type=MESH)
    met = len(always)
    for exists in follows + precedes:
        met = met + exists.astype(jnp.int32)
    pl.semaphore_wait(barrier, met)
    halos = []
    for at in range(shifts):
        there = pl.ds((shifts - 1 - at) * tokens, tokens)
        halos.append([
            remote(src, dst, h_send.at[at, which], h_recv.at[at, which], after[at])
            for which, (src, dst) in enumerate([
                (segment_hbm, segment_all.at[at]),
                (key_ref.at[:, own_lanes], key_all.at[there]),
                (value_ref.at[:, own_lanes], value_all.at[there]),
            ])
        ])

        @pl.when(follows[at])
        def _(at=at):
            for halo in halos[at]:
                halo.start()

        @pl.when(jnp.logical_not(precedes[at]))
        def _(at=at, there=there):
            segment_all[at] = jnp.full((1, tokens), -1, jnp.int32)
            key_all[there, :] = jnp.zeros((tokens, kv_width), key_all.dtype)
            value_all[there, :] = jnp.zeros((tokens, kv_width), value_all.dtype)
    rest = key_all.shape[0] - (shifts + 1) * tokens
    for every in [key_all, value_all]:
        if rest:
            every[pl.ds((shifts + 1) * tokens, rest), :] = jnp.zeros((rest, kv_width), every.dtype)
    for load in inputs[:7]:
        load.wait()
    meta_ref[:TOP, :] = ids_ref[...].astype(jnp.float32)
    meta_ref[TOP:, :] = weight_ref[...]
    local_meta = pltpu.make_async_copy(meta_ref, metas.at[row], l_sem)
    local_meta.start()
    for at in range(shifts):
        @pl.when(precedes[at])
        def _(at=at):
            for halo in halos[at]:
                halo.wait_recv()
    for load in loads:
        load.start()
    attend_all(row, shifts, query_ref, key_all, value_all, segment_ref, segment_all, sink_ref, attended)

    first_rows = pl.ds(pl.multiple_of((1 - col) * 2 * size, 2 * size), 2 * size)
    early = []
    for at, (start, width) in enumerate(out_tiles):
        for load in out_loads[:chips] if at == 0 else [out_loads[chips - 1 + at]]:
            load.wait()
        lanes = pl.ds(start, width)
        rows_out = (
            mix[:, :, :depth].reshape(held, depth) if at == 0 else w_out[pl.ds(start - held, width), :]
        )
        partial_ref[:, lanes] = lax.dot_general(
            attended[...], rows_out, (((1,), (1,)), ((), ())), preferred_element_type=jnp.float32
        ).astype(jnp.bfloat16)
        early.append(remote(partial_ref.at[first_rows, lanes], part_in.at[first_rows, lanes], c_send.at[PIECES + at],
                            c_recv.at[PIECES + at], partner))
        early[-1].start()
    crosses = {}
    for index in [1, 0]:
        at = piece_rows(index, size)
        named = PIECES - 1 - index
        crosses[index] = remote(partial_ref.at[at], part_in.at[at], c_send.at[named],
                                c_recv.at[named], partner)
        crosses[index].start()
    for load in inputs[7:]:
        load.wait()
    for copy in early:
        copy.wait_recv()

    def ready(index):
        at = piece_rows(index, size)
        if index >= 2:
            remote(partial_ref.at[at], part_in.at[at], c_send.at[index], c_recv.at[index],
                   partner).wait_recv()
        summed = partial_ref[at, :].astype(jnp.float32) + part_in[at, :].astype(jnp.float32)
        total = (residual_ref[at, :].astype(jnp.float32) + summed).astype(jnp.bfloat16)
        stream[at, :] = total
        gathered[row, at, :] = normalize(total, gain_ref[...])

    def part(offset, index, which):
        return gathered.at[ring_row(place + offset, chips, which), piece_rows(index, size)]

    def offset_of(way, distance):
        return -distance if way == 0 else distance

    def hop(way, distance, index, sending):
        at = part(offset_of(way, distance - 1 if sending else distance), index, core)
        return remote(at, at, send.at[way, distance - 1, index], recv.at[way, distance - 1, index],
                      ways[way])

    def over(way, distance, sending):
        at = part(offset_of(way, distance), 0 if sending else PIECES - 1, core)
        return remote(at, at, over_send.at[way, distance - 1], over_recv.at[way, distance - 1],
                      partner)

    def pass_on(way, distance, index, which):
        at = part(offset_of(way, distance), index, which)
        return remote(at, at, sib_send.at[way, distance, index], sib_recv.at[way, distance, index],
                      sibling)

    def routing_hop(way, distance, sending):
        back = offset_of(way, distance - 1 if sending else distance)
        at = metas.at[ring_row(place + back, chips, core)]
        return remote(at, at, m_send.at[way, distance - 1], m_recv.at[way, distance - 1], ways[way])

    def routing_on(way, distance, which):
        at = metas.at[ring_row(place + offset_of(way, distance), chips, which)]
        return remote(at, at, n_send.at[way, distance], n_recv.at[way, distance], sibling)

    sent = []

    def go(copy):
        copy.start()
        sent.append(copy)

    reach = [half_way, half_way - 1]
    theirs = gathered.at[other]

    def offsets(distances):
        return [
            offset for distance in distances for offset in sorted({distance, (chips - distance) % chips})
        ]

    def blocks_of(distances):
        return [(offset, which) for offset in offsets(distances) for which in range(2)]

    def first_slot(distance):
        return cap * len(blocks_of(range(distance)))

    def wait_for(distances):
        for distance in distances:
            if distance == 0:
                remote(theirs, theirs, x_sem.at[0], x_sem.at[1], sibling).wait_recv()
                routing_on(0, 0, 1 - core).wait_recv()
                continue
            for way in range(2):
                if distance <= reach[way]:
                    routing_on(way, distance, 1 - core).wait_recv()
                indices = list(ring_pieces(distance, half_way, way))
                for index in indices + ([PIECES - 1] if distance < half_way else []):
                    pass_on(way, distance, index, 1 - core).wait_recv()

    def pack(distance):
        blocks = blocks_of([distance])
        not_after = lax.broadcasted_iota(jnp.int32, (tokens, tokens), 0) <= lax.broadcasted_iota(
            jnp.int32, (tokens, tokens), 1
        )
        not_after = jnp.where(not_after, 1.0, 0.0).astype(jnp.bfloat16)
        numbers = lax.broadcasted_iota(jnp.int32, (cap, tokens), 0).astype(jnp.float32)
        named, weights = [], []
        wanted = [(offset, which, row) for offset, which in blocks]
        wanted += [(offset, 0, other) for offset, which in blocks if which == 0]
        for offset, which, expert in wanted:
            meta = metas[ring_row(place + offset, chips, core if which == 0 else 1 - core)]
            hit = jnp.where(meta[:TOP] == expert.astype(jnp.float32), 1.0, 0.0)
            named.append(jnp.max(hit, axis=0, keepdims=True))
            weights.append(jnp.sum(hit * meta[TOP:], axis=0, keepdims=True))
        hits = jnp.concatenate(named, 0)
        order = jnp.dot(hits.astype(jnp.bfloat16), not_after, preferred_element_type=jnp.float32)
        chosen = [
            jnp.where(order[at:at + 1] == numbers + 1.0, 1.0, 0.0) * named[at]
            for at in range(len(wanted))
        ]
        for at, (offset, which) in enumerate(blocks):
            here = pl.ds(first_slot(distance) + at * cap, cap)
            weight = jnp.sum(chosen[at] * weights[at], axis=1, keepdims=True)
            slot_weight[here, :] = jnp.broadcast_to(weight, (cap, slot_weight.shape[1]))
            source = ring_row(place + offset, chips, core if which == 0 else 1 - core)
            packed[here, :] = jnp.dot(
                chosen[at].astype(jnp.bfloat16), gathered[source],
                preferred_element_type=jnp.float32,
            ).astype(jnp.bfloat16)
        for at, (offset, which) in enumerate(blocks[::2]):
            both = jnp.concatenate([chosen[2 * at], chosen[len(blocks) + at]], 0)
            select[offset] = both.T.astype(jnp.bfloat16)

    def gate_and_up(distances, start, width):
        count = cap * len(blocks_of(distances))
        values = packed[pl.ds(first_slot(distances[0]), count), :]
        lanes = pl.ds(start, width)
        last = (((1,), (1,)), ((), ()))
        gate = lax.dot_general(values, gate_up[0, lanes, :], last, preferred_element_type=jnp.float32)
        up = lax.dot_general(values, gate_up[1, lanes, :], last, preferred_element_type=jnp.float32)
        active[:count, lanes] = ((up + 1.0) * gate * jax.nn.sigmoid(1.702 * gate)).astype(jnp.bfloat16)

    def go_down(distances, first, last, start, width):
        blocks = blocks_of(distances)[first:last]
        lanes = pl.ds(start, width)
        count = (last - first) * cap
        result = jnp.dot(
            active[pl.ds(first * cap, count), :], down[:, lanes], preferred_element_type=jnp.float32
        )
        scale = slot_weight[pl.ds(first_slot(distances[0]) + first * cap, count), :1]
        result = (result * scale).astype(jnp.bfloat16)
        for at, (offset, which) in enumerate(blocks):
            piece = result[at * cap:(at + 1) * cap]
            if which == 0:
                slots[offset, :cap, lanes] = piece
            else:
                sib_slots[offset, :, lanes] = piece

    def slot_copy(offset):
        return remote(sib_slots.at[offset], slots.at[offset, pl.ds(cap, cap)], slot_sem.at[0, offset],
                      slot_sem.at[1, offset], sibling)

    queue = []

    def work(budget):
        while queue and budget > 0:
            cost, step = queue.pop(0)
            step()
            budget -= cost

    def enqueue_pack(distance):
        queue.append((0.1, lambda: wait_for([distance])))
        queue.append((0.5, lambda: pack(distance)))

    def enqueue_products(distances, last_first):
        if distances[0] == 0:
            queue.append((0.0, lambda: loads[0].wait()))
        for start, width in tiles(gate_up.shape[1], 256):
            queue.append((1.0, lambda start=start, width=width: gate_and_up(distances, start, width)))
        if distances[0] == 0:
            queue.append((0.0, lambda: loads[1].wait()))
        count = len(blocks_of(distances))
        split = count - len(blocks_of(distances[-1:]))
        for begin, end in ((split, count), (0, split)) if last_first else ((0, count),):
            for start, width in tiles(down.shape[1], 512):
                queue.append((0.4, lambda start=start, width=width, begin=begin, end=end: go_down(
                    distances, begin, end, start, width)))
            queue.append((0.2, lambda begin=begin, end=end: [
                go(slot_copy(offset)) for offset in offsets(distances)[begin // 2:end // 2]]))

    near, mid = half_way // 4, half_way // 2
    batches = [range(near + 1), range(near + 1, mid + 1), range(mid + 1, half_way + 1)]
    for index in [0, 1, 2]:
        ready(index)
        for way in range(2):
            if index in ring_pieces(1, half_way, way):
                go(hop(way, 1, index, True))
    ready(PIECES - 1)
    local_meta.wait()
    for way in range(2):
        go(routing_hop(way, 1, True))
    go(routing_on(0, 0, core))
    mine = gathered.at[row]
    go(remote(mine, mine, x_sem.at[0], x_sem.at[1], sibling))

    def take_over(distance):
        for way in range(2):
            over(way, distance, False).wait_recv()
            if distance + 1 == half_way and way == 1:
                go(hop(way, half_way, PIECES - 1, True))
            go(pass_on(way, distance, PIECES - 1, core))

    for distance in range(1, half_way + 1):
        for step, index in enumerate([0, 1, 2] if distance < half_way else [0, 2, 1, 3]):
            for way in range(2):
                if index not in ring_pieces(distance, half_way, way):
                    continue
                hop(way, distance, index, False).wait_recv()
                if distance < half_way and index in ring_pieces(distance + 1, half_way, way):
                    go(hop(way, distance + 1, index, True))
                if index == 0 and distance < half_way:
                    go(over(way, distance, True))
                go(pass_on(way, distance, index, core))
            if step == 0:
                enqueue_pack(distance - 1)
                for batch in batches[:-1]:
                    if batch[-1] == distance - 1:
                        enqueue_products(batch, False)
            work(BUDGET)
        for way in range(2):
            if distance <= reach[way]:
                routing_hop(way, distance, False).wait_recv()
                if distance < reach[way]:
                    go(routing_hop(way, distance + 1, True))
                go(routing_on(way, distance, core))
        if distance < half_way:
            take_over(distance)
    enqueue_pack(half_way)
    enqueue_products(batches[-1], True)
    work(100)

    def combine(offset):
        slot_copy(offset).wait_recv()
        mix[offset] = jnp.dot(
            select[offset], slots[offset], preferred_element_type=jnp.float32
        ).astype(jnp.bfloat16)

    def fold_hop(way, distance, index):
        at = pl.ds(index % (PIECES - 1) * size, size)
        return remote(ring_out.at[way, distance - 1, at], ring_in.at[way, distance - 1, at],
                      f_send.at[way, distance - 1, index], f_recv.at[way, distance - 1, index],
                      ways[way])

    def arrived(way, distance, index):
        fold_hop(way, distance, index).wait_recv()
        return ring_in[way, distance - 1, pl.ds(index % (PIECES - 1) * size, size), :].astype(jnp.float32)

    def fold_over(offset):
        return remote(mix.at[offset, piece_rows(PIECES - 1, size)], over_in.at[offset],
                      fo_send.at[offset], fo_recv.at[offset], partner)

    def fold_step(way, distance, index):
        offset = distance if way == 0 else chips - distance
        at = piece_rows(index, size)
        value = mix[offset, at, :].astype(jnp.float32)
        if distance < half_way and index in ring_pieces(distance + 1, half_way, way):
            value = value + arrived(way, distance + 1, index)
        if distance < half_way and index == PIECES - 1:
            mix[offset, at, :] = value.astype(jnp.bfloat16)
            go(fold_over(offset))
            return
        if index == 0 and distance < half_way:
            fold_over(offset).wait_recv()
            value = value + over_in[offset].astype(jnp.float32)
        ring_out[way, distance - 1, pl.ds(index % (PIECES - 1) * size, size), :] = value.astype(
            jnp.bfloat16
        )
        go(fold_hop(way, distance, index))

    for distance in range(half_way, 0, -1):
        for offset in offsets([distance]):
            combine(offset)
        if distance == half_way:
            steps = [(1, 3), (0, 1), (1, 2), (0, 0)]
        elif distance == half_way - 1:
            steps = [(0, 3), (0, 2), (1, 1), (1, 3), (0, 1), (1, 2), (0, 0), (1, 0)]
        else:
            steps = [(0, 3), (1, 3), (0, 1), (1, 1), (0, 2), (1, 2), (0, 0), (1, 0)]
        for way, index in steps:
            fold_step(way, distance, index)
    combine(0)
    width = out_hbm.shape[1]
    for index in [3, 1, 2, 0]:
        at = piece_rows(index, size)
        value = mix[0, at, :].astype(jnp.float32)
        for way in range(2):
            if index in ring_pieces(1, half_way, way):
                value = value + arrived(way, 1, index)
        low, high = value[:, :width], value[:, width:]
        x_out[at, :] = jnp.where(col == 0, high, low).astype(jnp.bfloat16)
        go(remote(x_out.at[at], x_in.at[at], fx_sem.at[0, index], fx_sem.at[1, index], partner))
        base = stream[at, :].astype(jnp.float32)
        out_ref[at, :] = jnp.where(col == 0, low, high) + jnp.where(
            col == 0, base[:, :width], base[:, width:]
        )
    results = []
    for index in [0, 2, 1, 3]:
        at = piece_rows(index, size)
        named = PIECES - 1 - index
        remote(x_out.at[at], x_in.at[at], fx_sem.at[0, named], fx_sem.at[1, named],
               partner).wait_recv()
        result[at, :] = (out_ref[at, :] + x_in[at, :].astype(jnp.float32)).astype(jnp.bfloat16)
        results.append(pltpu.make_async_copy(result.at[at], out_hbm.at[at], y_sem.at[index]))
        results[-1].start()
    for copy in results:
        copy.wait()
    for copy in early + list(crosses.values()) + sent:
        copy.wait_send()
    for at in range(shifts):
        @pl.when(follows[at])
        def _(at=at):
            for halo in halos[at]:
                halo.wait_send()


def layer(residual, queries, keys, values, segments, sinks, w_out, gain, expert_ids, route_weight, w_gate_up,
          w_down, rows, cap, shifts, kv_width, width):
    w_gate_up = jnp.swapaxes(w_gate_up, 2, 3)
    w_out = w_out.T
    half_way = rows // 4
    chips = rows // 2
    tokens, features = residual.shape
    hidden = w_gate_up.shape[2]
    near, mid = half_way // 4, half_way // 2
    most = cap * 2 * max(2 * near + 1, 2 * (mid - near), 2 * (half_way - mid) - 1)
    key_rows = -(-(shifts + 1) * tokens // 128) * 128
    out_tiles = len(tiles(features, chips * tokens))
    meta = (2 * TOP, tokens)
    bf16, f32, dma = jnp.bfloat16, jnp.float32, pltpu.SemaphoreType.DMA
    hbm = pl.BlockSpec(memory_space=pl.ANY)
    return pl.pallas_call(
        lambda *refs: expert_kernel(rows, cap, shifts, *refs),
        out_shape=jax.ShapeDtypeStruct((tokens, width), bf16),
        in_specs=[hbm] * 12,
        out_specs=hbm,
        scratch_shapes=[
            pltpu.VMEM((tokens, features), bf16),
            pltpu.VMEM(queries.shape, bf16),
            pltpu.VMEM((1, features), f32),
            pltpu.VMEM((1, tokens), jnp.int32),
            pltpu.SMEM((1, sinks.shape[0]), f32),
            pltpu.VMEM((TOP, tokens), jnp.int32),
            pltpu.VMEM((TOP, tokens), f32),
            pltpu.VMEM((tokens, width), f32),
            pltpu.VMEM((tokens, width), bf16),
            dma((PIECES,)),
            dma((9,)),
            pltpu.VMEM((features - chips * tokens, w_out.shape[1]), bf16),
            pltpu.VMEM((key_rows, kv_width), bf16),
            pltpu.VMEM((key_rows, kv_width), bf16),
            pltpu.VMEM((shifts, 1, tokens), jnp.int32),
            pltpu.VMEM(queries.shape, bf16),
            pltpu.VMEM((tokens, features), bf16),
            pltpu.VMEM(meta, f32),
            pltpu.VMEM(w_gate_up.shape[1:], bf16),
            pltpu.VMEM(w_down.shape[1:], bf16),
            pltpu.VMEM((rows, tokens, features), bf16),
            pltpu.VMEM((rows, *meta), f32),
            pltpu.VMEM((tokens, features), bf16),
            pltpu.VMEM((tokens, features), bf16),
            pltpu.VMEM((rows * cap, features), bf16),
            pltpu.VMEM((most, hidden), bf16),
            pltpu.VMEM((rows * cap, 128), f32),
            pltpu.VMEM((chips, tokens, 2 * cap), bf16),
            pltpu.VMEM((chips, 2 * cap, features), bf16),
            pltpu.VMEM((chips, cap, features), bf16),
            pltpu.VMEM((chips, tokens, features), bf16),
            pltpu.VMEM((2, half_way, tokens // PIECES * (PIECES - 1), features), bf16),
            pltpu.VMEM((2, half_way, tokens // PIECES * (PIECES - 1), features), bf16),
            pltpu.VMEM((chips, tokens // PIECES, features), bf16),
            pltpu.VMEM((tokens, width), bf16),
            pltpu.VMEM((tokens, width), bf16),
            dma((out_tiles + chips,)),
            dma((shifts, 3)),
            dma((shifts, 3)),
            dma((2,)),
            dma((2,)),
            dma((PIECES + out_tiles,)),
            dma((PIECES + out_tiles,)),
            dma((2, half_way)),
            dma((2, half_way)),
            dma((2, half_way + 1)),
            dma((2, half_way + 1)),
            dma,
            dma((2, half_way, PIECES)),
            dma((2, half_way, PIECES)),
            dma((2, half_way)),
            dma((2, half_way)),
            dma((2, half_way + 1, PIECES)),
            dma((2, half_way + 1, PIECES)),
            dma((2, chips)),
            dma((2, half_way, PIECES)),
            dma((2, half_way, PIECES)),
            dma((chips,)),
            dma((chips,)),
            dma((2, PIECES)),
        ],
        compiler_params=pltpu.CompilerParams(
            collective_id=2, has_side_effects=True, vmem_limit_bytes=VMEM_BYTES
        ),
        name="layer",
    )(residual, queries, keys, values, segments.reshape(1, -1), sinks.reshape(1, -1), gain,
      expert_ids.T, route_weight.T, w_out, w_gate_up, w_down)


def local(
    residual,
    query_states,
    key_states,
    value_states,
    segment_ids,
    sink_logits,
    w_out,
    norm_gain,
    expert_ids,
    route_weight,
    w_gate_up,
    w_down,
):
    tok_rows = query_states.shape[0]
    row_count = lax.axis_size("row")
    col_count = lax.axis_size("col")
    row_index = lax.axis_index("row")
    col_index = lax.axis_index("col")
    local_heads = sink_logits.shape[0]
    group_size = HEADS // KV_HEADS
    if local_heads >= group_size:
        kv_count = local_heads // group_size
        kv_first = col_index * kv_count
    else:
        kv_count = 1
        kv_first = col_index * local_heads // group_size
    kv_width = kv_count * HEAD_DIM
    own_keys = lax.dynamic_slice_in_dim(key_states, kv_first * HEAD_DIM, kv_width, 1)
    own_values = lax.dynamic_slice_in_dim(value_states, kv_first * HEAD_DIM, kv_width, 1)
    shift_count = (WINDOW + tok_rows - 2) // tok_rows
    block_bytes = 2 * residual.shape[0] * residual.shape[1]
    experts_all = w_gate_up.shape[0] * row_count
    slot_cap = max(2, 2 * TOP * tok_rows // experts_all)
    weight_bytes = 2 * (w_out.size + w_gate_up.size + w_down.size)
    in_kernels = (
        col_count == 2 and row_count % 4 == 0 and row_count >= 8 and tok_rows % 64 == 0
        and kv_width % 128 == 0 and kv_width * col_count == key_states.shape[1]
        and row_count // 2 * tok_rows < residual.shape[1] and w_out.shape[0] <= residual.shape[1]
        and slot_cap % 16 == 0 and 2 * slot_cap == tok_rows and 2 * HEAD_DIM == 128
        and local_heads % (2 * kv_count) == 0 and weight_bytes + 3 * row_count * block_bytes < VMEM_BYTES
    )
    feature_count = residual.shape[1] // col_count
    if in_kernels:
        return layer(
            residual, query_states, key_states, value_states, segment_ids, sink_logits, w_out, norm_gain,
            expert_ids, route_weight, w_gate_up, w_down, row_count, slot_cap, shift_count, kv_width,
            feature_count,
        )
    routing = jnp.concatenate([expert_ids.astype(jnp.float32), route_weight], 1).T
    key_parts = []
    value_parts = []
    segment_parts = []
    start_parts = []
    for offset in range(shift_count, 0, -1):
        arrived = shifted((own_keys, own_values, segment_ids), "row", offset)
        key_parts.append(arrived[0])
        value_parts.append(arrived[1])
        segment_parts.append(arrived[2])
        start_parts.append((row_index - offset) * tok_rows)
    key_parts.append(own_keys)
    value_parts.append(own_values)
    segment_parts.append(segment_ids)
    start_parts.append(row_index * tok_rows)
    key_groups = jnp.concatenate(key_parts, 0).reshape(-1, kv_count, HEAD_DIM)
    value_groups = jnp.concatenate(value_parts, 0).reshape(-1, kv_count, HEAD_DIM)
    key_segments = jnp.concatenate(segment_parts, 0)
    positions = jnp.arange(tok_rows, dtype=jnp.int32)
    key_position = jnp.concatenate([start + positions for start in start_parts], 0)
    query_position = row_index * tok_rows + positions
    allowed = (key_position[None, :] >= 0) & (key_position[None, :] <= query_position[:, None])
    allowed = allowed & (key_position[None, :] > query_position[:, None] - WINDOW)
    allowed = allowed & (key_segments[None, :] == segment_ids[:, None])
    query_groups = query_states.reshape(tok_rows, kv_count, local_heads // kv_count, HEAD_DIM)
    sink_groups = sink_logits.reshape(kv_count, local_heads // kv_count, 1, 1)
    attended = attend(query_groups, key_groups, value_groups, allowed, sink_groups).reshape(
        tok_rows, local_heads * HEAD_DIM
    )
    partial_value = jnp.dot(attended, w_out, preferred_element_type=jnp.float32)
    expert_gate_up = w_gate_up[0]
    expert_down = w_down[0]
    partial_value = partial_value.astype(jnp.bfloat16)
    summed = lax.psum(partial_value, "col").astype(jnp.float32)
    stream = (residual.astype(jnp.float32) + summed).astype(jnp.bfloat16)
    gathered = lax.all_gather(normalize(stream, norm_gain), "row", axis=0, tiled=False)
    routing = lax.all_gather(routing, "row", axis=0, tiled=False)
    stream_part = lax.dynamic_slice_in_dim(stream, col_index * feature_count, feature_count, 1)
    names_mine = routing[:, :TOP] == row_index.astype(jnp.float32)
    mine = jnp.any(names_mine, axis=1)
    weight = jnp.sum(jnp.where(names_mine, routing[:, TOP:], 0.0), axis=1)
    token_order = jnp.arange(tok_rows, dtype=jnp.int32)
    not_after = (token_order[:, None] <= token_order[None, :]).astype(jnp.bfloat16)
    slot_of = jnp.dot(
        mine.astype(jnp.bfloat16), not_after, preferred_element_type=jnp.float32
    ).astype(jnp.int32) - 1
    slots = jnp.arange(slot_cap, dtype=jnp.int32)
    chosen = mine[:, None, :] & (slot_of[:, None, :] == slots[None, :, None])
    selector = chosen.astype(jnp.bfloat16)
    combine = jnp.where(chosen, weight[:, None, :], 0.0)
    packed = jnp.einsum(
        "nst,ntd->nsd", selector, gathered, preferred_element_type=jnp.float32
    ).astype(jnp.bfloat16).reshape(row_count * slot_cap, -1)
    gate = jnp.dot(packed, expert_gate_up[0], preferred_element_type=jnp.float32)
    up = jnp.dot(packed, expert_gate_up[1], preferred_element_type=jnp.float32)
    active = ((up + 1.0) * gate * jax.nn.sigmoid(1.702 * gate)).astype(jnp.bfloat16)
    expert_partial = jnp.dot(active, expert_down, preferred_element_type=jnp.float32)
    scaled = expert_partial.reshape(row_count, slot_cap, -1) * jnp.sum(combine, 2)[:, :, None]
    mixed = jnp.einsum(
        "nst,nsd->ntd", selector, scaled.astype(jnp.bfloat16), preferred_element_type=jnp.float32
    ).astype(jnp.bfloat16)
    mixed = mixed.reshape(row_count * tok_rows, -1)
    mixed = lax.psum_scatter(mixed, "row", scatter_dimension=0, tiled=True)
    mixed = lax.psum_scatter(mixed, "col", scatter_dimension=1, tiled=True)
    return (stream_part.astype(jnp.float32) + mixed.astype(jnp.float32)).astype(jnp.bfloat16)


def solution(mesh):
    in_specs = (
        P("row", None),
        P("row", "col"),
        P("row", None),
        P("row", None),
        P("row"),
        P("col"),
        P("col", None),
        P(),
        P("row", None),
        P("row", None),
        P("row", None, None, "col"),
        P("row", "col", None),
    )
    out_specs = P("row", "col")
    return jax.shard_map(local, mesh=mesh, in_specs=in_specs, out_specs=out_specs, check_vma=False)
```
